128 devices in a mesh: tensor: 8 (over y_hi, x), context: 16 (over z, y_lo, core).
Axes of the slice: x: 4, y: 4 (y_hi: 2, y_lo: 2; y = y_hi * 2 + y_lo), z: 4, core: 2. Of those that a mesh axis runs over, the one named last changes fastest.
Arguments:
- tokens: bfloat16 [16, 1024, 4096], P('context', 'tensor'), may hold values from -6 to 6
- norm_gain: float32 [4096], replicated, may hold values from 0.25 to 1.75
- q_weight: bfloat16 [4096, 2048], P(None, 'tensor')
- k_weight: bfloat16 [4096, 1024], P(None, 'tensor')
- v_weight: bfloat16 [4096, 1024], P(None, 'tensor'), may hold values from -0.75 to 0.75
- o_weight: bfloat16 [2048, 4096], P('tensor'), may hold values from -0.125 to 0.125
- doc_lengths: int32 [16], replicated, may hold values from 1 to 4096, 16384 in all
- span_order: int32 [32], replicated, may hold values from 0 to 31, each once
Outputs:
- layer_out: bfloat16 [16, 1024, 4096], P('context', 'tensor')
The draws below stay inside these ranges and needn't reach their ends.
Inputs may be any that keep to these rules, and one draw needn't show every extreme that they name: `doc_lengths`: documents fill the sequence in order; the longest has exactly 4096 tokens. `span_order`: each value appears once.
All inputs are finite; a program needn't handle non-finite values.
Results may differ from the reference program's by a relative error of at most 0.019.
Values may be sent and summed in bfloat16 or wider, within the bound.
A program may use at most 320 MiB of HBM per device.

```python
import math
import jax
import jax.numpy as jnp
import numpy as np
from jax import lax

D = 4096
HEADS = 16
KV_HEADS = 8
HEAD_DIM = 128
TOK_DEV = 1024
NDOCS = 16
BLOCKS = 16
SEQ = 16384
SPAN = 512
N_TENSOR = 8
N_CONTEXT = 16


def query_base(key):
    return jax.random.normal(jax.random.fold_in(key, 11), (D, HEADS * HEAD_DIM), jnp.float32) / math.sqrt(D)


def draw_q_weight(key, part):
    return query_base(key).astype(jnp.bfloat16)


def draw_k_weight(key, part):
    noise_part = jax.random.normal(jax.random.fold_in(key, 12), (D, KV_HEADS * HEAD_DIM), jnp.float32) / math.sqrt(D)
    return noise_part.astype(jnp.bfloat16)


def level_of(key, shape, pieces, least, high):
    def one(axis_at, parts):
        steps = jax.random.uniform(jax.random.fold_in(jax.random.fold_in(key, 6), axis_at), (parts,), jnp.float32, least / len(pieces), high / len(pieces))
        return jnp.repeat(jnp.exp(steps), shape[axis_at] // parts).reshape((-1,) + (1,) * (len(shape) - axis_at - 1))

    loudness = one(*pieces[0])
    for cut in pieces[1:]:
        loudness = loudness * one(*cut)
    return loudness


def length_profile(amount, total, reach, lean):
    portions = [(1 << 20) // math.isqrt(rank ** lean) + 1 for rank in range(2, amount + 1)]
    spare, given = total - reach - (amount - 1), [1] * (amount - 1)
    while spare > 0:
        candidates = [i for i in range(amount - 1) if given[i] < reach]
        mass, budget = sum([portions[i] for i in candidates]), spare
        for i in candidates:
            extra = min(reach - given[i], max(1, budget * portions[i] // mass), spare)
            given[i] = given[i] + extra
            spare = spare - extra
    return np.array([reach] + given)


def ragged(stream_key, amount, total, bound, skew):
    if amount == 2:
        one = jax.random.randint(stream_key, (), max(1, total - bound), min(bound, total - 1) + 1)
        return jnp.stack([one, total - one])
    tallies = jnp.asarray(length_profile(amount, total, bound, skew), jnp.int32)
    twos = (amount - 1) // 2
    donor, taker = tallies[1:1 + 2 * twos:2], tallies[2:2 + 2 * twos:2]
    slack = jnp.minimum(donor - 1, bound - taker)
    moved = jax.random.randint(jax.random.fold_in(stream_key, 1), (twos,), 0, 1 << 20) % (slack + 1)
    tallies = tallies.at[1:1 + 2 * twos:2].set(donor - moved).at[2:2 + 2 * twos:2].set(taker + moved)
    return tallies[jax.random.permutation(jax.random.fold_in(stream_key, 2), amount)]


def scatter_about(key, extent, spread, most, shards=(), held_as=jnp.bfloat16):
    result = spread * jax.random.normal(key, extent, jnp.float32)
    if shards:
        result = result * level_of(key, extent, shards, -0.22, 0.18)
    return jnp.clip(result, -most, most).astype(held_as)


def setup_inputs(seed: int = 0) -> dict:
    key_of = jax.random.split(jax.random.key(seed), 9)
    return {
        "tokens": scatter_about(key_of[0], (BLOCKS, TOK_DEV, D), 1.0, 6.0, ((0, 16), (1, 8))),
        "norm_gain": jnp.clip(1.0 + 0.15 * jax.random.normal(key_of[1], (D,), jnp.float32), 0.25, 1.75),
        "q_weight": draw_q_weight(jax.random.fold_in(key_of[8], 71), 0),
        "k_weight": draw_k_weight(jax.random.fold_in(key_of[8], 71), 0),
        "v_weight": scatter_about(key_of[4], (D, KV_HEADS * HEAD_DIM), (8.0 / D ** 0.5), 0.75, ((1, 8),)),
        "o_weight": scatter_about(key_of[5], (HEADS * HEAD_DIM, D), (HEADS * HEAD_DIM) ** -0.5, 0.125, ((0, 8),)),
        "doc_lengths": ragged(key_of[6], NDOCS, SEQ, SEQ // 4, 2).astype(jnp.int32),
        "span_order": jax.random.permutation(key_of[7], 2 * N_CONTEXT).astype(jnp.int32),
    }


rope_theta = 500000.0
epsilon = 1e-05
masked_score = -1e+30

def positions(rows, span_order, span_rows):
    slot_ids = jnp.arange(span_order.shape[0], dtype=jnp.int32)
    matches = (rows // span_rows)[:, None] == slot_ids[None, :]
    picked = lax.optimization_barrier(jnp.sum(jnp.where(matches, span_order[None, :], 0), axis=1)).astype(jnp.int32)
    return (picked * span_rows + rows % span_rows).astype(jnp.int32)

def documents(places, doc_lengths):
    doc_ends = jnp.cumsum(doc_lengths).astype(jnp.int32)
    return lax.optimization_barrier(jnp.sum((doc_ends[None, :] <= places[:, None]).astype(jnp.int32), axis=1)).astype(jnp.int32)

def rotary(values, places):
    head_dim = values.shape[-1]
    half_dim = head_dim // 2
    frequency = rope_theta ** (-(2.0 / head_dim) * jnp.arange(half_dim, dtype=jnp.float32))
    angles = places.astype(jnp.float32)[:, None] * frequency[None, :]
    cosine = jnp.cos(angles)[:, None, :]
    sine_part = jnp.sin(angles)[:, None, :]
    first_half = values[..., :half_dim]
    second = values[..., half_dim:]
    return jnp.concatenate([first_half * cosine - second * sine_part, second * cosine + first_half * sine_part], axis=-1)

def reference(tokens, norm_gain, q_weight, k_weight, v_weight, o_weight, doc_lengths, span_order):
    flat_rows = tokens.reshape(SEQ, D)
    rows_float = flat_rows.astype(jnp.float32)
    normed = (rows_float * lax.rsqrt(lax.optimization_barrier(jnp.mean(rows_float * rows_float, axis=-1, keepdims=True)) + epsilon) * norm_gain).astype(jnp.bfloat16)
    places = positions(jnp.arange(SEQ, dtype=jnp.int32), span_order, SPAN)
    doc_ids = documents(places, doc_lengths)
    query_rows = rotary(jnp.dot(normed, q_weight, preferred_element_type=jnp.float32).reshape(SEQ, HEADS, HEAD_DIM), places).astype(jnp.bfloat16)
    key_rows = rotary(jnp.dot(normed, k_weight, preferred_element_type=jnp.float32).reshape(SEQ, KV_HEADS, HEAD_DIM), places).astype(jnp.bfloat16)
    value_rows = jnp.dot(normed, v_weight, preferred_element_type=jnp.float32).astype(jnp.bfloat16).reshape(SEQ, KV_HEADS, HEAD_DIM)
    group_size = HEADS // KV_HEADS
    block_rows = math.gcd(SEQ, 1024)
    score_scale = 1.0 / math.sqrt(HEAD_DIM)
    query_heads = query_rows.reshape(SEQ // block_rows, block_rows, KV_HEADS, group_size, HEAD_DIM).transpose(2, 0, 1, 3, 4)
    key_heads = key_rows.transpose(1, 0, 2).astype(jnp.float32)
    value_heads = value_rows.transpose(1, 0, 2).astype(jnp.float32)
    place_blocks = places.reshape(SEQ // block_rows, block_rows)
    doc_blocks = doc_ids.reshape(SEQ // block_rows, block_rows)

    def one_head(operands):
        query_head, key_head, value_head = operands

        def one_block(block):
            query_block, query_places, query_docs = block
            scores = jnp.einsum('qgd,sd->gqs', query_block.astype(jnp.float32), key_head) * score_scale
            visible = (places[None, :] <= query_places[:, None]) & (doc_ids[None, :] == query_docs[:, None])
            limited = jnp.where(visible[None], scores, masked_score)
            row_max = lax.optimization_barrier(jnp.max(limited, axis=-1, keepdims=True))
            weights = jnp.where(visible[None], jnp.exp(scores - row_max), 0.0)
            row_sum = lax.optimization_barrier(jnp.sum(weights, axis=-1))
            rounded = lax.optimization_barrier(weights.astype(jnp.bfloat16))
            summed = jnp.einsum('gqs,sd->qgd', rounded.astype(jnp.float32), value_head)
            return summed / row_sum.T[:, :, None]
        return lax.map(one_block, (query_head, place_blocks, doc_blocks))
    attended = lax.map(one_head, (query_heads, key_heads, value_heads))
    attended = attended.transpose(1, 2, 0, 3, 4).reshape(SEQ, HEADS * HEAD_DIM).astype(jnp.bfloat16)
    group_cols = HEADS * HEAD_DIM // N_TENSOR
    split_attn = attended.reshape(SEQ, N_TENSOR, group_cols).transpose(1, 0, 2)
    split_out = o_weight.reshape(N_TENSOR, group_cols, D)

    def add_group(running, operands):
        part_attn, part_weight = operands
        term = jnp.dot(part_attn, part_weight, preferred_element_type=jnp.float32).astype(jnp.bfloat16)
        term = lax.optimization_barrier(term)
        return (running + term.astype(jnp.float32), None)
    summed, unused = lax.scan(add_group, jnp.zeros((SEQ, D), jnp.float32), (split_attn, split_out))
    return summed.astype(jnp.bfloat16).reshape(BLOCKS, TOK_DEV, D)
```

```python
import functools
import math

import jax
import jax.numpy as jnp
from jax import lax
from jax.experimental import pallas as pl
from jax.experimental.pallas import tpu as pltpu
from jax.sharding import PartitionSpec as P

HEAD_DIM = 128
SPAN = 512
KEY_SLOTS = 9

rope_theta = 500000.0
epsilon = 1e-05
masked_score = -1e30


def positions(rows, span_order, span_rows):
    slot_ids = jnp.arange(span_order.shape[0], dtype=jnp.int32)
    matches = (rows // span_rows)[:, None] == slot_ids[None, :]
    picked = jnp.sum(jnp.where(matches, span_order[None, :], 0), axis=1)
    return picked * span_rows + rows % span_rows


def rotary(values, places):
    head_dim = values.shape[-1]
    half_dim = head_dim // 2
    frequency = rope_theta ** (-(2.0 / head_dim) * jnp.arange(half_dim, dtype=jnp.float32))
    angles = places.astype(jnp.float32)[:, None] * frequency[None, :]
    cosine = jnp.cos(angles)[:, None, :]
    sine_part = jnp.sin(angles)[:, None, :]
    first_half = values[..., :half_dim]
    second = values[..., half_dim:]
    return jnp.concatenate(
        [first_half * cosine - second * sine_part, second * cosine + first_half * sine_part],
        axis=-1,
    )


def attention_kernel(heads, scale, tbl_ref, seq_ref, cnt_ref, q_ref, qpos_ref, qstart_ref,
                     k_ref, v_ref, o_ref, m_sc, l_sc, acc_sc):
    i = pl.program_id(0)
    j = pl.program_id(1)

    @pl.when(j == 0)
    def _():
        m_sc[...] = jnp.full_like(m_sc, masked_score)
        l_sc[...] = jnp.zeros_like(l_sc)
        acc_sc[...] = jnp.zeros_like(acc_sc)

    @pl.when(j < cnt_ref[i])
    def _():
        k = k_ref[...]
        v = v_ref[...]
        span = k.shape[0]
        kpos = seq_ref[i, j] * span + lax.broadcasted_iota(jnp.int32, (1, span), 1)
        visible = (kpos <= qpos_ref[...]) & (kpos >= qstart_ref[...])
        for h in range(heads):
            q = q_ref[:, h * HEAD_DIM:(h + 1) * HEAD_DIM]
            s = lax.dot_general(q, k, (((1,), (1,)), ((), ())),
                                preferred_element_type=jnp.float32) * scale
            m_old = m_sc[h]
            m_new = jnp.maximum(
                m_old, jnp.max(jnp.where(visible, s, masked_score), axis=-1, keepdims=True))
            p = jnp.where(visible, jnp.exp(s - m_new), 0.0)
            alpha = jnp.exp(m_old - m_new)
            l_sc[h] = alpha * l_sc[h] + jnp.sum(p, axis=-1, keepdims=True)
            acc_sc[h] = alpha * acc_sc[h] + jnp.dot(
                p.astype(jnp.bfloat16), v, preferred_element_type=jnp.float32)
            m_sc[h] = m_new

    @pl.when(j == pl.num_programs(1) - 1)
    def _():
        for h in range(heads):
            o_ref[:, h * HEAD_DIM:(h + 1) * HEAD_DIM] = (acc_sc[h] / l_sc[h]).astype(o_ref.dtype)


def span_attention(tbl, seq, cnt, queries, qpos, qstart, keys, values):
    rows, q_cols = queries.shape
    heads = q_cols // HEAD_DIM
    n_q = rows // SPAN
    kernel = functools.partial(attention_kernel, heads, 1.0 / math.sqrt(HEAD_DIM))
    steps = n_q * KEY_SLOTS
    cost = pl.CostEstimate(
        flops=4 * steps * heads * SPAN * SPAN * HEAD_DIM,
        transcendentals=steps * heads * SPAN * SPAN,
        bytes_accessed=steps * 2 * SPAN * HEAD_DIM * 2 + 2 * rows * q_cols * 2,
    )
    return pl.pallas_call(
        kernel,
        out_shape=jax.ShapeDtypeStruct((rows, q_cols), jnp.bfloat16),
        grid_spec=pltpu.PrefetchScalarGridSpec(
            num_scalar_prefetch=3,
            grid=(n_q, KEY_SLOTS),
            in_specs=[
                pl.BlockSpec((SPAN, q_cols), lambda i, j, t, s, c: (i, 0)),
                pl.BlockSpec((SPAN, 1), lambda i, j, t, s, c: (i, 0)),
                pl.BlockSpec((SPAN, 1), lambda i, j, t, s, c: (i, 0)),
                pl.BlockSpec((SPAN, HEAD_DIM), lambda i, j, t, s, c: (t[i, j], 0)),
                pl.BlockSpec((SPAN, HEAD_DIM), lambda i, j, t, s, c: (t[i, j], 0)),
            ],
            out_specs=pl.BlockSpec((SPAN, q_cols), lambda i, j, t, s, c: (i, 0)),
            scratch_shapes=[
                pltpu.VMEM((heads, SPAN, 1), jnp.float32),
                pltpu.VMEM((heads, SPAN, 1), jnp.float32),
                pltpu.VMEM((heads, SPAN, HEAD_DIM), jnp.float32),
            ],
        ),
        compiler_params=pltpu.CompilerParams(dimension_semantics=("arbitrary", "arbitrary")),
        cost_estimate=cost,
    )(tbl, seq, cnt, queries, qpos, qstart, keys, values)


def key_tables(span_order, doc_ends, query_spans):
    n_spans = span_order.shape[0]
    span_ids = jnp.arange(n_spans, dtype=jnp.int32)
    inverse = jnp.sum(
        jnp.where(span_order[None, :] == span_ids[:, None], span_ids[None, :], 0), axis=1)
    first_doc = jnp.sum((doc_ends[None, :] <= (span_ids * SPAN)[:, None]).astype(jnp.int32), axis=1)
    last_doc = jnp.sum(
        (doc_ends[None, :] <= (span_ids * SPAN + SPAN - 1)[:, None]).astype(jnp.int32), axis=1)
    sq = jnp.sum(jnp.where(query_spans[:, None] == span_ids[None, :], span_order[None, :], 0), axis=1)
    q_first = jnp.sum(jnp.where(sq[:, None] == span_ids[None, :], first_doc[None, :], 0), axis=1)
    back = jnp.arange(KEY_SLOTS, dtype=jnp.int32) - (KEY_SLOTS - 1)
    cand = sq[:, None] + back[None, :]
    cand_last = jnp.sum(
        jnp.where(cand[:, :, None] == span_ids[None, None, :], last_doc[None, None, :], 0), axis=2)
    valid = (cand >= 0) & (cand_last >= q_first[:, None])
    count = jnp.sum(valid.astype(jnp.int32), axis=1)
    slot = jnp.arange(KEY_SLOTS, dtype=jnp.int32)
    seq = jnp.minimum(sq[:, None] - count[:, None] + 1 + slot[None, :], sq[:, None])
    tbl = jnp.sum(jnp.where(seq[:, :, None] == span_ids[None, None, :], inverse[None, None, :], 0),
                  axis=2)
    return tbl.astype(jnp.int32), seq.astype(jnp.int32), count.astype(jnp.int32)


def per_device(tokens, norm_gain, q_weight, k_weight, v_weight, o_weight, doc_lengths, span_order):
    local_rows = tokens.shape[1]
    tok_dev = local_rows * lax.axis_size("tensor")
    model_width = tokens.shape[2]
    head_dim = HEAD_DIM
    q_cols = q_weight.shape[1]
    kv_cols = k_weight.shape[1]
    q_heads = q_cols // head_dim
    kv_local = kv_cols // head_dim
    span_rows = tok_dev // 2
    base_row = lax.axis_index("context") * tok_dev
    rows_float = tokens.astype(jnp.float32)
    normed = (
        rows_float
        * lax.rsqrt(jnp.mean(rows_float * rows_float, axis=-1, keepdims=True) + epsilon)
        * norm_gain
    ).astype(jnp.bfloat16)
    portion = lax.all_gather(normed, "tensor", axis=1, tiled=True)
    row_count = portion.shape[1]
    flat_rows = portion.reshape(row_count, model_width)
    places = positions(base_row + jnp.arange(row_count, dtype=jnp.int32), span_order, span_rows)
    query_rows = jnp.dot(flat_rows, q_weight, preferred_element_type=jnp.float32).reshape(
        row_count, q_heads, head_dim
    )
    key_rows = jnp.dot(flat_rows, k_weight, preferred_element_type=jnp.float32).reshape(
        row_count, kv_local, head_dim
    )
    value_rows = jnp.dot(flat_rows, v_weight, preferred_element_type=jnp.float32).astype(
        jnp.bfloat16
    )
    query_rows = rotary(query_rows, places).reshape(row_count, q_cols).astype(jnp.bfloat16)
    key_rows = rotary(key_rows, places).reshape(row_count, kv_cols).astype(jnp.bfloat16)
    kv_pair = jnp.stack([key_rows, value_rows])
    gathered = lax.all_gather(kv_pair, "context", axis=1, tiled=True)

    doc_ends = jnp.cumsum(doc_lengths)
    query_start = jnp.max(
        jnp.where(doc_ends[None, :] <= places[:, None], doc_ends[None, :], 0), axis=1)
    query_spans = lax.axis_index("context") * 2 + jnp.arange(2, dtype=jnp.int32)
    tbl, seq, cnt = key_tables(span_order, doc_ends, query_spans)
    attended = span_attention(
        tbl, seq, cnt, query_rows,
        places.astype(jnp.int32)[:, None], query_start.astype(jnp.int32)[:, None],
        gathered[0], gathered[1],
    )
    mixed_rows = lax.psum_scatter(
        jnp.dot(attended, o_weight, preferred_element_type=jnp.float32).astype(jnp.bfloat16),
        "tensor",
        scatter_dimension=0,
        tiled=True,
    )
    return mixed_rows.reshape(tokens.shape)


def solution(mesh):
    in_specs = (
        P("context", "tensor", None),
        P(),
        P(None, "tensor"),
        P(None, "tensor"),
        P(None, "tensor"),
        P("tensor", None),
        P(),
        P(),
    )
    out_specs = P("context", "tensor", None)
    return jax.shard_map(
        per_device, mesh=mesh, in_specs=in_specs, out_specs=out_specs, check_vma=False
    )
```

```python
import functools
import math

import jax
import jax.numpy as jnp
from jax import lax
from jax.experimental import pallas as pl
from jax.experimental.pallas import tpu as pltpu
from jax.sharding import PartitionSpec as P

HEAD_DIM = 128
SPAN = 512
KEY_SLOTS = 9

rope_theta = 500000.0
epsilon = 1e-05
masked_score = -1e30


def positions(rows, span_order, span_rows):
    slot_ids = jnp.arange(span_order.shape[0], dtype=jnp.int32)
    matches = (rows // span_rows)[:, None] == slot_ids[None, :]
    picked = jnp.sum(jnp.where(matches, span_order[None, :], 0), axis=1)
    return picked * span_rows + rows % span_rows


def rotary(values, places):
    head_dim = values.shape[-1]
    half_dim = head_dim // 2
    frequency = rope_theta ** (-(2.0 / head_dim) * jnp.arange(half_dim, dtype=jnp.float32))
    angles = places.astype(jnp.float32)[:, None] * frequency[None, :]
    cosine = jnp.cos(angles)[:, None, :]
    sine_part = jnp.sin(angles)[:, None, :]
    first_half = values[..., :half_dim]
    second = values[..., half_dim:]
    return jnp.concatenate(
        [first_half * cosine - second * sine_part, second * cosine + first_half * sine_part],
        axis=-1,
    )


def attention_kernel(heads, scale, tbl_ref, seq_ref, cnt_ref, q_ref, qpos_ref, qstart_ref,
                     k_ref, v_ref, o_ref, m_sc, l_sc, acc_sc):
    i = pl.program_id(0)
    j = pl.program_id(1)

    @pl.when(j == 0)
    def _():
        m_sc[...] = jnp.full_like(m_sc, masked_score)
        l_sc[...] = jnp.zeros_like(l_sc)
        acc_sc[...] = jnp.zeros_like(acc_sc)

    @pl.when(j < cnt_ref[i])
    def _():
        k = k_ref[...]
        v = v_ref[...]
        span = k.shape[0]
        kpos = seq_ref[i, j] * span + lax.broadcasted_iota(jnp.int32, (1, span), 1)
        visible = (kpos <= qpos_ref[...]) & (kpos >= qstart_ref[...])
        for h in range(heads):
            q = q_ref[:, h * HEAD_DIM:(h + 1) * HEAD_DIM]
            s = lax.dot_general(q, k, (((1,), (1,)), ((), ())),
                                preferred_element_type=jnp.float32) * scale
            m_old = m_sc[h]
            m_new = jnp.maximum(
                m_old, jnp.max(jnp.where(visible, s, masked_score), axis=-1, keepdims=True))
            p = jnp.where(visible, jnp.exp(s - m_new), 0.0)
            alpha = jnp.exp(m_old - m_new)
            l_sc[h] = alpha * l_sc[h] + jnp.sum(p, axis=-1, keepdims=True)
            acc_sc[h] = alpha * acc_sc[h] + jnp.dot(
                p.astype(jnp.bfloat16), v, preferred_element_type=jnp.float32)
            m_sc[h] = m_new

    @pl.when(j == pl.num_programs(1) - 1)
    def _():
        for h in range(heads):
            o_ref[:, h * HEAD_DIM:(h + 1) * HEAD_DIM] = (acc_sc[h] / l_sc[h]).astype(o_ref.dtype)


def span_attention(tbl, seq, cnt, queries, qpos, qstart, kv):
    rows, q_cols = queries.shape
    heads = q_cols // HEAD_DIM
    n_q = rows // SPAN
    kernel = functools.partial(attention_kernel, heads, 1.0 / math.sqrt(HEAD_DIM))
    steps = n_q * KEY_SLOTS
    cost = pl.CostEstimate(
        flops=4 * steps * heads * SPAN * SPAN * HEAD_DIM,
        transcendentals=steps * heads * SPAN * SPAN,
        bytes_accessed=steps * 2 * SPAN * HEAD_DIM * 2 + 2 * rows * q_cols * 2,
    )
    return pl.pallas_call(
        kernel,
        out_shape=jax.ShapeDtypeStruct((rows, q_cols), jnp.bfloat16),
        grid_spec=pltpu.PrefetchScalarGridSpec(
            num_scalar_prefetch=3,
            grid=(n_q, KEY_SLOTS),
            in_specs=[
                pl.BlockSpec((SPAN, q_cols), lambda i, j, t, s, c: (i, 0)),
                pl.BlockSpec((SPAN, 1), lambda i, j, t, s, c: (i, 0)),
                pl.BlockSpec((SPAN, 1), lambda i, j, t, s, c: (i, 0)),
                pl.BlockSpec((None, SPAN, HEAD_DIM), lambda i, j, t, s, c: (0, t[i, j], 0)),
                pl.BlockSpec((None, SPAN, HEAD_DIM), lambda i, j, t, s, c: (1, t[i, j], 0)),
            ],
            out_specs=pl.BlockSpec((SPAN, q_cols), lambda i, j, t, s, c: (i, 0)),
            scratch_shapes=[
                pltpu.VMEM((heads, SPAN, 1), jnp.float32),
                pltpu.VMEM((heads, SPAN, 1), jnp.float32),
                pltpu.VMEM((heads, SPAN, HEAD_DIM), jnp.float32),
            ],
        ),
        compiler_params=pltpu.CompilerParams(dimension_semantics=("arbitrary", "arbitrary")),
        cost_estimate=cost,
    )(tbl, seq, cnt, queries, qpos, qstart, kv, kv)


def key_tables(span_order, doc_ends, query_spans):
    n_spans = span_order.shape[0]
    span_ids = jnp.arange(n_spans, dtype=jnp.int32)
    inverse = jnp.sum(
        jnp.where(span_order[None, :] == span_ids[:, None], span_ids[None, :], 0), axis=1)
    first_doc = jnp.sum((doc_ends[None, :] <= (span_ids * SPAN)[:, None]).astype(jnp.int32), axis=1)
    last_doc = jnp.sum(
        (doc_ends[None, :] <= (span_ids * SPAN + SPAN - 1)[:, None]).astype(jnp.int32), axis=1)
    sq = jnp.sum(jnp.where(query_spans[:, None] == span_ids[None, :], span_order[None, :], 0), axis=1)
    q_first = jnp.sum(jnp.where(sq[:, None] == span_ids[None, :], first_doc[None, :], 0), axis=1)
    back = jnp.arange(KEY_SLOTS, dtype=jnp.int32) - (KEY_SLOTS - 1)
    cand = sq[:, None] + back[None, :]
    cand_last = jnp.sum(
        jnp.where(cand[:, :, None] == span_ids[None, None, :], last_doc[None, None, :], 0), axis=2)
    valid = (cand >= 0) & (cand_last >= q_first[:, None])
    count = jnp.sum(valid.astype(jnp.int32), axis=1)
    slot = jnp.arange(KEY_SLOTS, dtype=jnp.int32)
    seq = jnp.minimum(sq[:, None] - count[:, None] + 1 + slot[None, :], sq[:, None])
    tbl = jnp.sum(jnp.where(seq[:, :, None] == span_ids[None, None, :], inverse[None, None, :], 0),
                  axis=2)
    return tbl.astype(jnp.int32), seq.astype(jnp.int32), count.astype(jnp.int32)


def per_device(tokens, norm_gain, q_weight, k_weight, v_weight, o_weight, doc_lengths, span_order):
    local_rows = tokens.shape[1]
    tok_dev = local_rows * lax.axis_size(TENSOR)
    model_width = tokens.shape[2]
    head_dim = HEAD_DIM
    q_cols = q_weight.shape[1]
    kv_cols = k_weight.shape[1]
    q_heads = q_cols // head_dim
    kv_local = kv_cols // head_dim
    span_rows = tok_dev // 2
    base_row = lax.axis_index(CONTEXT) * tok_dev
    rows_float = tokens.astype(jnp.float32)
    normed = (
        rows_float
        * lax.rsqrt(jnp.mean(rows_float * rows_float, axis=-1, keepdims=True) + epsilon)
        * norm_gain
    ).astype(jnp.bfloat16)
    portion = lax.all_gather(normed, TENSOR, axis=1, tiled=True)
    row_count = portion.shape[1]
    flat_rows = portion.reshape(row_count, model_width)
    places = positions(base_row + jnp.arange(row_count, dtype=jnp.int32), span_order, span_rows)
    query_rows = jnp.dot(flat_rows, q_weight, preferred_element_type=jnp.float32).reshape(
        row_count, q_heads, head_dim
    )
    key_rows = jnp.dot(flat_rows, k_weight, preferred_element_type=jnp.float32).reshape(
        row_count, kv_local, head_dim
    )
    value_rows = jnp.dot(flat_rows, v_weight, preferred_element_type=jnp.float32).astype(
        jnp.bfloat16
    )
    query_rows = rotary(query_rows, places).reshape(row_count, q_cols).astype(jnp.bfloat16)
    key_rows = rotary(key_rows, places).reshape(row_count, kv_cols).astype(jnp.bfloat16)
    kv_pair = jnp.stack([key_rows, value_rows])
    gathered = lax.all_gather(kv_pair, CONTEXT, axis=1, tiled=True)

    doc_ends = jnp.cumsum(doc_lengths)
    query_start = jnp.max(
        jnp.where(doc_ends[None, :] <= places[:, None], doc_ends[None, :], 0), axis=1)
    query_spans = lax.axis_index(CONTEXT) * 2 + jnp.arange(2, dtype=jnp.int32)
    tbl, seq, cnt = key_tables(span_order, doc_ends, query_spans)
    attended = span_attention(
        tbl, seq, cnt, query_rows,
        places.astype(jnp.int32)[:, None], query_start.astype(jnp.int32)[:, None],
        gathered,
    )
    partner_o = lax.ppermute(o_weight, ("yh", "ylo"), [(0, 3), (3, 0), (1, 2), (2, 1)])
    plane = lax.axis_index("yh")
    half = row_count // 2
    own_rows = lax.dynamic_slice_in_dim(attended, plane * half, half, 0)
    other_rows = lax.dynamic_slice_in_dim(attended, (1 - plane) * half, half, 0)
    partner_rows = lax.ppermute(other_rows, "yh", [(0, 1), (1, 0)])
    mixed = jnp.dot(
        jnp.concatenate([own_rows, partner_rows], axis=1),
        jnp.concatenate([o_weight, partner_o], axis=0),
        preferred_element_type=jnp.float32,
    ).astype(jnp.bfloat16)
    mixed_rows = lax.psum_scatter(mixed, "x", scatter_dimension=0, tiled=True)
    return mixed_rows.reshape(tokens.shape)


TENSOR = ("yh", "x")
CONTEXT = ("z", "ylo", "core")


def solution(mesh):
    devices = mesh.devices.reshape(2, mesh.devices.shape[0] // 2, -1, 2, 2)
    split_mesh = jax.sharding.Mesh(devices, ("yh", "x", "z", "ylo", "core"))
    in_specs = (
        P(CONTEXT, TENSOR, None),
        P(),
        P(None, TENSOR),
        P(None, TENSOR),
        P(None, TENSOR),
        P(TENSOR, None),
        P(),
        P(),
    )
    out_specs = P(CONTEXT, TENSOR, None)
    return jax.shard_map(
        per_device, mesh=split_mesh, in_specs=in_specs, out_specs=out_specs, check_vma=False
    )
```

```python
import functools
import math

import jax
import jax.numpy as jnp
from jax import lax
from jax.experimental import pallas as pl
from jax.experimental.pallas import tpu as pltpu
from jax.sharding import PartitionSpec as P

HEAD_DIM = 128
SPAN = 512
KEY_SLOTS = 9

rope_theta = 500000.0
epsilon = 1e-05
masked_score = -1e30


def positions(rows, span_order, span_rows):
    slot_ids = jnp.arange(span_order.shape[0], dtype=jnp.int32)
    matches = (rows // span_rows)[:, None] == slot_ids[None, :]
    picked = jnp.sum(jnp.where(matches, span_order[None, :], 0), axis=1)
    return picked * span_rows + rows % span_rows


def rotary(values, places):
    head_dim = values.shape[-1]
    half_dim = head_dim // 2
    frequency = rope_theta ** (-(2.0 / head_dim) * jnp.arange(half_dim, dtype=jnp.float32))
    angles = places.astype(jnp.float32)[:, None] * frequency[None, :]
    cosine = jnp.cos(angles)[:, None, :]
    sine_part = jnp.sin(angles)[:, None, :]
    first_half = values[..., :half_dim]
    second = values[..., half_dim:]
    return jnp.concatenate(
        [first_half * cosine - second * sine_part, second * cosine + first_half * sine_part],
        axis=-1,
    )


def attention_kernel(heads, scale, tbl_ref, seq_ref, cnt_ref, q_ref, qpos_ref, qstart_ref,
                     k_ref, v_ref, o_ref, m_sc, l_sc, acc_sc):
    i = pl.program_id(0)
    j = pl.program_id(1)

    @pl.when(j == 0)
    def _():
        m_sc[...] = jnp.full_like(m_sc, masked_score)
        l_sc[...] = jnp.zeros_like(l_sc)
        acc_sc[...] = jnp.zeros_like(acc_sc)

    @pl.when(j < cnt_ref[i])
    def _():
        k = k_ref[...]
        v = v_ref[...]
        span = k.shape[0]
        kpos = seq_ref[i, j] * span + lax.broadcasted_iota(jnp.int32, (1, span), 1)
        visible = (kpos <= qpos_ref[...]) & (kpos >= qstart_ref[...])
        for h in range(heads):
            q = q_ref[:, h * HEAD_DIM:(h + 1) * HEAD_DIM]
            s = lax.dot_general(q, k, (((1,), (1,)), ((), ())),
                                preferred_element_type=jnp.float32) * scale
            m_old = m_sc[h]
            m_new = jnp.maximum(
                m_old, jnp.max(jnp.where(visible, s, masked_score), axis=-1, keepdims=True))
            p = jnp.where(visible, jnp.exp(s - m_new), 0.0)
            alpha = jnp.exp(m_old - m_new)
            l_sc[h] = alpha * l_sc[h] + jnp.sum(p, axis=-1, keepdims=True)
            acc_sc[h] = alpha * acc_sc[h] + jnp.dot(
                p.astype(jnp.bfloat16), v, preferred_element_type=jnp.float32)
            m_sc[h] = m_new

    @pl.when(j == pl.num_programs(1) - 1)
    def _():
        for h in range(heads):
            o_ref[:, h * HEAD_DIM:(h + 1) * HEAD_DIM] = (acc_sc[h] / l_sc[h]).astype(o_ref.dtype)


def span_attention(tbl, seq, cnt, queries, qpos, qstart, kv):
    rows, q_cols = queries.shape
    heads = q_cols // HEAD_DIM
    n_q = rows // SPAN
    kernel = functools.partial(attention_kernel, heads, 1.0 / math.sqrt(HEAD_DIM))
    steps = n_q * KEY_SLOTS
    cost = pl.CostEstimate(
        flops=4 * steps * heads * SPAN * SPAN * HEAD_DIM,
        transcendentals=steps * heads * SPAN * SPAN,
        bytes_accessed=steps * 2 * SPAN * HEAD_DIM * 2 + 2 * rows * q_cols * 2,
    )
    return pl.pallas_call(
        kernel,
        out_shape=jax.ShapeDtypeStruct((rows, q_cols), jnp.bfloat16),
        grid_spec=pltpu.PrefetchScalarGridSpec(
            num_scalar_prefetch=3,
            grid=(n_q, KEY_SLOTS),
            in_specs=[
                pl.BlockSpec((SPAN, q_cols), lambda i, j, t, s, c: (i, 0)),
                pl.BlockSpec((SPAN, 1), lambda i, j, t, s, c: (i, 0)),
                pl.BlockSpec((SPAN, 1), lambda i, j, t, s, c: (i, 0)),
                pl.BlockSpec((None, SPAN, HEAD_DIM), lambda i, j, t, s, c: (0, t[i, j], 0)),
                pl.BlockSpec((None, SPAN, HEAD_DIM), lambda i, j, t, s, c: (1, t[i, j], 0)),
            ],
            out_specs=pl.BlockSpec((SPAN, q_cols), lambda i, j, t, s, c: (i, 0)),
            scratch_shapes=[
                pltpu.VMEM((heads, SPAN, 1), jnp.float32),
                pltpu.VMEM((heads, SPAN, 1), jnp.float32),
                pltpu.VMEM((heads, SPAN, HEAD_DIM), jnp.float32),
            ],
        ),
        compiler_params=pltpu.CompilerParams(dimension_semantics=("arbitrary", "arbitrary")),
        cost_estimate=cost,
    )(tbl, seq, cnt, queries, qpos, qstart, kv, kv)


def key_tables(span_order, doc_ends, query_spans):
    n_spans = span_order.shape[0]
    span_ids = jnp.arange(n_spans, dtype=jnp.int32)
    inverse = jnp.sum(
        jnp.where(span_order[None, :] == span_ids[:, None], span_ids[None, :], 0), axis=1)
    first_doc = jnp.sum((doc_ends[None, :] <= (span_ids * SPAN)[:, None]).astype(jnp.int32), axis=1)
    last_doc = jnp.sum(
        (doc_ends[None, :] <= (span_ids * SPAN + SPAN - 1)[:, None]).astype(jnp.int32), axis=1)
    sq = jnp.sum(jnp.where(query_spans[:, None] == span_ids[None, :], span_order[None, :], 0), axis=1)
    q_first = jnp.sum(jnp.where(sq[:, None] == span_ids[None, :], first_doc[None, :], 0), axis=1)
    back = jnp.arange(KEY_SLOTS, dtype=jnp.int32) - (KEY_SLOTS - 1)
    cand = sq[:, None] + back[None, :]
    cand_last = jnp.sum(
        jnp.where(cand[:, :, None] == span_ids[None, None, :], last_doc[None, None, :], 0), axis=2)
    valid = (cand >= 0) & (cand_last >= q_first[:, None])
    count = jnp.sum(valid.astype(jnp.int32), axis=1)
    slot = jnp.arange(KEY_SLOTS, dtype=jnp.int32)
    seq = jnp.minimum(sq[:, None] - count[:, None] + 1 + slot[None, :], sq[:, None])
    tbl = jnp.sum(jnp.where(seq[:, :, None] == span_ids[None, None, :], inverse[None, None, :], 0),
                  axis=2)
    return tbl.astype(jnp.int32), seq.astype(jnp.int32), count.astype(jnp.int32)


def per_device(tokens, norm_gain, q_weight, k_weight, v_weight, o_weight, doc_lengths, span_order):
    local_rows = tokens.shape[1]
    tok_dev = local_rows * lax.axis_size(TENSOR)
    model_width = tokens.shape[2]
    head_dim = HEAD_DIM
    q_cols = q_weight.shape[1]
    kv_cols = k_weight.shape[1]
    q_heads = q_cols // head_dim
    kv_local = kv_cols // head_dim
    span_rows = tok_dev // 2
    base_row = lax.axis_index(CONTEXT) * tok_dev
    rows_float = tokens.astype(jnp.float32)
    normed = (
        rows_float
        * lax.rsqrt(jnp.mean(rows_float * rows_float, axis=-1, keepdims=True) + epsilon)
        * norm_gain
    ).astype(jnp.bfloat16)
    plane = lax.axis_index("yh")
    core = lax.axis_index("core")
    weights = jnp.concatenate([q_weight, k_weight, v_weight], axis=1)
    half_in = weights.shape[0] // 2
    sent_half = lax.dynamic_slice_in_dim(weights, core * half_in, half_in, 0)
    partner_half = lax.ppermute(sent_half, ("yh", "ylo"), NEIGHBOUR)
    partner_weights = lax.all_gather(partner_half, "core", axis=0, tiled=True)
    plane_rows = lax.all_gather(normed, "x", axis=1, tiled=True)
    half = plane_rows.shape[1]
    flat_rows = plane_rows.reshape(half, model_width)
    all_places = positions(base_row + jnp.arange(tok_dev, dtype=jnp.int32), span_order, span_rows)
    places = lax.dynamic_slice_in_dim(all_places, plane * half, half, 0)

    def project(w):
        out = jnp.dot(flat_rows, w, preferred_element_type=jnp.float32)
        q = rotary(out[:, :q_cols].reshape(half, q_heads, head_dim), places)
        k = rotary(out[:, q_cols:q_cols + kv_cols].reshape(half, kv_local, head_dim), places)
        return jnp.concatenate(
            [q.reshape(half, q_cols), k.reshape(half, kv_cols), out[:, q_cols + kv_cols:]], axis=1
        ).astype(jnp.bfloat16)

    own = project(weights)
    for_partner = project(partner_weights)
    received = lax.ppermute(for_partner, "yh", [(0, 1), (1, 0)])
    first = jnp.where(plane == 0, own, received)
    second = jnp.where(plane == 0, received, own)
    projected = jnp.concatenate([first, second], axis=0)
    query_rows = projected[:, :q_cols]
    kv_pair = jnp.stack([projected[:, q_cols:q_cols + kv_cols], projected[:, q_cols + kv_cols:]])
    gathered = lax.all_gather(kv_pair, CONTEXT, axis=1, tiled=True)
    places = all_places
    row_count = tok_dev

    doc_ends = jnp.cumsum(doc_lengths)
    query_start = jnp.max(
        jnp.where(doc_ends[None, :] <= places[:, None], doc_ends[None, :], 0), axis=1)
    query_spans = lax.axis_index(CONTEXT) * 2 + jnp.arange(2, dtype=jnp.int32)
    tbl, seq, cnt = key_tables(span_order, doc_ends, query_spans)
    attended = span_attention(
        tbl, seq, cnt, query_rows,
        places.astype(jnp.int32)[:, None], query_start.astype(jnp.int32)[:, None],
        gathered,
    )
    o_half = o_weight.shape[0] // 2
    o_sent = lax.dynamic_slice_in_dim(o_weight, core * o_half, o_half, 0)
    partner_o = lax.all_gather(
        lax.ppermute(o_sent, ("yh", "ylo"), NEIGHBOUR), "core", axis=0, tiled=True)
    half = row_count // 2
    own_rows = lax.dynamic_slice_in_dim(attended, plane * half, half, 0)
    other_rows = lax.dynamic_slice_in_dim(attended, (1 - plane) * half, half, 0)
    partner_rows = lax.ppermute(other_rows, "yh", [(0, 1), (1, 0)])
    mixed = jnp.dot(
        jnp.concatenate([own_rows, partner_rows], axis=1),
        jnp.concatenate([o_weight, partner_o], axis=0),
        preferred_element_type=jnp.float32,
    ).astype(jnp.bfloat16)
    mixed_rows = lax.psum_scatter(mixed, "x", scatter_dimension=0, tiled=True)
    return mixed_rows.reshape(tokens.shape)


TENSOR = ("yh", "x")
NEIGHBOUR = [(0, 3), (3, 0), (1, 2), (2, 1)]
CONTEXT = ("z", "ylo", "core")


def solution(mesh):
    devices = mesh.devices.reshape(2, mesh.devices.shape[0] // 2, -1, 2, 2)
    split_mesh = jax.sharding.Mesh(devices, ("yh", "x", "z", "ylo", "core"))
    in_specs = (
        P(CONTEXT, TENSOR, None),
        P(),
        P(None, TENSOR),
        P(None, TENSOR),
        P(None, TENSOR),
        P(TENSOR, None),
        P(),
        P(),
    )
    out_specs = P(CONTEXT, TENSOR, None)
    return jax.shard_map(
        per_device, mesh=split_mesh, in_specs=in_specs, out_specs=out_specs, check_vma=False
    )
```

```python
import functools
import math

import jax
import jax.numpy as jnp
from jax import lax
from jax.experimental import pallas as pl
from jax.experimental.pallas import tpu as pltpu
from jax.sharding import PartitionSpec as P

HEAD_DIM = 128
SPAN = 512
KEY_SLOTS = 9

rope_theta = 500000.0
epsilon = 1e-05
masked_score = -1e30


def positions(rows, span_order, span_rows):
    slot_ids = jnp.arange(span_order.shape[0], dtype=jnp.int32)
    matches = (rows // span_rows)[:, None] == slot_ids[None, :]
    picked = jnp.sum(jnp.where(matches, span_order[None, :], 0), axis=1)
    return picked * span_rows + rows % span_rows


def rotary(values, places):
    head_dim = values.shape[-1]
    half_dim = head_dim // 2
    frequency = rope_theta ** (-(2.0 / head_dim) * jnp.arange(half_dim, dtype=jnp.float32))
    angles = places.astype(jnp.float32)[:, None] * frequency[None, :]
    cosine = jnp.cos(angles)[:, None, :]
    sine_part = jnp.sin(angles)[:, None, :]
    first_half = values[..., :half_dim]
    second = values[..., half_dim:]
    return jnp.concatenate(
        [first_half * cosine - second * sine_part, second * cosine + first_half * sine_part],
        axis=-1,
    )


def attention_kernel(heads, scale, tbl_ref, seq_ref, cnt_ref, q_ref, qpos_ref, qstart_ref,
                     k_ref, v_ref, o_ref, m_sc, l_sc, acc_sc):
    i = pl.program_id(0)
    j = pl.program_id(1)

    @pl.when(j == 0)
    def _():
        m_sc[...] = jnp.full_like(m_sc, masked_score)
        l_sc[...] = jnp.zeros_like(l_sc)
        acc_sc[...] = jnp.zeros_like(acc_sc)

    @pl.when(j < cnt_ref[i])
    def _():
        k = k_ref[...]
        v = v_ref[...]
        span = k.shape[0]
        kpos = seq_ref[i, j] * span + lax.broadcasted_iota(jnp.int32, (1, span), 1)
        visible = (kpos <= qpos_ref[...]) & (kpos >= qstart_ref[...])
        for h in range(heads):
            q = q_ref[:, h * HEAD_DIM:(h + 1) * HEAD_DIM]
            s = lax.dot_general(q, k, (((1,), (1,)), ((), ())),
                                preferred_element_type=jnp.float32) * scale
            m_old = m_sc[h]
            m_new = jnp.maximum(
                m_old, jnp.max(jnp.where(visible, s, masked_score), axis=-1, keepdims=True))
            p = jnp.where(visible, jnp.exp(s - m_new), 0.0)
            alpha = jnp.exp(m_old - m_new)
            l_sc[h] = alpha * l_sc[h] + jnp.sum(p, axis=-1, keepdims=True)
            acc_sc[h] = alpha * acc_sc[h] + jnp.dot(
                p.astype(jnp.bfloat16), v, preferred_element_type=jnp.float32)
            m_sc[h] = m_new

    @pl.when(j == pl.num_programs(1) - 1)
    def _():
        for h in range(heads):
            o_ref[:, h * HEAD_DIM:(h + 1) * HEAD_DIM] = (acc_sc[h] / l_sc[h]).astype(o_ref.dtype)


def span_attention(tbl, seq, cnt, queries, qpos, qstart, kv):
    rows, q_cols = queries.shape
    heads = q_cols // HEAD_DIM
    n_q = rows // SPAN
    kernel = functools.partial(attention_kernel, heads, 1.0 / math.sqrt(HEAD_DIM))
    steps = n_q * KEY_SLOTS
    cost = pl.CostEstimate(
        flops=4 * steps * heads * SPAN * SPAN * HEAD_DIM,
        transcendentals=steps * heads * SPAN * SPAN,
        bytes_accessed=steps * 2 * SPAN * HEAD_DIM * 2 + 2 * rows * q_cols * 2,
    )
    return pl.pallas_call(
        kernel,
        out_shape=jax.ShapeDtypeStruct((rows, q_cols), jnp.bfloat16),
        grid_spec=pltpu.PrefetchScalarGridSpec(
            num_scalar_prefetch=3,
            grid=(n_q, KEY_SLOTS),
            in_specs=[
                pl.BlockSpec((SPAN, q_cols), lambda i, j, t, s, c: (i, 0)),
                pl.BlockSpec((SPAN, 1), lambda i, j, t, s, c: (i, 0)),
                pl.BlockSpec((SPAN, 1), lambda i, j, t, s, c: (i, 0)),
                pl.BlockSpec((None, SPAN, HEAD_DIM), lambda i, j, t, s, c: (0, t[i, j], 0)),
                pl.BlockSpec((None, SPAN, HEAD_DIM), lambda i, j, t, s, c: (1, t[i, j], 0)),
            ],
            out_specs=pl.BlockSpec((SPAN, q_cols), lambda i, j, t, s, c: (i, 0)),
            scratch_shapes=[
                pltpu.VMEM((heads, SPAN, 1), jnp.float32),
                pltpu.VMEM((heads, SPAN, 1), jnp.float32),
                pltpu.VMEM((heads, SPAN, HEAD_DIM), jnp.float32),
            ],
        ),
        compiler_params=pltpu.CompilerParams(dimension_semantics=("arbitrary", "arbitrary")),
        cost_estimate=cost,
    )(tbl, seq, cnt, queries, qpos, qstart, kv, kv)


def key_tables(span_order, doc_ends, query_spans):
    n_spans = span_order.shape[0]
    span_ids = jnp.arange(n_spans, dtype=jnp.int32)
    inverse = jnp.sum(
        jnp.where(span_order[None, :] == span_ids[:, None], span_ids[None, :], 0), axis=1)
    first_doc = jnp.sum((doc_ends[None, :] <= (span_ids * SPAN)[:, None]).astype(jnp.int32), axis=1)
    last_doc = jnp.sum(
        (doc_ends[None, :] <= (span_ids * SPAN + SPAN - 1)[:, None]).astype(jnp.int32), axis=1)
    sq = jnp.sum(jnp.where(query_spans[:, None] == span_ids[None, :], span_order[None, :], 0), axis=1)
    q_first = jnp.sum(jnp.where(sq[:, None] == span_ids[None, :], first_doc[None, :], 0), axis=1)
    back = jnp.arange(KEY_SLOTS, dtype=jnp.int32) - (KEY_SLOTS - 1)
    cand = sq[:, None] + back[None, :]
    cand_last = jnp.sum(
        jnp.where(cand[:, :, None] == span_ids[None, None, :], last_doc[None, None, :], 0), axis=2)
    valid = (cand >= 0) & (cand_last >= q_first[:, None])
    count = jnp.sum(valid.astype(jnp.int32), axis=1)
    slot = jnp.arange(KEY_SLOTS, dtype=jnp.int32)
    seq = jnp.minimum(sq[:, None] - count[:, None] + 1 + slot[None, :], sq[:, None])
    tbl = jnp.sum(jnp.where(seq[:, :, None] == span_ids[None, None, :], inverse[None, None, :], 0),
                  axis=2)
    return tbl.astype(jnp.int32), seq.astype(jnp.int32), count.astype(jnp.int32)


def per_device(tokens, norm_gain, q_weight, k_weight, v_weight, o_weight, doc_lengths, span_order):
    local_rows = tokens.shape[1]
    tok_dev = local_rows * lax.axis_size(TENSOR)
    model_width = tokens.shape[2]
    head_dim = HEAD_DIM
    q_cols = q_weight.shape[1]
    kv_cols = k_weight.shape[1]
    q_heads = q_cols // head_dim
    kv_local = kv_cols // head_dim
    span_rows = tok_dev // 2
    base_row = lax.axis_index(CONTEXT) * tok_dev
    rows_float = tokens.astype(jnp.float32)
    normed = (
        rows_float
        * lax.rsqrt(jnp.mean(rows_float * rows_float, axis=-1, keepdims=True) + epsilon)
        * norm_gain
    ).astype(jnp.bfloat16)
    plane = lax.axis_index("yh")
    core = lax.axis_index("core")
    weights = jnp.concatenate([q_weight, k_weight, v_weight], axis=1)
    half_in = weights.shape[0] // 2
    sent_half = lax.dynamic_slice_in_dim(weights, core * half_in, half_in, 0)
    plane_rows = lax.all_gather(normed, "x", axis=1, tiled=True)
    partner_half = lax.ppermute(sent_half, ("yh", "ylo"), NEIGHBOUR)
    plane_rows, partner_half = lax.optimization_barrier((plane_rows, partner_half))
    other_half = lax.ppermute(partner_half, "core", [(0, 1), (1, 0)])
    half = plane_rows.shape[1]
    flat_rows = plane_rows.reshape(half, model_width)
    all_places = positions(base_row + jnp.arange(tok_dev, dtype=jnp.int32), span_order, span_rows)
    places = lax.dynamic_slice_in_dim(all_places, plane * half, half, 0)
    rows_mine = lax.dynamic_slice_in_dim(flat_rows, core * half_in, half_in, 1)
    rows_other = lax.dynamic_slice_in_dim(flat_rows, (1 - core) * half_in, half_in, 1)

    def finish(out):
        q = rotary(out[:, :q_cols].reshape(half, q_heads, head_dim), places)
        k = rotary(out[:, q_cols:q_cols + kv_cols].reshape(half, kv_local, head_dim), places)
        return jnp.concatenate(
            [q.reshape(half, q_cols), k.reshape(half, kv_cols), out[:, q_cols + kv_cols:]], axis=1
        ).astype(jnp.bfloat16)

    def project(w):
        return finish(jnp.dot(flat_rows, w, preferred_element_type=jnp.float32))

    own = project(weights)
    for_partner = finish(
        jnp.dot(rows_mine, partner_half, preferred_element_type=jnp.float32)
        + jnp.dot(rows_other, other_half, preferred_element_type=jnp.float32))
    received = lax.ppermute(for_partner, "yh", [(0, 1), (1, 0)])
    first = jnp.where(plane == 0, own, received)
    second = jnp.where(plane == 0, received, own)
    projected = jnp.concatenate([first, second], axis=0)
    query_rows = projected[:, :q_cols]
    kv_pair = jnp.stack([projected[:, q_cols:q_cols + kv_cols], projected[:, q_cols + kv_cols:]])
    gathered = lax.all_gather(kv_pair, CONTEXT, axis=1, tiled=True)
    places = all_places
    row_count = tok_dev

    doc_ends = jnp.cumsum(doc_lengths)
    query_start = jnp.max(
        jnp.where(doc_ends[None, :] <= places[:, None], doc_ends[None, :], 0), axis=1)
    query_spans = lax.axis_index(CONTEXT) * 2 + jnp.arange(2, dtype=jnp.int32)
    tbl, seq, cnt = key_tables(span_order, doc_ends, query_spans)
    attended = span_attention(
        tbl, seq, cnt, query_rows,
        places.astype(jnp.int32)[:, None], query_start.astype(jnp.int32)[:, None],
        gathered,
    )
    partner_o = lax.ppermute(o_weight, ("yh", "ylo"), NEIGHBOUR)
    half = row_count // 2
    own_rows = lax.dynamic_slice_in_dim(attended, plane * half, half, 0)
    other_rows = lax.dynamic_slice_in_dim(attended, (1 - plane) * half, half, 0)
    partner_rows = lax.ppermute(other_rows, "yh", [(0, 1), (1, 0)])
    mixed = jnp.dot(
        jnp.concatenate([own_rows, partner_rows], axis=1),
        jnp.concatenate([o_weight, partner_o], axis=0),
        preferred_element_type=jnp.float32,
    ).astype(jnp.bfloat16)
    mixed_rows = lax.psum_scatter(mixed, "x", scatter_dimension=0, tiled=True)
    return mixed_rows.reshape(tokens.shape)


TENSOR = ("yh", "x")
NEIGHBOUR = [(0, 3), (3, 0), (1, 2), (2, 1)]
CONTEXT = ("z", "ylo", "core")


def solution(mesh):
    devices = mesh.devices.reshape(2, mesh.devices.shape[0] // 2, -1, 2, 2)
    split_mesh = jax.sharding.Mesh(devices, ("yh", "x", "z", "ylo", "core"))
    in_specs = (
        P(CONTEXT, TENSOR, None),
        P(),
        P(None, TENSOR),
        P(None, TENSOR),
        P(None, TENSOR),
        P(TENSOR, None),
        P(),
        P(),
    )
    out_specs = P(CONTEXT, TENSOR, None)
    return jax.shard_map(
        per_device, mesh=split_mesh, in_specs=in_specs, out_specs=out_specs, check_vma=False
    )
```

```python
import functools
import math

import jax
import jax.numpy as jnp
from jax import lax
from jax.experimental import pallas as pl
from jax.experimental.pallas import tpu as pltpu
from jax.sharding import PartitionSpec as P

HEAD_DIM = 128
SPAN = 512
KEY_SLOTS = 9

rope_theta = 500000.0
epsilon = 1e-05
masked_score = -1e30


def positions(rows, span_order, span_rows):
    slot_ids = jnp.arange(span_order.shape[0], dtype=jnp.int32)
    matches = (rows // span_rows)[:, None] == slot_ids[None, :]
    picked = jnp.sum(jnp.where(matches, span_order[None, :], 0), axis=1)
    return picked * span_rows + rows % span_rows


def rotary(values, places):
    head_dim = values.shape[-1]
    half_dim = head_dim // 2
    frequency = rope_theta ** (-(2.0 / head_dim) * jnp.arange(half_dim, dtype=jnp.float32))
    angles = places.astype(jnp.float32)[:, None] * frequency[None, :]
    cosine = jnp.cos(angles)[:, None, :]
    sine_part = jnp.sin(angles)[:, None, :]
    first_half = values[..., :half_dim]
    second = values[..., half_dim:]
    return jnp.concatenate(
        [first_half * cosine - second * sine_part, second * cosine + first_half * sine_part],
        axis=-1,
    )


def attention_kernel(heads, scale, tbl_ref, seq_ref, cnt_ref, q_ref, qpos_ref, qstart_ref,
                     k_ref, v_ref, o_ref, m_sc, l_sc, acc_sc):
    i = pl.program_id(0)
    j = pl.program_id(1)

    @pl.when(j == 0)
    def _():
        m_sc[...] = jnp.full_like(m_sc, masked_score)
        l_sc[...] = jnp.zeros_like(l_sc)
        acc_sc[...] = jnp.zeros_like(acc_sc)

    @pl.when(j < cnt_ref[i])
    def _():
        k = k_ref[...]
        v = v_ref[...]
        span = k.shape[0]
        kpos = seq_ref[i, j] * span + lax.broadcasted_iota(jnp.int32, (1, span), 1)
        visible = (kpos <= qpos_ref[...]) & (kpos >= qstart_ref[...])
        for h in range(heads):
            q = q_ref[:, h * HEAD_DIM:(h + 1) * HEAD_DIM]
            s = lax.dot_general(q, k, (((1,), (1,)), ((), ())),
                                preferred_element_type=jnp.float32) * scale
            m_old = m_sc[h]
            m_new = jnp.maximum(
                m_old, jnp.max(jnp.where(visible, s, masked_score), axis=-1, keepdims=True))
            p = jnp.where(visible, jnp.exp(s - m_new), 0.0)
            alpha = jnp.exp(m_old - m_new)
            l_sc[h] = alpha * l_sc[h] + jnp.sum(p, axis=-1, keepdims=True)
            acc_sc[h] = alpha * acc_sc[h] + jnp.dot(
                p.astype(jnp.bfloat16), v, preferred_element_type=jnp.float32)
            m_sc[h] = m_new

    @pl.when(j == pl.num_programs(1) - 1)
    def _():
        for h in range(heads):
            o_ref[:, h * HEAD_DIM:(h + 1) * HEAD_DIM] = (acc_sc[h] / l_sc[h]).astype(o_ref.dtype)


def span_attention(tbl, seq, cnt, queries, qpos, qstart, kv):
    rows, q_cols = queries.shape
    heads = q_cols // HEAD_DIM
    n_q = rows // SPAN
    kernel = functools.partial(attention_kernel, heads, 1.0 / math.sqrt(HEAD_DIM))
    steps = n_q * KEY_SLOTS
    cost = pl.CostEstimate(
        flops=4 * steps * heads * SPAN * SPAN * HEAD_DIM,
        transcendentals=steps * heads * SPAN * SPAN,
        bytes_accessed=steps * 2 * SPAN * HEAD_DIM * 2 + 2 * rows * q_cols * 2,
    )
    return pl.pallas_call(
        kernel,
        out_shape=jax.ShapeDtypeStruct((rows, q_cols), jnp.bfloat16),
        grid_spec=pltpu.PrefetchScalarGridSpec(
            num_scalar_prefetch=3,
            grid=(n_q, KEY_SLOTS),
            in_specs=[
                pl.BlockSpec((SPAN, q_cols), lambda i, j, t, s, c: (i, 0)),
                pl.BlockSpec((SPAN, 1), lambda i, j, t, s, c: (i, 0)),
                pl.BlockSpec((SPAN, 1), lambda i, j, t, s, c: (i, 0)),
                pl.BlockSpec((None, SPAN, HEAD_DIM), lambda i, j, t, s, c: (0, t[i, j], 0)),
                pl.BlockSpec((None, SPAN, HEAD_DIM), lambda i, j, t, s, c: (1, t[i, j], 0)),
            ],
            out_specs=pl.BlockSpec((SPAN, q_cols), lambda i, j, t, s, c: (i, 0)),
            scratch_shapes=[
                pltpu.VMEM((heads, SPAN, 1), jnp.float32),
                pltpu.VMEM((heads, SPAN, 1), jnp.float32),
                pltpu.VMEM((heads, SPAN, HEAD_DIM), jnp.float32),
            ],
        ),
        compiler_params=pltpu.CompilerParams(dimension_semantics=("arbitrary", "arbitrary")),
        cost_estimate=cost,
    )(tbl, seq, cnt, queries, qpos, qstart, kv, kv)


def key_tables(span_order, doc_ends, query_spans, cores):
    n_spans = span_order.shape[0]
    span_ids = jnp.arange(n_spans, dtype=jnp.int32)
    inverse = jnp.sum(
        jnp.where(span_order[None, :] == span_ids[:, None], span_ids[None, :], 0), axis=1)
    first_doc = jnp.sum((doc_ends[None, :] <= (span_ids * SPAN)[:, None]).astype(jnp.int32), axis=1)
    last_doc = jnp.sum(
        (doc_ends[None, :] <= (span_ids * SPAN + SPAN - 1)[:, None]).astype(jnp.int32), axis=1)
    sq = jnp.sum(jnp.where(query_spans[:, None] == span_ids[None, :], span_order[None, :], 0), axis=1)
    q_first = jnp.sum(jnp.where(sq[:, None] == span_ids[None, :], first_doc[None, :], 0), axis=1)
    back = jnp.arange(KEY_SLOTS, dtype=jnp.int32) - (KEY_SLOTS - 1)
    cand = sq[:, None] + back[None, :]
    cand_last = jnp.sum(
        jnp.where(cand[:, :, None] == span_ids[None, None, :], last_doc[None, None, :], 0), axis=2)
    valid = (cand >= 0) & (cand_last >= q_first[:, None])
    count = jnp.sum(valid.astype(jnp.int32), axis=1)
    slot = jnp.arange(KEY_SLOTS, dtype=jnp.int32)
    seq = jnp.minimum(sq[:, None] - count[:, None] + 1 + slot[None, :], sq[:, None])
    storage = jnp.sum(
        jnp.where(seq[:, :, None] == span_ids[None, None, :], inverse[None, None, :], 0), axis=2)
    block = storage // 2
    tbl = ((block % cores) * (n_spans // 2 // cores) + block // cores) * 2 + storage % 2
    return tbl.astype(jnp.int32), seq.astype(jnp.int32), count.astype(jnp.int32)


def per_device(tokens, norm_gain, q_weight, k_weight, v_weight, o_weight, doc_lengths, span_order):
    local_rows = tokens.shape[1]
    tok_dev = local_rows * lax.axis_size(TENSOR)
    model_width = tokens.shape[2]
    head_dim = HEAD_DIM
    q_cols = q_weight.shape[1]
    kv_cols = k_weight.shape[1]
    q_heads = q_cols // head_dim
    kv_local = kv_cols // head_dim
    span_rows = tok_dev // 2
    base_row = lax.axis_index(CONTEXT) * tok_dev
    rows_float = tokens.astype(jnp.float32)
    normed = (
        rows_float
        * lax.rsqrt(jnp.mean(rows_float * rows_float, axis=-1, keepdims=True) + epsilon)
        * norm_gain
    ).astype(jnp.bfloat16)
    plane = lax.axis_index("yh")
    core = lax.axis_index("core")
    weights = jnp.concatenate([q_weight, k_weight, v_weight], axis=1)
    half_in = weights.shape[0] // 2
    sent_half = lax.dynamic_slice_in_dim(weights, core * half_in, half_in, 0)
    plane_rows = lax.all_gather(normed, "x", axis=1, tiled=True)
    partner_half = lax.ppermute(sent_half, ("yh", "ylo"), NEIGHBOUR)
    plane_rows, partner_half = lax.optimization_barrier((plane_rows, partner_half))
    other_half = lax.ppermute(partner_half, "core", [(0, 1), (1, 0)])
    half = plane_rows.shape[1]
    flat_rows = plane_rows.reshape(half, model_width)
    all_places = positions(base_row + jnp.arange(tok_dev, dtype=jnp.int32), span_order, span_rows)
    places = lax.dynamic_slice_in_dim(all_places, plane * half, half, 0)
    rows_mine = lax.dynamic_slice_in_dim(flat_rows, core * half_in, half_in, 1)
    rows_other = lax.dynamic_slice_in_dim(flat_rows, (1 - core) * half_in, half_in, 1)

    def finish(out):
        q = rotary(out[:, :q_cols].reshape(half, q_heads, head_dim), places)
        k = rotary(out[:, q_cols:q_cols + kv_cols].reshape(half, kv_local, head_dim), places)
        return jnp.concatenate(
            [q.reshape(half, q_cols), k.reshape(half, kv_cols), out[:, q_cols + kv_cols:]], axis=1
        ).astype(jnp.bfloat16)

    def project(w):
        return finish(jnp.dot(flat_rows, w, preferred_element_type=jnp.float32))

    for_partner = finish(
        jnp.dot(rows_mine, partner_half, preferred_element_type=jnp.float32)
        + jnp.dot(rows_other, other_half, preferred_element_type=jnp.float32))
    received = lax.ppermute(for_partner, "yh", [(0, 1), (1, 0)])
    flat_rows, for_partner = lax.optimization_barrier((flat_rows, for_partner))
    own = project(weights)
    first = jnp.where(plane == 0, own, received)
    second = jnp.where(plane == 0, received, own)
    projected = jnp.concatenate([first, second], axis=0)
    query_rows = projected[:, :q_cols]
    kv_pair = jnp.stack([projected[:, q_cols:q_cols + kv_cols], projected[:, q_cols + kv_cols:]])
    gathered = lax.all_gather(
        lax.all_gather(kv_pair, ("z", "ylo"), axis=1, tiled=True), "core", axis=1, tiled=True)
    places = all_places
    row_count = tok_dev

    doc_ends = jnp.cumsum(doc_lengths)
    query_start = jnp.max(
        jnp.where(doc_ends[None, :] <= places[:, None], doc_ends[None, :], 0), axis=1)
    query_spans = lax.axis_index(CONTEXT) * 2 + jnp.arange(2, dtype=jnp.int32)
    tbl, seq, cnt = key_tables(span_order, doc_ends, query_spans, lax.axis_size("core"))
    attended = span_attention(
        tbl, seq, cnt, query_rows,
        places.astype(jnp.int32)[:, None], query_start.astype(jnp.int32)[:, None],
        gathered,
    )
    partner_o = lax.ppermute(o_weight, ("yh", "ylo"), NEIGHBOUR)
    half = row_count // 2
    own_rows = lax.dynamic_slice_in_dim(attended, plane * half, half, 0)
    other_rows = lax.dynamic_slice_in_dim(attended, (1 - plane) * half, half, 0)
    partner_rows = lax.ppermute(other_rows, "yh", [(0, 1), (1, 0)])
    mixed = jnp.dot(
        jnp.concatenate([own_rows, partner_rows], axis=1),
        jnp.concatenate([o_weight, partner_o], axis=0),
        preferred_element_type=jnp.float32,
    ).astype(jnp.bfloat16)
    mixed_rows = lax.psum_scatter(mixed, "x", scatter_dimension=0, tiled=True)
    return mixed_rows.reshape(tokens.shape)


TENSOR = ("yh", "x")
NEIGHBOUR = [(0, 3), (3, 0), (1, 2), (2, 1)]
CONTEXT = ("z", "ylo", "core")


def solution(mesh):
    devices = mesh.devices.reshape(2, mesh.devices.shape[0] // 2, -1, 2, 2)
    split_mesh = jax.sharding.Mesh(devices, ("yh", "x", "z", "ylo", "core"))
    in_specs = (
        P(CONTEXT, TENSOR, None),
        P(),
        P(None, TENSOR),
        P(None, TENSOR),
        P(None, TENSOR),
        P(TENSOR, None),
        P(),
        P(),
    )
    out_specs = P(CONTEXT, TENSOR, None)
    return jax.shard_map(
        per_device, mesh=split_mesh, in_specs=in_specs, out_specs=out_specs, check_vma=False
    )
```

```python
import functools
import math

import jax
import jax.numpy as jnp
from jax import lax
from jax.experimental import pallas as pl
from jax.experimental.pallas import tpu as pltpu
from jax.sharding import PartitionSpec as P

HEAD_DIM = 128
SPAN = 512
KEY_SLOTS = 9

rope_theta = 500000.0
epsilon = 1e-05
masked_score = -1e30


def positions(rows, span_order, span_rows):
    slot_ids = jnp.arange(span_order.shape[0], dtype=jnp.int32)
    matches = (rows // span_rows)[:, None] == slot_ids[None, :]
    picked = jnp.sum(jnp.where(matches, span_order[None, :], 0), axis=1)
    return picked * span_rows + rows % span_rows


def rotary(values, places):
    head_dim = values.shape[-1]
    half_dim = head_dim // 2
    frequency = rope_theta ** (-(2.0 / head_dim) * jnp.arange(half_dim, dtype=jnp.float32))
    angles = places.astype(jnp.float32)[:, None] * frequency[None, :]
    cosine = jnp.cos(angles)[:, None, :]
    sine_part = jnp.sin(angles)[:, None, :]
    first_half = values[..., :half_dim]
    second = values[..., half_dim:]
    return jnp.concatenate(
        [first_half * cosine - second * sine_part, second * cosine + first_half * sine_part],
        axis=-1,
    )


def attention_kernel(heads, scale, tbl_ref, seq_ref, cnt_ref, q_ref, qpos_ref, qstart_ref,
                     k_ref, v_ref, o_ref, m_sc, l_sc, acc_sc):
    i = pl.program_id(0)
    j = pl.program_id(1)

    @pl.when(j == 0)
    def _():
        m_sc[...] = jnp.full_like(m_sc, masked_score)
        l_sc[...] = jnp.zeros_like(l_sc)
        acc_sc[...] = jnp.zeros_like(acc_sc)

    @pl.when(j < cnt_ref[i])
    def _():
        k = k_ref[...]
        v = v_ref[...]
        span = k.shape[0]
        kpos = seq_ref[i, j] * span + lax.broadcasted_iota(jnp.int32, (1, span), 1)
        visible = (kpos <= qpos_ref[...]) & (kpos >= qstart_ref[...])
        for h in range(heads):
            q = q_ref[:, h * HEAD_DIM:(h + 1) * HEAD_DIM]
            s = lax.dot_general(q, k, (((1,), (1,)), ((), ())),
                                preferred_element_type=jnp.float32) * scale
            m_old = m_sc[h]
            m_new = jnp.maximum(
                m_old, jnp.max(jnp.where(visible, s, masked_score), axis=-1, keepdims=True))
            p = jnp.where(visible, jnp.exp(s - m_new), 0.0)
            alpha = jnp.exp(m_old - m_new)
            l_sc[h] = alpha * l_sc[h] + jnp.sum(p, axis=-1, keepdims=True)
            acc_sc[h] = alpha * acc_sc[h] + jnp.dot(
                p.astype(jnp.bfloat16), v, preferred_element_type=jnp.float32)
            m_sc[h] = m_new

    @pl.when(j == pl.num_programs(1) - 1)
    def _():
        for h in range(heads):
            o_ref[:, h * HEAD_DIM:(h + 1) * HEAD_DIM] = (acc_sc[h] / l_sc[h]).astype(o_ref.dtype)


def span_attention(tbl, seq, cnt, queries, qpos, qstart, kv):
    rows, q_cols = queries.shape
    heads = q_cols // HEAD_DIM
    n_q = rows // SPAN
    kernel = functools.partial(attention_kernel, heads, 1.0 / math.sqrt(HEAD_DIM))
    steps = n_q * KEY_SLOTS
    cost = pl.CostEstimate(
        flops=4 * steps * heads * SPAN * SPAN * HEAD_DIM,
        transcendentals=steps * heads * SPAN * SPAN,
        bytes_accessed=steps * 2 * SPAN * HEAD_DIM * 2 + 2 * rows * q_cols * 2,
    )
    return pl.pallas_call(
        kernel,
        out_shape=jax.ShapeDtypeStruct((rows, q_cols), jnp.bfloat16),
        grid_spec=pltpu.PrefetchScalarGridSpec(
            num_scalar_prefetch=3,
            grid=(n_q, KEY_SLOTS),
            in_specs=[
                pl.BlockSpec((SPAN, q_cols), lambda i, j, t, s, c: (i, 0)),
                pl.BlockSpec((SPAN, 1), lambda i, j, t, s, c: (i, 0)),
                pl.BlockSpec((SPAN, 1), lambda i, j, t, s, c: (i, 0)),
                pl.BlockSpec((None, SPAN, HEAD_DIM), lambda i, j, t, s, c: (0, t[i, j], 0)),
                pl.BlockSpec((None, SPAN, HEAD_DIM), lambda i, j, t, s, c: (1, t[i, j], 0)),
            ],
            out_specs=pl.BlockSpec((SPAN, q_cols), lambda i, j, t, s, c: (i, 0)),
            scratch_shapes=[
                pltpu.VMEM((heads, SPAN, 1), jnp.float32),
                pltpu.VMEM((heads, SPAN, 1), jnp.float32),
                pltpu.VMEM((heads, SPAN, HEAD_DIM), jnp.float32),
            ],
        ),
        compiler_params=pltpu.CompilerParams(dimension_semantics=("arbitrary", "arbitrary")),
        cost_estimate=cost,
    )(tbl, seq, cnt, queries, qpos, qstart, kv, kv)


def key_tables(span_order, doc_ends, query_spans):
    n_spans = span_order.shape[0]
    span_ids = jnp.arange(n_spans, dtype=jnp.int32)
    inverse = jnp.sum(
        jnp.where(span_order[None, :] == span_ids[:, None], span_ids[None, :], 0), axis=1)
    first_doc = jnp.sum((doc_ends[None, :] <= (span_ids * SPAN)[:, None]).astype(jnp.int32), axis=1)
    last_doc = jnp.sum(
        (doc_ends[None, :] <= (span_ids * SPAN + SPAN - 1)[:, None]).astype(jnp.int32), axis=1)
    sq = jnp.sum(jnp.where(query_spans[:, None] == span_ids[None, :], span_order[None, :], 0), axis=1)
    q_first = jnp.sum(jnp.where(sq[:, None] == span_ids[None, :], first_doc[None, :], 0), axis=1)
    back = jnp.arange(KEY_SLOTS, dtype=jnp.int32) - (KEY_SLOTS - 1)
    cand = sq[:, None] + back[None, :]
    cand_last = jnp.sum(
        jnp.where(cand[:, :, None] == span_ids[None, None, :], last_doc[None, None, :], 0), axis=2)
    valid = (cand >= 0) & (cand_last >= q_first[:, None])
    count = jnp.sum(valid.astype(jnp.int32), axis=1)
    slot = jnp.arange(KEY_SLOTS, dtype=jnp.int32)
    seq = jnp.minimum(sq[:, None] - count[:, None] + 1 + slot[None, :], sq[:, None])
    storage = jnp.sum(
        jnp.where(seq[:, :, None] == span_ids[None, None, :], inverse[None, None, :], 0), axis=2)
    return storage.astype(jnp.int32), seq.astype(jnp.int32), count.astype(jnp.int32)


def shift_x(value, d, n):
    return lax.ppermute(value, "x", [(i, (i + d) % n) for i in range(n)])


def gather_x(chunk):
    n = lax.axis_size("x")
    me = lax.axis_index("x")
    from_right = jnp.stack([chunk] + [shift_x(chunk, n - e, n) for e in range(1, n)])
    order = (jnp.arange(n, dtype=jnp.int32) - me) % n
    return jnp.take(from_right, order, axis=0).reshape(n * chunk.shape[0], *chunk.shape[1:])


def reduce_scatter_x(value):
    n = lax.axis_size("x")
    me = lax.axis_index("x")
    parts = value.reshape(n, value.shape[0] // n, *value.shape[1:])
    total = jnp.take(parts, me, axis=0).astype(jnp.float32)
    for d in range(1, n):
        total = total + shift_x(jnp.take(parts, (me + d) % n, axis=0), d, n).astype(jnp.float32)
    return total.astype(value.dtype)


def per_device(tokens, norm_gain, q_weight, k_weight, v_weight, o_weight, doc_lengths, span_order):
    local_rows = tokens.shape[1]
    tok_dev = local_rows * lax.axis_size(TENSOR)
    model_width = tokens.shape[2]
    head_dim = HEAD_DIM
    q_cols = q_weight.shape[1]
    kv_cols = k_weight.shape[1]
    q_heads = q_cols // head_dim
    kv_local = kv_cols // head_dim
    span_rows = tok_dev // 2
    base_row = lax.axis_index(CONTEXT) * tok_dev
    rows_float = tokens.astype(jnp.float32)
    normed = (
        rows_float
        * lax.rsqrt(jnp.mean(rows_float * rows_float, axis=-1, keepdims=True) + epsilon)
        * norm_gain
    ).astype(jnp.bfloat16)
    plane = lax.axis_index("yh")
    core = lax.axis_index("core")
    weights = jnp.concatenate([q_weight, k_weight, v_weight], axis=1)
    half_in = weights.shape[0] // 2
    sent_half = lax.dynamic_slice_in_dim(weights, core * half_in, half_in, 0)
    plane_rows = gather_x(normed[0])[None]
    partner_half = lax.ppermute(sent_half, ("yh", "ylo"), NEIGHBOUR)
    plane_rows, partner_half = lax.optimization_barrier((plane_rows, partner_half))
    other_half = lax.ppermute(partner_half, "core", [(0, 1), (1, 0)])
    half = plane_rows.shape[1]
    flat_rows = plane_rows.reshape(half, model_width)
    all_places = positions(base_row + jnp.arange(tok_dev, dtype=jnp.int32), span_order, span_rows)
    places = lax.dynamic_slice_in_dim(all_places, plane * half, half, 0)
    rows_mine = lax.dynamic_slice_in_dim(flat_rows, core * half_in, half_in, 1)
    rows_other = lax.dynamic_slice_in_dim(flat_rows, (1 - core) * half_in, half_in, 1)

    def finish(out):
        q = rotary(out[:, :q_cols].reshape(half, q_heads, head_dim), places)
        k = rotary(out[:, q_cols:q_cols + kv_cols].reshape(half, kv_local, head_dim), places)
        return jnp.concatenate(
            [q.reshape(half, q_cols), k.reshape(half, kv_cols), out[:, q_cols + kv_cols:]], axis=1
        ).astype(jnp.bfloat16)

    def project(w):
        return finish(jnp.dot(flat_rows, w, preferred_element_type=jnp.float32))

    for_partner = finish(
        jnp.dot(rows_mine, partner_half, preferred_element_type=jnp.float32)
        + jnp.dot(rows_other, other_half, preferred_element_type=jnp.float32))
    received = lax.ppermute(for_partner, "yh", [(0, 1), (1, 0)])
    flat_rows, for_partner = lax.optimization_barrier((flat_rows, for_partner))
    own = project(weights)
    first = jnp.where(plane == 0, own, received)
    second = jnp.where(plane == 0, received, own)
    projected = jnp.concatenate([first, second], axis=0)
    query_rows = projected[:, :q_cols]
    kv_pair = jnp.stack([projected[:, q_cols:q_cols + kv_cols], projected[:, q_cols + kv_cols:]])
    gathered = lax.all_gather(kv_pair, CONTEXT, axis=1, tiled=True)
    places = all_places
    row_count = tok_dev

    doc_ends = jnp.cumsum(doc_lengths)
    query_start = jnp.max(
        jnp.where(doc_ends[None, :] <= places[:, None], doc_ends[None, :], 0), axis=1)
    query_spans = lax.axis_index(CONTEXT) * 2 + jnp.arange(2, dtype=jnp.int32)
    tbl, seq, cnt = key_tables(span_order, doc_ends, query_spans)
    attended = span_attention(
        tbl, seq, cnt, query_rows,
        places.astype(jnp.int32)[:, None], query_start.astype(jnp.int32)[:, None],
        gathered,
    )
    partner_o = lax.ppermute(o_weight, ("yh", "ylo"), NEIGHBOUR)
    half = row_count // 2
    own_rows = lax.dynamic_slice_in_dim(attended, plane * half, half, 0)
    other_rows = lax.dynamic_slice_in_dim(attended, (1 - plane) * half, half, 0)
    partner_rows = lax.ppermute(other_rows, "yh", [(0, 1), (1, 0)])
    mixed = jnp.dot(
        jnp.concatenate([own_rows, partner_rows], axis=1),
        jnp.concatenate([o_weight, partner_o], axis=0),
        preferred_element_type=jnp.float32,
    ).astype(jnp.bfloat16)
    mixed_rows = reduce_scatter_x(mixed)
    return mixed_rows.reshape(tokens.shape)


TENSOR = ("yh", "x")
NEIGHBOUR = [(0, 3), (3, 0), (1, 2), (2, 1)]
CONTEXT = ("z", "ylo", "core")


def solution(mesh):
    devices = mesh.devices.reshape(2, mesh.devices.shape[0] // 2, -1, 2, 2)
    split_mesh = jax.sharding.Mesh(devices, ("yh", "x", "z", "ylo", "core"))
    in_specs = (
        P(CONTEXT, TENSOR, None),
        P(),
        P(None, TENSOR),
        P(None, TENSOR),
        P(None, TENSOR),
        P(TENSOR, None),
        P(),
        P(),
    )
    out_specs = P(CONTEXT, TENSOR, None)
    return jax.shard_map(
        per_device, mesh=split_mesh, in_specs=in_specs, out_specs=out_specs, check_vma=False
    )
```

```python
import functools
import math

import jax
import jax.numpy as jnp
from jax import lax
from jax.experimental import pallas as pl
from jax.experimental.pallas import tpu as pltpu
from jax.sharding import PartitionSpec as P

HEAD_DIM = 128
SPAN = 512
KEY_SLOTS = 9

rope_theta = 500000.0
epsilon = 1e-05
masked_score = -1e30


def positions(rows, span_order, span_rows):
    slot_ids = jnp.arange(span_order.shape[0], dtype=jnp.int32)
    matches = (rows // span_rows)[:, None] == slot_ids[None, :]
    picked = jnp.sum(jnp.where(matches, span_order[None, :], 0), axis=1)
    return picked * span_rows + rows % span_rows


def rotary(values, places):
    head_dim = values.shape[-1]
    half_dim = head_dim // 2
    frequency = rope_theta ** (-(2.0 / head_dim) * jnp.arange(half_dim, dtype=jnp.float32))
    angles = places.astype(jnp.float32)[:, None] * frequency[None, :]
    cosine = jnp.cos(angles)[:, None, :]
    sine_part = jnp.sin(angles)[:, None, :]
    first_half = values[..., :half_dim]
    second = values[..., half_dim:]
    return jnp.concatenate(
        [first_half * cosine - second * sine_part, second * cosine + first_half * sine_part],
        axis=-1,
    )


def attention_kernel(heads, scale, tbl_ref, seq_ref, cnt_ref, q_ref, qpos_ref, qstart_ref,
                     k_ref, v_ref, o_ref, m_sc, l_sc, acc_sc):
    i = pl.program_id(0)
    j = pl.program_id(1)

    @pl.when(j == 0)
    def _():
        m_sc[...] = jnp.full_like(m_sc, masked_score)
        l_sc[...] = jnp.zeros_like(l_sc)
        acc_sc[...] = jnp.zeros_like(acc_sc)

    @pl.when(j < cnt_ref[i])
    def _():
        k = k_ref[...]
        v = v_ref[...]
        span = k.shape[0]
        kpos = seq_ref[i, j] * span + lax.broadcasted_iota(jnp.int32, (1, span), 1)
        visible = (kpos <= qpos_ref[...]) & (kpos >= qstart_ref[...])
        for h in range(heads):
            q = q_ref[:, h * HEAD_DIM:(h + 1) * HEAD_DIM]
            s = lax.dot_general(q, k, (((1,), (1,)), ((), ())),
                                preferred_element_type=jnp.float32) * scale
            m_old = m_sc[h]
            m_new = jnp.maximum(
                m_old, jnp.max(jnp.where(visible, s, masked_score), axis=-1, keepdims=True))
            p = jnp.where(visible, jnp.exp(s - m_new), 0.0)
            alpha = jnp.exp(m_old - m_new)
            l_sc[h] = alpha * l_sc[h] + jnp.sum(p, axis=-1, keepdims=True)
            acc_sc[h] = alpha * acc_sc[h] + jnp.dot(
                p.astype(jnp.bfloat16), v, preferred_element_type=jnp.float32)
            m_sc[h] = m_new

    @pl.when(j == pl.num_programs(1) - 1)
    def _():
        for h in range(heads):
            o_ref[:, h * HEAD_DIM:(h + 1) * HEAD_DIM] = (acc_sc[h] / l_sc[h]).astype(o_ref.dtype)


def span_attention(tbl, seq, cnt, queries, qpos, qstart, kv):
    rows, q_cols = queries.shape
    heads = q_cols // HEAD_DIM
    n_q = rows // SPAN
    kernel = functools.partial(attention_kernel, heads, 1.0 / math.sqrt(HEAD_DIM))
    steps = n_q * KEY_SLOTS
    cost = pl.CostEstimate(
        flops=4 * steps * heads * SPAN * SPAN * HEAD_DIM,
        transcendentals=steps * heads * SPAN * SPAN,
        bytes_accessed=steps * 2 * SPAN * HEAD_DIM * 2 + 2 * rows * q_cols * 2,
    )
    return pl.pallas_call(
        kernel,
        out_shape=jax.ShapeDtypeStruct((rows, q_cols), jnp.bfloat16),
        grid_spec=pltpu.PrefetchScalarGridSpec(
            num_scalar_prefetch=3,
            grid=(n_q, KEY_SLOTS),
            in_specs=[
                pl.BlockSpec((SPAN, q_cols), lambda i, j, t, s, c: (i, 0)),
                pl.BlockSpec((SPAN, 1), lambda i, j, t, s, c: (i, 0)),
                pl.BlockSpec((SPAN, 1), lambda i, j, t, s, c: (i, 0)),
                pl.BlockSpec((None, SPAN, HEAD_DIM), lambda i, j, t, s, c: (0, t[i, j], 0)),
                pl.BlockSpec((None, SPAN, HEAD_DIM), lambda i, j, t, s, c: (1, t[i, j], 0)),
            ],
            out_specs=pl.BlockSpec((SPAN, q_cols), lambda i, j, t, s, c: (i, 0)),
            scratch_shapes=[
                pltpu.VMEM((heads, SPAN, 1), jnp.float32),
                pltpu.VMEM((heads, SPAN, 1), jnp.float32),
                pltpu.VMEM((heads, SPAN, HEAD_DIM), jnp.float32),
            ],
        ),
        compiler_params=pltpu.CompilerParams(dimension_semantics=("arbitrary", "arbitrary")),
        cost_estimate=cost,
    )(tbl, seq, cnt, queries, qpos, qstart, kv, kv)


def key_tables(span_order, doc_ends, query_spans):
    n_spans = span_order.shape[0]
    span_ids = jnp.arange(n_spans, dtype=jnp.int32)
    inverse = jnp.sum(
        jnp.where(span_order[None, :] == span_ids[:, None], span_ids[None, :], 0), axis=1)
    first_doc = jnp.sum((doc_ends[None, :] <= (span_ids * SPAN)[:, None]).astype(jnp.int32), axis=1)
    last_doc = jnp.sum(
        (doc_ends[None, :] <= (span_ids * SPAN + SPAN - 1)[:, None]).astype(jnp.int32), axis=1)
    sq = jnp.sum(jnp.where(query_spans[:, None] == span_ids[None, :], span_order[None, :], 0), axis=1)
    q_first = jnp.sum(jnp.where(sq[:, None] == span_ids[None, :], first_doc[None, :], 0), axis=1)
    back = jnp.arange(KEY_SLOTS, dtype=jnp.int32) - (KEY_SLOTS - 1)
    cand = sq[:, None] + back[None, :]
    cand_last = jnp.sum(
        jnp.where(cand[:, :, None] == span_ids[None, None, :], last_doc[None, None, :], 0), axis=2)
    valid = (cand >= 0) & (cand_last >= q_first[:, None])
    count = jnp.sum(valid.astype(jnp.int32), axis=1)
    slot = jnp.arange(KEY_SLOTS, dtype=jnp.int32)
    seq = jnp.minimum(sq[:, None] - count[:, None] + 1 + slot[None, :], sq[:, None])
    storage = jnp.sum(
        jnp.where(seq[:, :, None] == span_ids[None, None, :], inverse[None, None, :], 0), axis=2)
    return storage.astype(jnp.int32), seq.astype(jnp.int32), count.astype(jnp.int32)


def shift_x(value, d, n):
    return lax.ppermute(value, "x", [(i, (i + d) % n) for i in range(n)])


def gather_x(chunk):
    n = lax.axis_size("x")
    me = lax.axis_index("x")
    from_right = jnp.stack([chunk] + [shift_x(chunk, n - e, n) for e in range(1, n)])
    order = (jnp.arange(n, dtype=jnp.int32) - me) % n
    return jnp.take(from_right, order, axis=0).reshape(n * chunk.shape[0], *chunk.shape[1:])


def reduce_scatter_x(value):
    n = lax.axis_size("x")
    me = lax.axis_index("x")
    parts = value.reshape(n, value.shape[0] // n, *value.shape[1:])
    total = jnp.take(parts, me, axis=0).astype(jnp.float32)
    for d in range(1, n):
        total = total + shift_x(jnp.take(parts, (me + d) % n, axis=0), d, n).astype(jnp.float32)
    return total.astype(value.dtype)


def per_device(tokens, norm_gain, q_weight, k_weight, v_weight, o_weight, doc_lengths, span_order):
    local_rows = tokens.shape[1]
    tok_dev = local_rows * lax.axis_size(TENSOR)
    model_width = tokens.shape[2]
    head_dim = HEAD_DIM
    q_cols = q_weight.shape[1]
    kv_cols = k_weight.shape[1]
    q_heads = q_cols // head_dim
    kv_local = kv_cols // head_dim
    span_rows = tok_dev // 2
    base_row = lax.axis_index(CONTEXT) * tok_dev
    rows_float = tokens.astype(jnp.float32)
    normed = (
        rows_float
        * lax.rsqrt(jnp.mean(rows_float * rows_float, axis=-1, keepdims=True) + epsilon)
        * norm_gain
    ).astype(jnp.bfloat16)
    plane = lax.axis_index("yh")
    core = lax.axis_index("core")
    weights = jnp.concatenate([q_weight, k_weight, v_weight], axis=1)
    part_cols = weights.shape[1] // 2
    sent_part = jnp.where(core == 0, weights[:, :part_cols], weights[:, part_cols:])
    n_x = lax.axis_size("x")
    me_x = lax.axis_index("x")
    chunk = normed[0]
    chunks = [chunk] + [shift_x(chunk, n_x - e, n_x) for e in range(1, n_x)]
    partner_part = lax.ppermute(sent_part, ("yh", "ylo"), NEIGHBOUR)
    got = lax.optimization_barrier((chunks, partner_part))
    chunks, partner_part = got
    other_part = lax.ppermute(partner_part, "core", [(0, 1), (1, 0)])
    half = n_x * chunk.shape[0]
    all_places = positions(base_row + jnp.arange(tok_dev, dtype=jnp.int32), span_order, span_rows)
    places = lax.dynamic_slice_in_dim(all_places, plane * half, half, 0)
    order = (jnp.arange(n_x, dtype=jnp.int32) - me_x) % n_x

    def in_order(parts):
        stacked = jnp.stack(parts)
        return jnp.take(stacked, order, axis=0).reshape(half, stacked.shape[-1])

    def finish(out):
        q = rotary(out[:, :q_cols].reshape(half, q_heads, head_dim), places)
        k = rotary(out[:, q_cols:q_cols + kv_cols].reshape(half, kv_local, head_dim), places)
        return jnp.concatenate(
            [q.reshape(half, q_cols), k.reshape(half, kv_cols), out[:, q_cols + kv_cols:]], axis=1
        ).astype(jnp.bfloat16)

    def project(rows_list, w):
        return in_order([jnp.dot(r, w, preferred_element_type=jnp.float32) for r in rows_list])

    got_part = project(chunks, partner_part)
    swapped_part = project(chunks, other_part)
    for_partner = finish(jnp.concatenate([
        jnp.where(core == 0, got_part, swapped_part),
        jnp.where(core == 0, swapped_part, got_part)], axis=1))
    received = lax.ppermute(for_partner, "yh", [(0, 1), (1, 0)])
    chunks, for_partner = lax.optimization_barrier((chunks, for_partner))
    own = finish(project(chunks, weights))
    first = jnp.where(plane == 0, own, received)
    second = jnp.where(plane == 0, received, own)
    projected = jnp.concatenate([first, second], axis=0)
    query_rows = projected[:, :q_cols]
    kv_pair = jnp.stack([projected[:, q_cols:q_cols + kv_cols], projected[:, q_cols + kv_cols:]])
    gathered = lax.all_gather(kv_pair, CONTEXT, axis=1, tiled=True)
    places = all_places
    row_count = tok_dev

    doc_ends = jnp.cumsum(doc_lengths)
    query_start = jnp.max(
        jnp.where(doc_ends[None, :] <= places[:, None], doc_ends[None, :], 0), axis=1)
    query_spans = lax.axis_index(CONTEXT) * 2 + jnp.arange(2, dtype=jnp.int32)
    tbl, seq, cnt = key_tables(span_order, doc_ends, query_spans)
    attended = span_attention(
        tbl, seq, cnt, query_rows,
        places.astype(jnp.int32)[:, None], query_start.astype(jnp.int32)[:, None],
        gathered,
    )
    partner_o = lax.ppermute(o_weight, ("yh", "ylo"), NEIGHBOUR)
    half = row_count // 2
    own_rows = lax.dynamic_slice_in_dim(attended, plane * half, half, 0)
    other_rows = lax.dynamic_slice_in_dim(attended, (1 - plane) * half, half, 0)
    partner_rows = lax.ppermute(other_rows, "yh", [(0, 1), (1, 0)])
    mixed = jnp.dot(
        jnp.concatenate([own_rows, partner_rows], axis=1),
        jnp.concatenate([o_weight, partner_o], axis=0),
        preferred_element_type=jnp.float32,
    ).astype(jnp.bfloat16)
    mixed_rows = reduce_scatter_x(mixed)
    return mixed_rows.reshape(tokens.shape)


TENSOR = ("yh", "x")
NEIGHBOUR = [(0, 3), (3, 0), (1, 2), (2, 1)]
CONTEXT = ("z", "ylo", "core")


def solution(mesh):
    devices = mesh.devices.reshape(2, mesh.devices.shape[0] // 2, -1, 2, 2)
    split_mesh = jax.sharding.Mesh(devices, ("yh", "x", "z", "ylo", "core"))
    in_specs = (
        P(CONTEXT, TENSOR, None),
        P(),
        P(None, TENSOR),
        P(None, TENSOR),
        P(None, TENSOR),
        P(TENSOR, None),
        P(),
        P(),
    )
    out_specs = P(CONTEXT, TENSOR, None)
    return jax.shard_map(
        per_device, mesh=split_mesh, in_specs=in_specs, out_specs=out_specs, check_vma=False
    )
```

```python
import functools
import math

import jax
import jax.numpy as jnp
from jax import lax
from jax.experimental import pallas as pl
from jax.experimental.pallas import tpu as pltpu
from jax.sharding import PartitionSpec as P

HEAD_DIM = 128
SPAN = 512
KEY_SLOTS = 9

rope_theta = 500000.0
epsilon = 1e-05
masked_score = -1e30


def positions(rows, span_order, span_rows):
    slot_ids = jnp.arange(span_order.shape[0], dtype=jnp.int32)
    matches = (rows // span_rows)[:, None] == slot_ids[None, :]
    picked = jnp.sum(jnp.where(matches, span_order[None, :], 0), axis=1)
    return picked * span_rows + rows % span_rows


def rotary(values, places):
    head_dim = values.shape[-1]
    half_dim = head_dim // 2
    frequency = rope_theta ** (-(2.0 / head_dim) * jnp.arange(half_dim, dtype=jnp.float32))
    angles = places.astype(jnp.float32)[:, None] * frequency[None, :]
    cosine = jnp.cos(angles)[:, None, :]
    sine_part = jnp.sin(angles)[:, None, :]
    first_half = values[..., :half_dim]
    second = values[..., half_dim:]
    return jnp.concatenate(
        [first_half * cosine - second * sine_part, second * cosine + first_half * sine_part],
        axis=-1,
    )


def attention_kernel(heads, scale, tbl_ref, seq_ref, cnt_ref, q_ref, qpos_ref, qstart_ref,
                     k_ref, v_ref, o_ref, m_sc, l_sc, acc_sc):
    i = pl.program_id(0)
    j = pl.program_id(1)

    @pl.when(j == 0)
    def _():
        m_sc[...] = jnp.full_like(m_sc, masked_score)
        l_sc[...] = jnp.zeros_like(l_sc)
        acc_sc[...] = jnp.zeros_like(acc_sc)

    @pl.when(j < cnt_ref[i])
    def _():
        k = k_ref[...]
        v = v_ref[...]
        span = k.shape[0]
        kpos = seq_ref[i, j] * span + lax.broadcasted_iota(jnp.int32, (1, span), 1)
        visible = (kpos <= qpos_ref[...]) & (kpos >= qstart_ref[...])
        for h in range(heads):
            q = q_ref[:, h * HEAD_DIM:(h + 1) * HEAD_DIM]
            s = lax.dot_general(q, k, (((1,), (1,)), ((), ())),
                                preferred_element_type=jnp.float32) * scale
            m_old = m_sc[h]
            m_new = jnp.maximum(
                m_old, jnp.max(jnp.where(visible, s, masked_score), axis=-1, keepdims=True))
            p = jnp.where(visible, jnp.exp(s - m_new), 0.0)
            alpha = jnp.exp(m_old - m_new)
            l_sc[h] = alpha * l_sc[h] + jnp.sum(p, axis=-1, keepdims=True)
            acc_sc[h] = alpha * acc_sc[h] + jnp.dot(
                p.astype(jnp.bfloat16), v, preferred_element_type=jnp.float32)
            m_sc[h] = m_new

    @pl.when(j == pl.num_programs(1) - 1)
    def _():
        for h in range(heads):
            o_ref[:, h * HEAD_DIM:(h + 1) * HEAD_DIM] = (acc_sc[h] / l_sc[h]).astype(o_ref.dtype)


def span_attention(tbl, seq, cnt, queries, qpos, qstart, kv):
    rows, q_cols = queries.shape
    heads = q_cols // HEAD_DIM
    n_q = rows // SPAN
    kernel = functools.partial(attention_kernel, heads, 1.0 / math.sqrt(HEAD_DIM))
    steps = n_q * KEY_SLOTS
    cost = pl.CostEstimate(
        flops=4 * steps * heads * SPAN * SPAN * HEAD_DIM,
        transcendentals=steps * heads * SPAN * SPAN,
        bytes_accessed=steps * 2 * SPAN * HEAD_DIM * 2 + 2 * rows * q_cols * 2,
    )
    return pl.pallas_call(
        kernel,
        out_shape=jax.ShapeDtypeStruct((rows, q_cols), jnp.bfloat16),
        grid_spec=pltpu.PrefetchScalarGridSpec(
            num_scalar_prefetch=3,
            grid=(n_q, KEY_SLOTS),
            in_specs=[
                pl.BlockSpec((SPAN, q_cols), lambda i, j, t, s, c: (i, 0)),
                pl.BlockSpec((SPAN, 1), lambda i, j, t, s, c: (i, 0)),
                pl.BlockSpec((SPAN, 1), lambda i, j, t, s, c: (i, 0)),
                pl.BlockSpec((None, SPAN, HEAD_DIM), lambda i, j, t, s, c: (0, t[i, j], 0)),
                pl.BlockSpec((None, SPAN, HEAD_DIM), lambda i, j, t, s, c: (1, t[i, j], 0)),
            ],
            out_specs=pl.BlockSpec((SPAN, q_cols), lambda i, j, t, s, c: (i, 0)),
            scratch_shapes=[
                pltpu.VMEM((heads, SPAN, 1), jnp.float32),
                pltpu.VMEM((heads, SPAN, 1), jnp.float32),
                pltpu.VMEM((heads, SPAN, HEAD_DIM), jnp.float32),
            ],
        ),
        compiler_params=pltpu.CompilerParams(dimension_semantics=("arbitrary", "arbitrary")),
        cost_estimate=cost,
    )(tbl, seq, cnt, queries, qpos, qstart, kv, kv)


def key_tables(span_order, doc_ends, query_spans):
    n_spans = span_order.shape[0]
    span_ids = jnp.arange(n_spans, dtype=jnp.int32)
    inverse = jnp.sum(
        jnp.where(span_order[None, :] == span_ids[:, None], span_ids[None, :], 0), axis=1)
    first_doc = jnp.sum((doc_ends[None, :] <= (span_ids * SPAN)[:, None]).astype(jnp.int32), axis=1)
    last_doc = jnp.sum(
        (doc_ends[None, :] <= (span_ids * SPAN + SPAN - 1)[:, None]).astype(jnp.int32), axis=1)
    sq = jnp.sum(jnp.where(query_spans[:, None] == span_ids[None, :], span_order[None, :], 0), axis=1)
    q_first = jnp.sum(jnp.where(sq[:, None] == span_ids[None, :], first_doc[None, :], 0), axis=1)
    back = jnp.arange(KEY_SLOTS, dtype=jnp.int32) - (KEY_SLOTS - 1)
    cand = sq[:, None] + back[None, :]
    cand_last = jnp.sum(
        jnp.where(cand[:, :, None] == span_ids[None, None, :], last_doc[None, None, :], 0), axis=2)
    valid = (cand >= 0) & (cand_last >= q_first[:, None])
    count = jnp.sum(valid.astype(jnp.int32), axis=1)
    slot = jnp.arange(KEY_SLOTS, dtype=jnp.int32)
    seq = jnp.minimum(sq[:, None] - count[:, None] + 1 + slot[None, :], sq[:, None])
    tbl = jnp.sum(jnp.where(seq[:, :, None] == span_ids[None, None, :], inverse[None, None, :], 0),
                  axis=2)
    return tbl.astype(jnp.int32), seq.astype(jnp.int32), count.astype(jnp.int32)


def shift_x(value, d, n):
    return lax.ppermute(value, "x", [(i, (i + d) % n) for i in range(n)])


def reduce_scatter_x(value):
    n = lax.axis_size("x")
    me = lax.axis_index("x")
    parts = value.reshape(n, value.shape[0] // n, *value.shape[1:])
    total = jnp.take(parts, me, axis=0).astype(jnp.float32)
    for d in range(1, n):
        total = total + shift_x(jnp.take(parts, (me + d) % n, axis=0), d, n).astype(jnp.float32)
    return total.astype(value.dtype)


def per_device(tokens, norm_gain, q_weight, k_weight, v_weight, o_weight, doc_lengths, span_order):
    local_rows = tokens.shape[1]
    tok_dev = local_rows * lax.axis_size(TENSOR)
    model_width = tokens.shape[2]
    head_dim = HEAD_DIM
    q_cols = q_weight.shape[1]
    kv_cols = k_weight.shape[1]
    q_heads = q_cols // head_dim
    kv_local = kv_cols // head_dim
    span_rows = tok_dev // 2
    base_row = lax.axis_index(CONTEXT) * tok_dev
    rows_float = tokens.astype(jnp.float32)
    normed = (
        rows_float
        * lax.rsqrt(jnp.mean(rows_float * rows_float, axis=-1, keepdims=True) + epsilon)
        * norm_gain
    ).astype(jnp.bfloat16)
    plane = lax.axis_index("yh")
    core = lax.axis_index("core")
    weights = jnp.concatenate([q_weight, k_weight, v_weight], axis=1)
    half_in = weights.shape[0] // 2
    sent_half = lax.dynamic_slice_in_dim(weights, core * half_in, half_in, 0)
    plane_rows = lax.all_gather(normed, "x", axis=1, tiled=True)
    partner_half = lax.ppermute(sent_half, ("yh", "ylo"), NEIGHBOUR)
    plane_rows, partner_half = lax.optimization_barrier((plane_rows, partner_half))
    other_half = lax.ppermute(partner_half, "core", [(0, 1), (1, 0)])
    half = plane_rows.shape[1]
    flat_rows = plane_rows.reshape(half, model_width)
    all_places = positions(base_row + jnp.arange(tok_dev, dtype=jnp.int32), span_order, span_rows)
    places = lax.dynamic_slice_in_dim(all_places, plane * half, half, 0)
    rows_mine = lax.dynamic_slice_in_dim(flat_rows, core * half_in, half_in, 1)
    rows_other = lax.dynamic_slice_in_dim(flat_rows, (1 - core) * half_in, half_in, 1)

    def finish(out):
        q = rotary(out[:, :q_cols].reshape(half, q_heads, head_dim), places)
        k = rotary(out[:, q_cols:q_cols + kv_cols].reshape(half, kv_local, head_dim), places)
        return jnp.concatenate(
            [q.reshape(half, q_cols), k.reshape(half, kv_cols), out[:, q_cols + kv_cols:]], axis=1
        ).astype(jnp.bfloat16)

    def project(w):
        return finish(jnp.dot(flat_rows, w, preferred_element_type=jnp.float32))

    for_partner = finish(
        jnp.dot(rows_mine, partner_half, preferred_element_type=jnp.float32)
        + jnp.dot(rows_other, other_half, preferred_element_type=jnp.float32))
    received = lax.ppermute(for_partner, "yh", [(0, 1), (1, 0)])
    flat_rows, for_partner = lax.optimization_barrier((flat_rows, for_partner))
    own = project(weights)
    first = jnp.where(plane == 0, own, received)
    second = jnp.where(plane == 0, received, own)
    projected = jnp.concatenate([first, second], axis=0)
    query_rows = projected[:, :q_cols]
    kv_pair = jnp.stack([projected[:, q_cols:q_cols + kv_cols], projected[:, q_cols + kv_cols:]])
    gathered = lax.all_gather(kv_pair, CONTEXT, axis=1, tiled=True)
    places = all_places
    row_count = tok_dev

    doc_ends = jnp.cumsum(doc_lengths)
    query_start = jnp.max(
        jnp.where(doc_ends[None, :] <= places[:, None], doc_ends[None, :], 0), axis=1)
    query_spans = lax.axis_index(CONTEXT) * 2 + jnp.arange(2, dtype=jnp.int32)
    tbl, seq, cnt = key_tables(span_order, doc_ends, query_spans)
    attended = span_attention(
        tbl, seq, cnt, query_rows,
        places.astype(jnp.int32)[:, None], query_start.astype(jnp.int32)[:, None],
        gathered,
    )
    partner_o = lax.ppermute(o_weight, ("yh", "ylo"), NEIGHBOUR)
    half = row_count // 2
    own_rows = lax.dynamic_slice_in_dim(attended, plane * half, half, 0)
    other_rows = lax.dynamic_slice_in_dim(attended, (1 - plane) * half, half, 0)
    partner_rows = lax.ppermute(other_rows, "yh", [(0, 1), (1, 0)])
    mixed = jnp.dot(
        jnp.concatenate([own_rows, partner_rows], axis=1),
        jnp.concatenate([o_weight, partner_o], axis=0),
        preferred_element_type=jnp.float32,
    ).astype(jnp.bfloat16)
    mixed_rows = reduce_scatter_x(mixed)
    return mixed_rows.reshape(tokens.shape)


TENSOR = ("yh", "x")
NEIGHBOUR = [(0, 3), (3, 0), (1, 2), (2, 1)]
CONTEXT = ("z", "ylo", "core")


def solution(mesh):
    devices = mesh.devices.reshape(2, mesh.devices.shape[0] // 2, -1, 2, 2)
    split_mesh = jax.sharding.Mesh(devices, ("yh", "x", "z", "ylo", "core"))
    in_specs = (
        P(CONTEXT, TENSOR, None),
        P(),
        P(None, TENSOR),
        P(None, TENSOR),
        P(None, TENSOR),
        P(TENSOR, None),
        P(),
        P(),
    )
    out_specs = P(CONTEXT, TENSOR, None)
    return jax.shard_map(
        per_device, mesh=split_mesh, in_specs=in_specs, out_specs=out_specs, check_vma=False
    )
```

```python
import functools
import math

import jax
import jax.numpy as jnp
from jax import lax
from jax.experimental import pallas as pl
from jax.experimental.pallas import tpu as pltpu
from jax.sharding import PartitionSpec as P

HEAD_DIM = 128
SPAN = 512
KEY_SLOTS = 9

rope_theta = 500000.0
epsilon = 1e-05
masked_score = -1e30


def positions(rows, span_order, span_rows):
    slot_ids = jnp.arange(span_order.shape[0], dtype=jnp.int32)
    matches = (rows // span_rows)[:, None] == slot_ids[None, :]
    picked = jnp.sum(jnp.where(matches, span_order[None, :], 0), axis=1)
    return picked * span_rows + rows % span_rows


def rotary(values, places):
    head_dim = values.shape[-1]
    half_dim = head_dim // 2
    frequency = rope_theta ** (-(2.0 / head_dim) * jnp.arange(half_dim, dtype=jnp.float32))
    angles = places.astype(jnp.float32)[:, None] * frequency[None, :]
    cosine = jnp.cos(angles)[:, None, :]
    sine_part = jnp.sin(angles)[:, None, :]
    first_half = values[..., :half_dim]
    second = values[..., half_dim:]
    return jnp.concatenate(
        [first_half * cosine - second * sine_part, second * cosine + first_half * sine_part],
        axis=-1,
    )


def attention_kernel(heads, scale, tbl_ref, seq_ref, cnt_ref, full_ref, q_ref, qpos_ref, qstart_ref,
                     k_ref, v_ref, o_ref, m_sc, l_sc, acc_sc):
    i = pl.program_id(0)
    j = pl.program_id(1)

    @pl.when(j == 0)
    def _():
        m_sc[...] = jnp.full_like(m_sc, masked_score)
        l_sc[...] = jnp.zeros_like(l_sc)
        acc_sc[...] = jnp.zeros_like(acc_sc)

    def update(visible):
        k = k_ref[...]
        v = v_ref[...]
        for h in range(heads):
            q = q_ref[:, h * HEAD_DIM:(h + 1) * HEAD_DIM]
            s = lax.dot_general(q, k, (((1,), (1,)), ((), ())),
                                preferred_element_type=jnp.float32) * scale
            if visible is not None:
                s = jnp.where(visible, s, masked_score)
            m_old = m_sc[h]
            m_new = jnp.maximum(m_old, jnp.max(s, axis=-1, keepdims=True))
            p = jnp.exp(s - m_new)
            alpha = jnp.exp(m_old - m_new)
            l_sc[h] = alpha * l_sc[h] + jnp.sum(p, axis=-1, keepdims=True)
            acc_sc[h] = alpha * acc_sc[h] + jnp.dot(
                p.astype(jnp.bfloat16), v, preferred_element_type=jnp.float32)
            m_sc[h] = m_new

    live = j < cnt_ref[i]
    full = full_ref[i, j] == 1

    @pl.when(live & full)
    def _():
        update(None)

    @pl.when(live & jnp.logical_not(full))
    def _():
        span = k_ref.shape[0]
        kpos = seq_ref[i, j] * span + lax.broadcasted_iota(jnp.int32, (1, span), 1)
        update((kpos <= qpos_ref[...]) & (kpos >= qstart_ref[...]))

    @pl.when(j == pl.num_programs(1) - 1)
    def _():
        for h in range(heads):
            o_ref[:, h * HEAD_DIM:(h + 1) * HEAD_DIM] = (acc_sc[h] / l_sc[h]).astype(o_ref.dtype)


def span_attention(tbl, seq, cnt, full, queries, qpos, qstart, kv):
    rows, q_cols = queries.shape
    heads = q_cols // HEAD_DIM
    n_q = rows // SPAN
    kernel = functools.partial(attention_kernel, heads, 1.0 / math.sqrt(HEAD_DIM))
    steps = n_q * KEY_SLOTS
    cost = pl.CostEstimate(
        flops=4 * steps * heads * SPAN * SPAN * HEAD_DIM,
        transcendentals=steps * heads * SPAN * SPAN,
        bytes_accessed=steps * 2 * SPAN * HEAD_DIM * 2 + 2 * rows * q_cols * 2,
    )
    return pl.pallas_call(
        kernel,
        out_shape=jax.ShapeDtypeStruct((rows, q_cols), jnp.bfloat16),
        grid_spec=pltpu.PrefetchScalarGridSpec(
            num_scalar_prefetch=4,
            grid=(n_q, KEY_SLOTS),
            in_specs=[
                pl.BlockSpec((SPAN, q_cols), lambda i, j, t, s, c, f: (i, 0)),
                pl.BlockSpec((SPAN, 1), lambda i, j, t, s, c, f: (i, 0)),
                pl.BlockSpec((SPAN, 1), lambda i, j, t, s, c, f: (i, 0)),
                pl.BlockSpec((None, SPAN, HEAD_DIM), lambda i, j, t, s, c, f: (0, t[i, j], 0)),
                pl.BlockSpec((None, SPAN, HEAD_DIM), lambda i, j, t, s, c, f: (1, t[i, j], 0)),
            ],
            out_specs=pl.BlockSpec((SPAN, q_cols), lambda i, j, t, s, c, f: (i, 0)),
            scratch_shapes=[
                pltpu.VMEM((heads, SPAN, 1), jnp.float32),
                pltpu.VMEM((heads, SPAN, 1), jnp.float32),
                pltpu.VMEM((heads, SPAN, HEAD_DIM), jnp.float32),
            ],
        ),
        compiler_params=pltpu.CompilerParams(dimension_semantics=("arbitrary", "arbitrary")),
        cost_estimate=cost,
    )(tbl, seq, cnt, full, queries, qpos, qstart, kv, kv)


def key_tables(span_order, doc_ends, query_spans):
    n_spans = span_order.shape[0]
    span_ids = jnp.arange(n_spans, dtype=jnp.int32)
    inverse = jnp.sum(
        jnp.where(span_order[None, :] == span_ids[:, None], span_ids[None, :], 0), axis=1)
    first_doc = jnp.sum((doc_ends[None, :] <= (span_ids * SPAN)[:, None]).astype(jnp.int32), axis=1)
    last_doc = jnp.sum(
        (doc_ends[None, :] <= (span_ids * SPAN + SPAN - 1)[:, None]).astype(jnp.int32), axis=1)
    sq = jnp.sum(jnp.where(query_spans[:, None] == span_ids[None, :], span_order[None, :], 0), axis=1)
    q_first = jnp.sum(jnp.where(sq[:, None] == span_ids[None, :], first_doc[None, :], 0), axis=1)
    back = jnp.arange(KEY_SLOTS, dtype=jnp.int32) - (KEY_SLOTS - 1)
    cand = sq[:, None] + back[None, :]
    cand_last = jnp.sum(
        jnp.where(cand[:, :, None] == span_ids[None, None, :], last_doc[None, None, :], 0), axis=2)
    valid = (cand >= 0) & (cand_last >= q_first[:, None])
    count = jnp.sum(valid.astype(jnp.int32), axis=1)
    slot = jnp.arange(KEY_SLOTS, dtype=jnp.int32)
    seq = jnp.minimum(sq[:, None] - count[:, None] + 1 + slot[None, :], sq[:, None])
    tbl = jnp.sum(jnp.where(seq[:, :, None] == span_ids[None, None, :], inverse[None, None, :], 0),
                  axis=2)
    last_start = jnp.max(
        jnp.where(doc_ends[None, :] <= (sq * SPAN + SPAN - 1)[:, None], doc_ends[None, :], 0), axis=1)
    full = (seq < sq[:, None]) & (seq * SPAN >= last_start[:, None])
    return (tbl.astype(jnp.int32), seq.astype(jnp.int32), count.astype(jnp.int32),
            full.astype(jnp.int32))


def shift_x(value, d, n):
    return lax.ppermute(value, "x", [(i, (i + d) % n) for i in range(n)])


def reduce_scatter_x(value):
    n = lax.axis_size("x")
    me = lax.axis_index("x")
    parts = value.reshape(n, value.shape[0] // n, *value.shape[1:])
    total = jnp.take(parts, me, axis=0).astype(jnp.float32)
    for d in range(1, n):
        total = total + shift_x(jnp.take(parts, (me + d) % n, axis=0), d, n).astype(jnp.float32)
    return total.astype(value.dtype)


def per_device(tokens, norm_gain, q_weight, k_weight, v_weight, o_weight, doc_lengths, span_order):
    local_rows = tokens.shape[1]
    tok_dev = local_rows * lax.axis_size(TENSOR)
    model_width = tokens.shape[2]
    head_dim = HEAD_DIM
    q_cols = q_weight.shape[1]
    kv_cols = k_weight.shape[1]
    q_heads = q_cols // head_dim
    kv_local = kv_cols // head_dim
    span_rows = tok_dev // 2
    base_row = lax.axis_index(CONTEXT) * tok_dev
    rows_float = tokens.astype(jnp.float32)
    normed = (
        rows_float
        * lax.rsqrt(jnp.mean(rows_float * rows_float, axis=-1, keepdims=True) + epsilon)
        * norm_gain
    ).astype(jnp.bfloat16)
    plane = lax.axis_index("yh")
    core = lax.axis_index("core")
    weights = jnp.concatenate([q_weight, k_weight, v_weight], axis=1)
    half_in = weights.shape[0] // 2
    sent_half = lax.dynamic_slice_in_dim(weights, core * half_in, half_in, 0)
    plane_rows = lax.all_gather(normed, "x", axis=1, tiled=True)
    partner_half = lax.ppermute(sent_half, ("yh", "ylo"), NEIGHBOUR)
    plane_rows, partner_half = lax.optimization_barrier((plane_rows, partner_half))
    other_half = lax.ppermute(partner_half, "core", [(0, 1), (1, 0)])
    half = plane_rows.shape[1]
    flat_rows = plane_rows.reshape(half, model_width)
    all_places = positions(base_row + jnp.arange(tok_dev, dtype=jnp.int32), span_order, span_rows)
    places = lax.dynamic_slice_in_dim(all_places, plane * half, half, 0)
    rows_mine = lax.dynamic_slice_in_dim(flat_rows, core * half_in, half_in, 1)
    rows_other = lax.dynamic_slice_in_dim(flat_rows, (1 - core) * half_in, half_in, 1)

    def finish(out):
        q = rotary(out[:, :q_cols].reshape(half, q_heads, head_dim), places)
        k = rotary(out[:, q_cols:q_cols + kv_cols].reshape(half, kv_local, head_dim), places)
        return jnp.concatenate(
            [q.reshape(half, q_cols), k.reshape(half, kv_cols), out[:, q_cols + kv_cols:]], axis=1
        ).astype(jnp.bfloat16)

    def project(w):
        return finish(jnp.dot(flat_rows, w, preferred_element_type=jnp.float32))

    for_partner = finish(
        jnp.dot(rows_mine, partner_half, preferred_element_type=jnp.float32)
        + jnp.dot(rows_other, other_half, preferred_element_type=jnp.float32))
    received = lax.ppermute(for_partner, "yh", [(0, 1), (1, 0)])
    flat_rows, for_partner = lax.optimization_barrier((flat_rows, for_partner))
    own = project(weights)
    first = jnp.where(plane == 0, own, received)
    second = jnp.where(plane == 0, received, own)
    projected = jnp.concatenate([first, second], axis=0)
    query_rows = projected[:, :q_cols]
    kv_pair = jnp.stack([projected[:, q_cols:q_cols + kv_cols], projected[:, q_cols + kv_cols:]])
    gathered = lax.all_gather(kv_pair, CONTEXT, axis=1, tiled=True)
    places = all_places
    row_count = tok_dev

    doc_ends = jnp.cumsum(doc_lengths)
    query_start = jnp.max(
        jnp.where(doc_ends[None, :] <= places[:, None], doc_ends[None, :], 0), axis=1)
    query_spans = lax.axis_index(CONTEXT) * 2 + jnp.arange(2, dtype=jnp.int32)
    tbl, seq, cnt, full = key_tables(span_order, doc_ends, query_spans)
    attended = span_attention(
        tbl, seq, cnt, full, query_rows,
        places.astype(jnp.int32)[:, None], query_start.astype(jnp.int32)[:, None],
        gathered,
    )
    partner_o = lax.ppermute(o_weight, ("yh", "ylo"), NEIGHBOUR)
    half = row_count // 2
    own_rows = lax.dynamic_slice_in_dim(attended, plane * half, half, 0)
    other_rows = lax.dynamic_slice_in_dim(attended, (1 - plane) * half, half, 0)
    partner_rows = lax.ppermute(other_rows, "yh", [(0, 1), (1, 0)])
    mixed = jnp.dot(
        jnp.concatenate([own_rows, partner_rows], axis=1),
        jnp.concatenate([o_weight, partner_o], axis=0),
        preferred_element_type=jnp.float32,
    ).astype(jnp.bfloat16)
    mixed_rows = reduce_scatter_x(mixed)
    return mixed_rows.reshape(tokens.shape)


TENSOR = ("yh", "x")
NEIGHBOUR = [(0, 3), (3, 0), (1, 2), (2, 1)]
CONTEXT = ("z", "ylo", "core")


def solution(mesh):
    devices = mesh.devices.reshape(2, mesh.devices.shape[0] // 2, -1, 2, 2)
    split_mesh = jax.sharding.Mesh(devices, ("yh", "x", "z", "ylo", "core"))
    in_specs = (
        P(CONTEXT, TENSOR, None),
        P(),
        P(None, TENSOR),
        P(None, TENSOR),
        P(None, TENSOR),
        P(TENSOR, None),
        P(),
        P(),
    )
    out_specs = P(CONTEXT, TENSOR, None)
    return jax.shard_map(
        per_device, mesh=split_mesh, in_specs=in_specs, out_specs=out_specs, check_vma=False
    )
```

```python
import functools
import math

import jax
import jax.numpy as jnp
from jax import lax
from jax.experimental import pallas as pl
from jax.experimental.pallas import tpu as pltpu
from jax.sharding import PartitionSpec as P

HEAD_DIM = 128
SPAN = 512
KEY_SLOTS = 9

rope_theta = 500000.0
epsilon = 1e-05
masked_score = -1e30


def positions(rows, span_order, span_rows):
    slot_ids = jnp.arange(span_order.shape[0], dtype=jnp.int32)
    matches = (rows // span_rows)[:, None] == slot_ids[None, :]
    picked = jnp.sum(jnp.where(matches, span_order[None, :], 0), axis=1)
    return picked * span_rows + rows % span_rows


def rotary(values, places):
    head_dim = values.shape[-1]
    half_dim = head_dim // 2
    frequency = rope_theta ** (-(2.0 / head_dim) * jnp.arange(half_dim, dtype=jnp.float32))
    angles = places.astype(jnp.float32)[:, None] * frequency[None, :]
    cosine = jnp.cos(angles)[:, None, :]
    sine_part = jnp.sin(angles)[:, None, :]
    first_half = values[..., :half_dim]
    second = values[..., half_dim:]
    return jnp.concatenate(
        [first_half * cosine - second * sine_part, second * cosine + first_half * sine_part],
        axis=-1,
    )


def attention_kernel(heads, scale, which_ref, tbl_ref, seq_ref, cnt_ref, full_ref, q_ref, qpos_ref, qstart_ref,
                     k_ref, v_ref, o_ref, m_sc, l_sc, acc_sc):
    i = pl.program_id(0)
    j = pl.program_id(1)

    @pl.when(j == 0)
    def _():
        m_sc[...] = jnp.full_like(m_sc, masked_score)
        l_sc[...] = jnp.zeros_like(l_sc)
        acc_sc[...] = jnp.zeros_like(acc_sc)

    def update(visible):
        k = k_ref[...]
        v = v_ref[...]
        for h in range(heads):
            q = q_ref[:, h * HEAD_DIM:(h + 1) * HEAD_DIM]
            s = lax.dot_general(q, k, (((1,), (1,)), ((), ())),
                                preferred_element_type=jnp.float32) * scale
            if visible is not None:
                s = jnp.where(visible, s, masked_score)
            m_old = m_sc[h]
            m_new = jnp.maximum(m_old, jnp.max(s, axis=-1, keepdims=True))
            p = jnp.exp(s - m_new)
            alpha = jnp.exp(m_old - m_new)
            l_sc[h] = alpha * l_sc[h] + jnp.sum(p, axis=-1, keepdims=True)
            acc_sc[h] = alpha * acc_sc[h] + jnp.dot(
                p.astype(jnp.bfloat16), v, preferred_element_type=jnp.float32)
            m_sc[h] = m_new

    live = j < cnt_ref[i]
    full = full_ref[i, j] == 1

    @pl.when(live & full)
    def _():
        update(None)

    @pl.when(live & jnp.logical_not(full))
    def _():
        span = k_ref.shape[0]
        kpos = seq_ref[i, j] * span + lax.broadcasted_iota(jnp.int32, (1, span), 1)
        update((kpos <= qpos_ref[...]) & (kpos >= qstart_ref[...]))

    @pl.when(j == pl.num_programs(1) - 1)
    def _():
        for h in range(heads):
            o_ref[:, h * HEAD_DIM:(h + 1) * HEAD_DIM] = (acc_sc[h] / l_sc[h]).astype(o_ref.dtype)


def span_attention(which, tbl, seq, cnt, full, queries, qpos, qstart, kv):
    rows, q_cols = queries.shape
    heads = q_cols // HEAD_DIM
    n_q = 1
    kernel = functools.partial(attention_kernel, heads, 1.0 / math.sqrt(HEAD_DIM))
    steps = n_q * KEY_SLOTS
    cost = pl.CostEstimate(
        flops=4 * steps * heads * SPAN * SPAN * HEAD_DIM,
        transcendentals=steps * heads * SPAN * SPAN,
        bytes_accessed=steps * 2 * SPAN * HEAD_DIM * 2 + 2 * SPAN * q_cols * 2,
    )
    return pl.pallas_call(
        kernel,
        out_shape=jax.ShapeDtypeStruct((SPAN, q_cols), jnp.bfloat16),
        grid_spec=pltpu.PrefetchScalarGridSpec(
            num_scalar_prefetch=5,
            grid=(n_q, KEY_SLOTS),
            in_specs=[
                pl.BlockSpec((SPAN, q_cols), lambda i, j, w, t, s, c, f: (w[0], 0)),
                pl.BlockSpec((SPAN, 1), lambda i, j, w, t, s, c, f: (w[0], 0)),
                pl.BlockSpec((SPAN, 1), lambda i, j, w, t, s, c, f: (w[0], 0)),
                pl.BlockSpec((None, SPAN, HEAD_DIM), lambda i, j, w, t, s, c, f: (0, t[i, j], 0)),
                pl.BlockSpec((None, SPAN, HEAD_DIM), lambda i, j, w, t, s, c, f: (1, t[i, j], 0)),
            ],
            out_specs=pl.BlockSpec((SPAN, q_cols), lambda i, j, w, t, s, c, f: (0, 0)),
            scratch_shapes=[
                pltpu.VMEM((heads, SPAN, 1), jnp.float32),
                pltpu.VMEM((heads, SPAN, 1), jnp.float32),
                pltpu.VMEM((heads, SPAN, HEAD_DIM), jnp.float32),
            ],
        ),
        compiler_params=pltpu.CompilerParams(dimension_semantics=("arbitrary", "arbitrary")),
        cost_estimate=cost,
    )(which, tbl, seq, cnt, full, queries, qpos, qstart, kv, kv)


def key_tables(span_order, doc_ends, query_spans):
    n_spans = span_order.shape[0]
    span_ids = jnp.arange(n_spans, dtype=jnp.int32)
    inverse = jnp.sum(
        jnp.where(span_order[None, :] == span_ids[:, None], span_ids[None, :], 0), axis=1)
    first_doc = jnp.sum((doc_ends[None, :] <= (span_ids * SPAN)[:, None]).astype(jnp.int32), axis=1)
    last_doc = jnp.sum(
        (doc_ends[None, :] <= (span_ids * SPAN + SPAN - 1)[:, None]).astype(jnp.int32), axis=1)
    sq = jnp.sum(jnp.where(query_spans[:, None] == span_ids[None, :], span_order[None, :], 0), axis=1)
    q_first = jnp.sum(jnp.where(sq[:, None] == span_ids[None, :], first_doc[None, :], 0), axis=1)
    back = jnp.arange(KEY_SLOTS, dtype=jnp.int32) - (KEY_SLOTS - 1)
    cand = sq[:, None] + back[None, :]
    cand_last = jnp.sum(
        jnp.where(cand[:, :, None] == span_ids[None, None, :], last_doc[None, None, :], 0), axis=2)
    valid = (cand >= 0) & (cand_last >= q_first[:, None])
    count = jnp.sum(valid.astype(jnp.int32), axis=1)
    slot = jnp.arange(KEY_SLOTS, dtype=jnp.int32)
    seq = jnp.minimum(sq[:, None] - count[:, None] + 1 + slot[None, :], sq[:, None])
    tbl = jnp.sum(jnp.where(seq[:, :, None] == span_ids[None, None, :], inverse[None, None, :], 0),
                  axis=2)
    last_start = jnp.max(
        jnp.where(doc_ends[None, :] <= (sq * SPAN + SPAN - 1)[:, None], doc_ends[None, :], 0), axis=1)
    full = (seq < sq[:, None]) & (seq * SPAN >= last_start[:, None])
    return (tbl.astype(jnp.int32), seq.astype(jnp.int32), count.astype(jnp.int32),
            full.astype(jnp.int32))


def shift_x(value, d, n):
    return lax.ppermute(value, "x", [(i, (i + d) % n) for i in range(n)])


def reduce_scatter_x(value):
    n = lax.axis_size("x")
    me = lax.axis_index("x")
    parts = value.reshape(n, value.shape[0] // n, *value.shape[1:])
    total = jnp.take(parts, me, axis=0).astype(jnp.float32)
    for d in range(1, n):
        total = total + shift_x(jnp.take(parts, (me + d) % n, axis=0), d, n).astype(jnp.float32)
    return total.astype(value.dtype)


def per_device(tokens, norm_gain, q_weight, k_weight, v_weight, o_weight, doc_lengths, span_order):
    local_rows = tokens.shape[1]
    tok_dev = local_rows * lax.axis_size(TENSOR)
    model_width = tokens.shape[2]
    head_dim = HEAD_DIM
    q_cols = q_weight.shape[1]
    kv_cols = k_weight.shape[1]
    q_heads = q_cols // head_dim
    kv_local = kv_cols // head_dim
    span_rows = tok_dev // 2
    base_row = lax.axis_index(CONTEXT) * tok_dev
    rows_float = tokens.astype(jnp.float32)
    normed = (
        rows_float
        * lax.rsqrt(jnp.mean(rows_float * rows_float, axis=-1, keepdims=True) + epsilon)
        * norm_gain
    ).astype(jnp.bfloat16)
    plane = lax.axis_index("yh")
    core = lax.axis_index("core")
    weights = jnp.concatenate([q_weight, k_weight, v_weight], axis=1)
    half_in = weights.shape[0] // 2
    sent_half = lax.dynamic_slice_in_dim(weights, core * half_in, half_in, 0)
    plane_rows = lax.all_gather(normed, "x", axis=1, tiled=True)
    partner_half = lax.ppermute(sent_half, ("yh", "ylo"), NEIGHBOUR)
    plane_rows, partner_half = lax.optimization_barrier((plane_rows, partner_half))
    other_half = lax.ppermute(partner_half, "core", [(0, 1), (1, 0)])
    half = plane_rows.shape[1]
    flat_rows = plane_rows.reshape(half, model_width)
    all_places = positions(base_row + jnp.arange(tok_dev, dtype=jnp.int32), span_order, span_rows)
    places = lax.dynamic_slice_in_dim(all_places, plane * half, half, 0)
    rows_mine = lax.dynamic_slice_in_dim(flat_rows, core * half_in, half_in, 1)
    rows_other = lax.dynamic_slice_in_dim(flat_rows, (1 - core) * half_in, half_in, 1)

    def finish(out):
        q = rotary(out[:, :q_cols].reshape(half, q_heads, head_dim), places)
        k = rotary(out[:, q_cols:q_cols + kv_cols].reshape(half, kv_local, head_dim), places)
        return jnp.concatenate(
            [q.reshape(half, q_cols), k.reshape(half, kv_cols), out[:, q_cols + kv_cols:]], axis=1
        ).astype(jnp.bfloat16)

    def project(w):
        return finish(jnp.dot(flat_rows, w, preferred_element_type=jnp.float32))

    for_partner = finish(
        jnp.dot(rows_mine, partner_half, preferred_element_type=jnp.float32)
        + jnp.dot(rows_other, other_half, preferred_element_type=jnp.float32))
    received = lax.ppermute(for_partner, "yh", [(0, 1), (1, 0)])
    flat_rows, for_partner = lax.optimization_barrier((flat_rows, for_partner))
    own = project(weights)
    first = jnp.where(plane == 0, own, received)
    second = jnp.where(plane == 0, received, own)
    projected = jnp.concatenate([first, second], axis=0)
    query_rows = projected[:, :q_cols]
    kv_pair = jnp.stack([projected[:, q_cols:q_cols + kv_cols], projected[:, q_cols + kv_cols:]])
    gathered = lax.all_gather(kv_pair, CONTEXT, axis=1, tiled=True)
    places = all_places
    row_count = tok_dev

    doc_ends = jnp.cumsum(doc_lengths)
    query_start = jnp.max(
        jnp.where(doc_ends[None, :] <= places[:, None], doc_ends[None, :], 0), axis=1)
    query_spans = lax.axis_index(CONTEXT) * 2 + jnp.arange(2, dtype=jnp.int32)
    tbl, seq, cnt, full = key_tables(span_order, doc_ends, query_spans)
    plane_q = lax.axis_index("yh")
    qpos_col = places.astype(jnp.int32)[:, None]
    qstart_col = query_start.astype(jnp.int32)[:, None]

    def attend(which):
        pick = lambda a: lax.dynamic_slice_in_dim(a, which, 1, 0)
        return span_attention(
            jnp.reshape(which, (1,)).astype(jnp.int32), pick(tbl), pick(seq), pick(cnt), pick(full),
            query_rows, qpos_col, qstart_col, gathered)

    other_rows = attend(1 - plane_q)
    partner_o = lax.ppermute(o_weight, ("yh", "ylo"), NEIGHBOUR)
    partner_rows = lax.ppermute(other_rows, "yh", [(0, 1), (1, 0)])
    own_rows = attend(plane_q)
    mixed = jnp.dot(
        jnp.concatenate([own_rows, partner_rows], axis=1),
        jnp.concatenate([o_weight, partner_o], axis=0),
        preferred_element_type=jnp.float32,
    ).astype(jnp.bfloat16)
    mixed_rows = reduce_scatter_x(mixed)
    return mixed_rows.reshape(tokens.shape)


TENSOR = ("yh", "x")
NEIGHBOUR = [(0, 3), (3, 0), (1, 2), (2, 1)]
CONTEXT = ("z", "ylo", "core")


def solution(mesh):
    devices = mesh.devices.reshape(2, mesh.devices.shape[0] // 2, -1, 2, 2)
    split_mesh = jax.sharding.Mesh(devices, ("yh", "x", "z", "ylo", "core"))
    in_specs = (
        P(CONTEXT, TENSOR, None),
        P(),
        P(None, TENSOR),
        P(None, TENSOR),
        P(None, TENSOR),
        P(TENSOR, None),
        P(),
        P(),
    )
    out_specs = P(CONTEXT, TENSOR, None)
    return jax.shard_map(
        per_device, mesh=split_mesh, in_specs=in_specs, out_specs=out_specs, check_vma=False
    )
```

```python
import functools
import math

import jax
import jax.numpy as jnp
from jax import lax
from jax.experimental import pallas as pl
from jax.experimental.pallas import tpu as pltpu
from jax.sharding import PartitionSpec as P

HEAD_DIM = 128
SPAN = 512
KEY_SLOTS = 9

rope_theta = 500000.0
epsilon = 1e-05
masked_score = -1e30


def positions(rows, span_order, span_rows):
    slot_ids = jnp.arange(span_order.shape[0], dtype=jnp.int32)
    matches = (rows // span_rows)[:, None] == slot_ids[None, :]
    picked = jnp.sum(jnp.where(matches, span_order[None, :], 0), axis=1)
    return picked * span_rows + rows % span_rows


def rotary(values, places):
    head_dim = values.shape[-1]
    half_dim = head_dim // 2
    frequency = rope_theta ** (-(2.0 / head_dim) * jnp.arange(half_dim, dtype=jnp.float32))
    angles = places.astype(jnp.float32)[:, None] * frequency[None, :]
    cosine = jnp.cos(angles)[:, None, :]
    sine_part = jnp.sin(angles)[:, None, :]
    first_half = values[..., :half_dim]
    second = values[..., half_dim:]
    return jnp.concatenate(
        [first_half * cosine - second * sine_part, second * cosine + first_half * sine_part],
        axis=-1,
    )


def attention_kernel(heads, scale, tbl_ref, seq_ref, cnt_ref, full_ref, q_ref, qpos_ref, qstart_ref,
                     k_ref, v_ref, o_ref, m_sc, l_sc, acc_sc):
    i = pl.program_id(0)
    j = pl.program_id(1)

    @pl.when(j == 0)
    def _():
        m_sc[...] = jnp.full_like(m_sc, masked_score)
        l_sc[...] = jnp.zeros_like(l_sc)
        acc_sc[...] = jnp.zeros_like(acc_sc)

    def update(visible):
        k = k_ref[...]
        v = v_ref[...]
        for h in range(heads):
            q = q_ref[:, h * HEAD_DIM:(h + 1) * HEAD_DIM]
            s = lax.dot_general(q, k, (((1,), (1,)), ((), ())),
                                preferred_element_type=jnp.float32) * scale
            if visible is not None:
                s = jnp.where(visible, s, masked_score)
            m_old = m_sc[h]
            m_new = jnp.maximum(m_old, jnp.max(s, axis=-1, keepdims=True))
            p = jnp.exp(s - m_new)
            alpha = jnp.exp(m_old - m_new)
            l_sc[h] = alpha * l_sc[h] + jnp.sum(p, axis=-1, keepdims=True)
            acc_sc[h] = alpha * acc_sc[h] + jnp.dot(
                p.astype(jnp.bfloat16), v, preferred_element_type=jnp.float32)
            m_sc[h] = m_new

    live = j < cnt_ref[i]
    full = full_ref[i, j] == 1

    @pl.when(live & full)
    def _():
        update(None)

    @pl.when(live & jnp.logical_not(full))
    def _():
        span = k_ref.shape[0]
        kpos = seq_ref[i, j] * span + lax.broadcasted_iota(jnp.int32, (1, span), 1)
        update((kpos <= qpos_ref[...]) & (kpos >= qstart_ref[...]))

    @pl.when(j == pl.num_programs(1) - 1)
    def _():
        for h in range(heads):
            o_ref[:, h * HEAD_DIM:(h + 1) * HEAD_DIM] = (acc_sc[h] / l_sc[h]).astype(o_ref.dtype)


def span_attention(tbl, seq, cnt, full, queries, qpos, qstart, kv):
    rows, q_cols = queries.shape
    heads = q_cols // HEAD_DIM
    n_q = rows // SPAN
    kernel = functools.partial(attention_kernel, heads, 1.0 / math.sqrt(HEAD_DIM))
    steps = n_q * KEY_SLOTS
    cost = pl.CostEstimate(
        flops=4 * steps * heads * SPAN * SPAN * HEAD_DIM,
        transcendentals=steps * heads * SPAN * SPAN,
        bytes_accessed=steps * 2 * SPAN * HEAD_DIM * 2 + 2 * rows * q_cols * 2,
    )
    return pl.pallas_call(
        kernel,
        out_shape=jax.ShapeDtypeStruct((rows, q_cols), jnp.bfloat16),
        grid_spec=pltpu.PrefetchScalarGridSpec(
            num_scalar_prefetch=4,
            grid=(n_q, KEY_SLOTS),
            in_specs=[
                pl.BlockSpec((SPAN, q_cols), lambda i, j, t, s, c, f: (i, 0)),
                pl.BlockSpec((SPAN, 1), lambda i, j, t, s, c, f: (i, 0)),
                pl.BlockSpec((SPAN, 1), lambda i, j, t, s, c, f: (i, 0)),
                pl.BlockSpec((None, SPAN, HEAD_DIM), lambda i, j, t, s, c, f: (0, t[i, j], 0)),
                pl.BlockSpec((None, SPAN, HEAD_DIM), lambda i, j, t, s, c, f: (1, t[i, j], 0)),
            ],
            out_specs=pl.BlockSpec((SPAN, q_cols), lambda i, j, t, s, c, f: (i, 0)),
            scratch_shapes=[
                pltpu.VMEM((heads, SPAN, 1), jnp.float32),
                pltpu.VMEM((heads, SPAN, 1), jnp.float32),
                pltpu.VMEM((heads, SPAN, HEAD_DIM), jnp.float32),
            ],
        ),
        compiler_params=pltpu.CompilerParams(dimension_semantics=("arbitrary", "arbitrary")),
        cost_estimate=cost,
    )(tbl, seq, cnt, full, queries, qpos, qstart, kv, kv)


def key_tables(span_order, doc_ends, query_spans):
    n_spans = span_order.shape[0]
    span_ids = jnp.arange(n_spans, dtype=jnp.int32)
    inverse = jnp.sum(
        jnp.where(span_order[None, :] == span_ids[:, None], span_ids[None, :], 0), axis=1)
    first_doc = jnp.sum((doc_ends[None, :] <= (span_ids * SPAN)[:, None]).astype(jnp.int32), axis=1)
    last_doc = jnp.sum(
        (doc_ends[None, :] <= (span_ids * SPAN + SPAN - 1)[:, None]).astype(jnp.int32), axis=1)
    sq = jnp.sum(jnp.where(query_spans[:, None] == span_ids[None, :], span_order[None, :], 0), axis=1)
    q_first = jnp.sum(jnp.where(sq[:, None] == span_ids[None, :], first_doc[None, :], 0), axis=1)
    back = jnp.arange(KEY_SLOTS, dtype=jnp.int32) - (KEY_SLOTS - 1)
    cand = sq[:, None] + back[None, :]
    cand_last = jnp.sum(
        jnp.where(cand[:, :, None] == span_ids[None, None, :], last_doc[None, None, :], 0), axis=2)
    valid = (cand >= 0) & (cand_last >= q_first[:, None])
    count = jnp.sum(valid.astype(jnp.int32), axis=1)
    slot = jnp.arange(KEY_SLOTS, dtype=jnp.int32)
    seq = jnp.minimum(sq[:, None] - count[:, None] + 1 + slot[None, :], sq[:, None])
    tbl = jnp.sum(jnp.where(seq[:, :, None] == span_ids[None, None, :], inverse[None, None, :], 0),
                  axis=2)
    last_start = jnp.max(
        jnp.where(doc_ends[None, :] <= (sq * SPAN + SPAN - 1)[:, None], doc_ends[None, :], 0), axis=1)
    full = (seq < sq[:, None]) & (seq * SPAN >= last_start[:, None])
    return (tbl.astype(jnp.int32), seq.astype(jnp.int32), count.astype(jnp.int32),
            full.astype(jnp.int32))


def shift_x(value, d, n):
    return lax.ppermute(value, "x", [(i, (i + d) % n) for i in range(n)])


def reduce_scatter_x(value):
    n = lax.axis_size("x")
    me = lax.axis_index("x")
    parts = value.reshape(n, value.shape[0] // n, *value.shape[1:])
    total = jnp.take(parts, me, axis=0).astype(jnp.float32)
    for d in range(1, n):
        total = total + shift_x(jnp.take(parts, (me + d) % n, axis=0), d, n).astype(jnp.float32)
    return total.astype(value.dtype)


def per_device(tokens, norm_gain, q_weight, k_weight, v_weight, o_weight, doc_lengths, span_order):
    local_rows = tokens.shape[1]
    tok_dev = local_rows * lax.axis_size(TENSOR)
    model_width = tokens.shape[2]
    head_dim = HEAD_DIM
    q_cols = q_weight.shape[1]
    kv_cols = k_weight.shape[1]
    q_heads = q_cols // head_dim
    kv_local = kv_cols // head_dim
    span_rows = tok_dev // 2
    base_row = lax.axis_index(CONTEXT) * tok_dev
    rows_float = tokens.astype(jnp.float32)
    normed = (
        rows_float
        * lax.rsqrt(jnp.mean(rows_float * rows_float, axis=-1, keepdims=True) + epsilon)
        * norm_gain
    ).astype(jnp.bfloat16)
    plane = lax.axis_index("yh")
    core = lax.axis_index("core")
    own_parts = (q_weight, k_weight, v_weight)
    half_in = q_weight.shape[0] // 2
    sent_parts = [lax.dynamic_slice_in_dim(w, core * half_in, half_in, 0) for w in own_parts]
    plane_rows = lax.all_gather(normed, "x", axis=1, tiled=True)
    partner_parts = [lax.ppermute(w, ("yh", "ylo"), NEIGHBOUR) for w in sent_parts]
    plane_rows, partner_parts = lax.optimization_barrier((plane_rows, partner_parts))
    other_parts = [lax.ppermute(w, "core", [(0, 1), (1, 0)]) for w in partner_parts]
    half = plane_rows.shape[1]
    flat_rows = plane_rows.reshape(half, model_width)
    all_places = positions(base_row + jnp.arange(tok_dev, dtype=jnp.int32), span_order, span_rows)
    places = lax.dynamic_slice_in_dim(all_places, plane * half, half, 0)
    rows_mine = lax.dynamic_slice_in_dim(flat_rows, core * half_in, half_in, 1)
    rows_other = lax.dynamic_slice_in_dim(flat_rows, (1 - core) * half_in, half_in, 1)

    def finish(q, k, v):
        q = rotary(q.reshape(half, q_heads, head_dim), places)
        k = rotary(k.reshape(half, kv_local, head_dim), places)
        return jnp.concatenate(
            [q.reshape(half, q_cols), k.reshape(half, kv_cols), v], axis=1).astype(jnp.bfloat16)

    for_partner = finish(*[
        jnp.dot(rows_mine, a, preferred_element_type=jnp.float32)
        + jnp.dot(rows_other, b, preferred_element_type=jnp.float32)
        for a, b in zip(partner_parts, other_parts)])
    received = lax.ppermute(for_partner, "yh", [(0, 1), (1, 0)])
    flat_rows, for_partner = lax.optimization_barrier((flat_rows, for_partner))
    own = finish(*[jnp.dot(flat_rows, w, preferred_element_type=jnp.float32) for w in own_parts])
    first = jnp.where(plane == 0, own, received)
    second = jnp.where(plane == 0, received, own)
    projected = jnp.concatenate([first, second], axis=0)
    query_rows = projected[:, :q_cols]
    kv_pair = jnp.stack([projected[:, q_cols:q_cols + kv_cols], projected[:, q_cols + kv_cols:]])
    gathered = lax.all_gather(kv_pair, CONTEXT, axis=1, tiled=True)
    places = all_places
    row_count = tok_dev

    doc_ends = jnp.cumsum(doc_lengths)
    query_start = jnp.max(
        jnp.where(doc_ends[None, :] <= places[:, None], doc_ends[None, :], 0), axis=1)
    query_spans = lax.axis_index(CONTEXT) * 2 + jnp.arange(2, dtype=jnp.int32)
    tbl, seq, cnt, full = key_tables(span_order, doc_ends, query_spans)
    attended = span_attention(
        tbl, seq, cnt, full, query_rows,
        places.astype(jnp.int32)[:, None], query_start.astype(jnp.int32)[:, None],
        gathered,
    )
    partner_o = lax.ppermute(o_weight, ("yh", "ylo"), NEIGHBOUR)
    half = row_count // 2
    own_rows = lax.dynamic_slice_in_dim(attended, plane * half, half, 0)
    other_rows = lax.dynamic_slice_in_dim(attended, (1 - plane) * half, half, 0)
    partner_rows = lax.ppermute(other_rows, "yh", [(0, 1), (1, 0)])
    mixed = jnp.dot(
        jnp.concatenate([own_rows, partner_rows], axis=1),
        jnp.concatenate([o_weight, partner_o], axis=0),
        preferred_element_type=jnp.float32,
    ).astype(jnp.bfloat16)
    mixed_rows = reduce_scatter_x(mixed)
    return mixed_rows.reshape(tokens.shape)


TENSOR = ("yh", "x")
NEIGHBOUR = [(0, 3), (3, 0), (1, 2), (2, 1)]
CONTEXT = ("z", "ylo", "core")


def solution(mesh):
    devices = mesh.devices.reshape(2, mesh.devices.shape[0] // 2, -1, 2, 2)
    split_mesh = jax.sharding.Mesh(devices, ("yh", "x", "z", "ylo", "core"))
    in_specs = (
        P(CONTEXT, TENSOR, None),
        P(),
        P(None, TENSOR),
        P(None, TENSOR),
        P(None, TENSOR),
        P(TENSOR, None),
        P(),
        P(),
    )
    out_specs = P(CONTEXT, TENSOR, None)
    return jax.shard_map(
        per_device, mesh=split_mesh, in_specs=in_specs, out_specs=out_specs, check_vma=False
    )
```

```python
import functools
import math

import jax
import jax.numpy as jnp
from jax import lax
from jax.experimental import pallas as pl
from jax.experimental.pallas import tpu as pltpu
from jax.sharding import PartitionSpec as P

HEAD_DIM = 128
SPAN = 512
KEY_SLOTS = 9

rope_theta = 500000.0
epsilon = 1e-05
masked_score = -1e30


def positions(rows, span_order, span_rows):
    slot_ids = jnp.arange(span_order.shape[0], dtype=jnp.int32)
    matches = (rows // span_rows)[:, None] == slot_ids[None, :]
    picked = jnp.sum(jnp.where(matches, span_order[None, :], 0), axis=1)
    return picked * span_rows + rows % span_rows


def rotary(values, places):
    head_dim = values.shape[-1]
    half_dim = head_dim // 2
    frequency = rope_theta ** (-(2.0 / head_dim) * jnp.arange(half_dim, dtype=jnp.float32))
    angles = places.astype(jnp.float32)[:, None] * frequency[None, :]
    cosine = jnp.cos(angles)[:, None, :]
    sine_part = jnp.sin(angles)[:, None, :]
    first_half = values[..., :half_dim]
    second = values[..., half_dim:]
    return jnp.concatenate(
        [first_half * cosine - second * sine_part, second * cosine + first_half * sine_part],
        axis=-1,
    )


def online_update(heads, scale, q_ref, k_ref, v_ref, visible, m_sc, l_sc, acc_sc):
    k = k_ref[...]
    v = v_ref[...]
    for h in range(heads):
        q = q_ref[:, h * HEAD_DIM:(h + 1) * HEAD_DIM]
        s = lax.dot_general(q, k, (((1,), (1,)), ((), ())),
                            preferred_element_type=jnp.float32) * scale
        m_old = m_sc[h]
        m_new = jnp.maximum(
            m_old, jnp.max(jnp.where(visible, s, masked_score), axis=-1, keepdims=True))
        p = jnp.where(visible, jnp.exp(s - m_new), 0.0)
        alpha = jnp.exp(m_old - m_new)
        l_sc[h] = alpha * l_sc[h] + jnp.sum(p, axis=-1, keepdims=True)
        acc_sc[h] = alpha * acc_sc[h] + jnp.dot(
            p.astype(jnp.bfloat16), v, preferred_element_type=jnp.float32)
        m_sc[h] = m_new


def diagonal_kernel(heads, scale, sq_ref, q_ref, qpos_ref, qstart_ref, k_ref, v_ref,
                    m_ref, l_ref, acc_ref):
    i = pl.program_id(0)
    m_ref[...] = jnp.full_like(m_ref, masked_score)
    l_ref[...] = jnp.zeros_like(l_ref)
    acc_ref[...] = jnp.zeros_like(acc_ref)
    span = k_ref.shape[0]
    kpos = sq_ref[i] * span + lax.broadcasted_iota(jnp.int32, (1, span), 1)
    visible = (kpos <= qpos_ref[...]) & (kpos >= qstart_ref[...])
    online_update(heads, scale, q_ref, k_ref, v_ref, visible, m_ref, l_ref, acc_ref)


def attention_kernel(heads, scale, tbl_ref, seq_ref, cnt_ref, q_ref, qpos_ref, qstart_ref,
                     k_ref, v_ref, m_in, l_in, acc_in, o_ref, m_sc, l_sc, acc_sc):
    i = pl.program_id(0)
    j = pl.program_id(1)

    @pl.when(j == 0)
    def _():
        m_sc[...] = m_in[...]
        l_sc[...] = l_in[...]
        acc_sc[...] = acc_in[...]

    @pl.when(j < cnt_ref[i])
    def _():
        span = k_ref.shape[0]
        kpos = seq_ref[i, j] * span + lax.broadcasted_iota(jnp.int32, (1, span), 1)
        visible = (kpos <= qpos_ref[...]) & (kpos >= qstart_ref[...])
        online_update(heads, scale, q_ref, k_ref, v_ref, visible, m_sc, l_sc, acc_sc)

    @pl.when(j == pl.num_programs(1) - 1)
    def _():
        for h in range(heads):
            o_ref[:, h * HEAD_DIM:(h + 1) * HEAD_DIM] = (acc_sc[h] / l_sc[h]).astype(o_ref.dtype)


def diagonal_attention(sq, queries, qpos, qstart, local_kv):
    rows, q_cols = queries.shape
    heads = q_cols // HEAD_DIM
    n_q = rows // SPAN
    kernel = functools.partial(diagonal_kernel, heads, 1.0 / math.sqrt(HEAD_DIM))
    state = lambda w: pl.BlockSpec((None, heads, SPAN, w), lambda i, s: (i, 0, 0, 0))
    cost = pl.CostEstimate(
        flops=4 * n_q * heads * SPAN * SPAN * HEAD_DIM,
        transcendentals=n_q * heads * SPAN * SPAN,
        bytes_accessed=2 * rows * q_cols + 4 * rows * HEAD_DIM + 4 * n_q * heads * SPAN * 130,
    )
    return pl.pallas_call(
        kernel,
        out_shape=(
            jax.ShapeDtypeStruct((n_q, heads, SPAN, 1), jnp.float32),
            jax.ShapeDtypeStruct((n_q, heads, SPAN, 1), jnp.float32),
            jax.ShapeDtypeStruct((n_q, heads, SPAN, HEAD_DIM), jnp.float32),
        ),
        grid_spec=pltpu.PrefetchScalarGridSpec(
            num_scalar_prefetch=1,
            grid=(n_q,),
            in_specs=[
                pl.BlockSpec((SPAN, q_cols), lambda i, s: (i, 0)),
                pl.BlockSpec((SPAN, 1), lambda i, s: (i, 0)),
                pl.BlockSpec((SPAN, 1), lambda i, s: (i, 0)),
                pl.BlockSpec((None, SPAN, HEAD_DIM), lambda i, s: (0, i, 0)),
                pl.BlockSpec((None, SPAN, HEAD_DIM), lambda i, s: (1, i, 0)),
            ],
            out_specs=[state(1), state(1), state(HEAD_DIM)],
        ),
        compiler_params=pltpu.CompilerParams(dimension_semantics=("arbitrary",)),
        cost_estimate=cost,
    )(sq, queries, qpos, qstart, local_kv, local_kv)


def span_attention(tbl, seq, cnt, queries, qpos, qstart, kv, m0, l0, acc0):
    rows, q_cols = queries.shape
    heads = q_cols // HEAD_DIM
    n_q = rows // SPAN
    slots = tbl.shape[1]
    kernel = functools.partial(attention_kernel, heads, 1.0 / math.sqrt(HEAD_DIM))
    steps = n_q * slots
    state = lambda w: pl.BlockSpec((None, heads, SPAN, w), lambda i, j, t, s, c: (i, 0, 0, 0))
    cost = pl.CostEstimate(
        flops=4 * steps * heads * SPAN * SPAN * HEAD_DIM,
        transcendentals=steps * heads * SPAN * SPAN,
        bytes_accessed=steps * 2 * SPAN * HEAD_DIM * 2 + 2 * rows * q_cols * 2,
    )
    return pl.pallas_call(
        kernel,
        out_shape=jax.ShapeDtypeStruct((rows, q_cols), jnp.bfloat16),
        grid_spec=pltpu.PrefetchScalarGridSpec(
            num_scalar_prefetch=3,
            grid=(n_q, slots),
            in_specs=[
                pl.BlockSpec((SPAN, q_cols), lambda i, j, t, s, c: (i, 0)),
                pl.BlockSpec((SPAN, 1), lambda i, j, t, s, c: (i, 0)),
                pl.BlockSpec((SPAN, 1), lambda i, j, t, s, c: (i, 0)),
                pl.BlockSpec((None, SPAN, HEAD_DIM), lambda i, j, t, s, c: (0, t[i, j], 0)),
                pl.BlockSpec((None, SPAN, HEAD_DIM), lambda i, j, t, s, c: (1, t[i, j], 0)),
                state(1), state(1), state(HEAD_DIM),
            ],
            out_specs=pl.BlockSpec((SPAN, q_cols), lambda i, j, t, s, c: (i, 0)),
            scratch_shapes=[
                pltpu.VMEM((heads, SPAN, 1), jnp.float32),
                pltpu.VMEM((heads, SPAN, 1), jnp.float32),
                pltpu.VMEM((heads, SPAN, HEAD_DIM), jnp.float32),
            ],
        ),
        compiler_params=pltpu.CompilerParams(dimension_semantics=("arbitrary", "arbitrary")),
        cost_estimate=cost,
    )(tbl, seq, cnt, queries, qpos, qstart, kv, kv, m0, l0, acc0)


def key_tables(span_order, doc_ends, query_spans):
    n_spans = span_order.shape[0]
    span_ids = jnp.arange(n_spans, dtype=jnp.int32)
    inverse = jnp.sum(
        jnp.where(span_order[None, :] == span_ids[:, None], span_ids[None, :], 0), axis=1)
    first_doc = jnp.sum((doc_ends[None, :] <= (span_ids * SPAN)[:, None]).astype(jnp.int32), axis=1)
    last_doc = jnp.sum(
        (doc_ends[None, :] <= (span_ids * SPAN + SPAN - 1)[:, None]).astype(jnp.int32), axis=1)
    sq = jnp.sum(jnp.where(query_spans[:, None] == span_ids[None, :], span_order[None, :], 0), axis=1)
    q_first = jnp.sum(jnp.where(sq[:, None] == span_ids[None, :], first_doc[None, :], 0), axis=1)
    back = jnp.arange(KEY_SLOTS, dtype=jnp.int32) - (KEY_SLOTS - 1)
    cand = sq[:, None] + back[None, :]
    cand_last = jnp.sum(
        jnp.where(cand[:, :, None] == span_ids[None, None, :], last_doc[None, None, :], 0), axis=2)
    valid = (cand >= 0) & (cand_last >= q_first[:, None])
    count = jnp.sum(valid.astype(jnp.int32), axis=1)
    before = count - 1
    slot = jnp.arange(KEY_SLOTS - 1, dtype=jnp.int32)
    last = jnp.maximum(sq - 1, 0)
    seq = jnp.clip(sq[:, None] - before[:, None] + slot[None, :], 0, last[:, None])
    tbl = jnp.sum(jnp.where(seq[:, :, None] == span_ids[None, None, :], inverse[None, None, :], 0),
                  axis=2)
    return tbl.astype(jnp.int32), seq.astype(jnp.int32), before.astype(jnp.int32), sq.astype(jnp.int32)


def shift_x(value, d, n):
    return lax.ppermute(value, "x", [(i, (i + d) % n) for i in range(n)])


def reduce_scatter_x(value):
    n = lax.axis_size("x")
    me = lax.axis_index("x")
    parts = value.reshape(n, value.shape[0] // n, *value.shape[1:])
    total = jnp.take(parts, me, axis=0).astype(jnp.float32)
    for d in range(1, n):
        total = total + shift_x(jnp.take(parts, (me + d) % n, axis=0), d, n).astype(jnp.float32)
    return total.astype(value.dtype)


def per_device(tokens, norm_gain, q_weight, k_weight, v_weight, o_weight, doc_lengths, span_order):
    local_rows = tokens.shape[1]
    tok_dev = local_rows * lax.axis_size(TENSOR)
    model_width = tokens.shape[2]
    head_dim = HEAD_DIM
    q_cols = q_weight.shape[1]
    kv_cols = k_weight.shape[1]
    q_heads = q_cols // head_dim
    kv_local = kv_cols // head_dim
    span_rows = tok_dev // 2
    base_row = lax.axis_index(CONTEXT) * tok_dev
    rows_float = tokens.astype(jnp.float32)
    normed = (
        rows_float
        * lax.rsqrt(jnp.mean(rows_float * rows_float, axis=-1, keepdims=True) + epsilon)
        * norm_gain
    ).astype(jnp.bfloat16)
    plane = lax.axis_index("yh")
    core = lax.axis_index("core")
    weights = jnp.concatenate([q_weight, k_weight, v_weight], axis=1)
    half_in = weights.shape[0] // 2
    sent_half = lax.dynamic_slice_in_dim(weights, core * half_in, half_in, 0)
    plane_rows = lax.all_gather(normed, "x", axis=1, tiled=True)
    partner_half = lax.ppermute(sent_half, ("yh", "ylo"), NEIGHBOUR)
    plane_rows, partner_half = lax.optimization_barrier((plane_rows, partner_half))
    other_half = lax.ppermute(partner_half, "core", [(0, 1), (1, 0)])
    half = plane_rows.shape[1]
    flat_rows = plane_rows.reshape(half, model_width)
    all_places = positions(base_row + jnp.arange(tok_dev, dtype=jnp.int32), span_order, span_rows)
    places = lax.dynamic_slice_in_dim(all_places, plane * half, half, 0)
    rows_mine = lax.dynamic_slice_in_dim(flat_rows, core * half_in, half_in, 1)
    rows_other = lax.dynamic_slice_in_dim(flat_rows, (1 - core) * half_in, half_in, 1)

    def finish(out):
        q = rotary(out[:, :q_cols].reshape(half, q_heads, head_dim), places)
        k = rotary(out[:, q_cols:q_cols + kv_cols].reshape(half, kv_local, head_dim), places)
        return jnp.concatenate(
            [q.reshape(half, q_cols), k.reshape(half, kv_cols), out[:, q_cols + kv_cols:]], axis=1
        ).astype(jnp.bfloat16)

    def project(w):
        return finish(jnp.dot(flat_rows, w, preferred_element_type=jnp.float32))

    for_partner = finish(
        jnp.dot(rows_mine, partner_half, preferred_element_type=jnp.float32)
        + jnp.dot(rows_other, other_half, preferred_element_type=jnp.float32))
    received = lax.ppermute(for_partner, "yh", [(0, 1), (1, 0)])
    flat_rows, for_partner = lax.optimization_barrier((flat_rows, for_partner))
    own = project(weights)
    first = jnp.where(plane == 0, own, received)
    second = jnp.where(plane == 0, received, own)
    projected = jnp.concatenate([first, second], axis=0)
    query_rows = projected[:, :q_cols]
    kv_pair = jnp.stack([projected[:, q_cols:q_cols + kv_cols], projected[:, q_cols + kv_cols:]])
    gathered = lax.all_gather(kv_pair, CONTEXT, axis=1, tiled=True)
    places = all_places
    row_count = tok_dev

    doc_ends = jnp.cumsum(doc_lengths)
    query_start = jnp.max(
        jnp.where(doc_ends[None, :] <= places[:, None], doc_ends[None, :], 0), axis=1)
    query_spans = lax.axis_index(CONTEXT) * 2 + jnp.arange(2, dtype=jnp.int32)
    tbl, seq, cnt, sq = key_tables(span_order, doc_ends, query_spans)
    qpos_col = places.astype(jnp.int32)[:, None]
    qstart_col = query_start.astype(jnp.int32)[:, None]
    m0, l0, acc0 = diagonal_attention(sq, query_rows, qpos_col, qstart_col, kv_pair)
    attended = span_attention(
        tbl, seq, cnt, query_rows, qpos_col, qstart_col, gathered, m0, l0, acc0)
    partner_o = lax.ppermute(o_weight, ("yh", "ylo"), NEIGHBOUR)
    half = row_count // 2
    own_rows = lax.dynamic_slice_in_dim(attended, plane * half, half, 0)
    other_rows = lax.dynamic_slice_in_dim(attended, (1 - plane) * half, half, 0)
    partner_rows = lax.ppermute(other_rows, "yh", [(0, 1), (1, 0)])
    mixed = jnp.dot(
        jnp.concatenate([own_rows, partner_rows], axis=1),
        jnp.concatenate([o_weight, partner_o], axis=0),
        preferred_element_type=jnp.float32,
    ).astype(jnp.bfloat16)
    mixed_rows = reduce_scatter_x(mixed)
    return mixed_rows.reshape(tokens.shape)


TENSOR = ("yh", "x")
NEIGHBOUR = [(0, 3), (3, 0), (1, 2), (2, 1)]
CONTEXT = ("z", "ylo", "core")


def solution(mesh):
    devices = mesh.devices.reshape(2, mesh.devices.shape[0] // 2, -1, 2, 2)
    split_mesh = jax.sharding.Mesh(devices, ("yh", "x", "z", "ylo", "core"))
    in_specs = (
        P(CONTEXT, TENSOR, None),
        P(),
        P(None, TENSOR),
        P(None, TENSOR),
        P(None, TENSOR),
        P(TENSOR, None),
        P(),
        P(),
    )
    out_specs = P(CONTEXT, TENSOR, None)
    return jax.shard_map(
        per_device, mesh=split_mesh, in_specs=in_specs, out_specs=out_specs, check_vma=False
    )
```

```python
import functools
import math

import jax
import jax.numpy as jnp
from jax import lax
from jax.experimental import pallas as pl
from jax.experimental.pallas import tpu as pltpu
from jax.sharding import PartitionSpec as P

HEAD_DIM = 128
SPAN = 512
KEY_SLOTS = 9

rope_theta = 500000.0
epsilon = 1e-05
masked_score = -1e30


def positions(rows, span_order, span_rows):
    slot_ids = jnp.arange(span_order.shape[0], dtype=jnp.int32)
    matches = (rows // span_rows)[:, None] == slot_ids[None, :]
    picked = jnp.sum(jnp.where(matches, span_order[None, :], 0), axis=1)
    return picked * span_rows + rows % span_rows


def rotary(values, places):
    head_dim = values.shape[-1]
    half_dim = head_dim // 2
    frequency = rope_theta ** (-(2.0 / head_dim) * jnp.arange(half_dim, dtype=jnp.float32))
    angles = places.astype(jnp.float32)[:, None] * frequency[None, :]
    cosine = jnp.cos(angles)[:, None, :]
    sine_part = jnp.sin(angles)[:, None, :]
    first_half = values[..., :half_dim]
    second = values[..., half_dim:]
    return jnp.concatenate(
        [first_half * cosine - second * sine_part, second * cosine + first_half * sine_part],
        axis=-1,
    )


def online_update(heads, scale, q_ref, k_ref, v_ref, visible, m_sc, l_sc, acc_sc):
    k = k_ref[...]
    v = v_ref[...]
    for h in range(heads):
        q = q_ref[:, h * HEAD_DIM:(h + 1) * HEAD_DIM]
        s = lax.dot_general(q, k, (((1,), (1,)), ((), ())),
                            preferred_element_type=jnp.float32) * scale
        m_old = m_sc[h]
        if visible is None:
            m_new = jnp.maximum(m_old, jnp.max(s, axis=-1, keepdims=True))
            p = jnp.exp(s - m_new)
        else:
            m_new = jnp.maximum(
                m_old, jnp.max(jnp.where(visible, s, masked_score), axis=-1, keepdims=True))
            p = jnp.where(visible, jnp.exp(s - m_new), 0.0)
        alpha = jnp.exp(m_old - m_new)
        l_sc[h] = alpha * l_sc[h] + jnp.sum(p, axis=-1, keepdims=True)
        acc_sc[h] = alpha * acc_sc[h] + jnp.dot(
            p.astype(jnp.bfloat16), v, preferred_element_type=jnp.float32)
        m_sc[h] = m_new


def diagonal_kernel(heads, scale, sq_ref, q_ref, qpos_ref, qstart_ref, k_ref, v_ref,
                    m_ref, l_ref, acc_ref):
    i = pl.program_id(0)
    m_ref[...] = jnp.full_like(m_ref, masked_score)
    l_ref[...] = jnp.zeros_like(l_ref)
    acc_ref[...] = jnp.zeros_like(acc_ref)
    span = k_ref.shape[0]
    kpos = sq_ref[i] * span + lax.broadcasted_iota(jnp.int32, (1, span), 1)
    visible = (kpos <= qpos_ref[...]) & (kpos >= qstart_ref[...])
    online_update(heads, scale, q_ref, k_ref, v_ref, visible, m_ref, l_ref, acc_ref)


def attention_kernel(heads, scale, tbl_ref, seq_ref, cnt_ref, full_ref, q_ref, qpos_ref, qstart_ref,
                     k_ref, v_ref, m_in, l_in, acc_in, o_ref, m_sc, l_sc, acc_sc):
    i = pl.program_id(0)
    j = pl.program_id(1)

    @pl.when(j == 0)
    def _():
        m_sc[...] = m_in[...]
        l_sc[...] = l_in[...]
        acc_sc[...] = acc_in[...]

    live = j < cnt_ref[i]
    full = full_ref[i, j] == 1

    @pl.when(live & full)
    def _():
        online_update(heads, scale, q_ref, k_ref, v_ref, None, m_sc, l_sc, acc_sc)

    @pl.when(live & jnp.logical_not(full))
    def _():
        span = k_ref.shape[0]
        kpos = seq_ref[i, j] * span + lax.broadcasted_iota(jnp.int32, (1, span), 1)
        visible = (kpos <= qpos_ref[...]) & (kpos >= qstart_ref[...])
        online_update(heads, scale, q_ref, k_ref, v_ref, visible, m_sc, l_sc, acc_sc)

    @pl.when(j == pl.num_programs(1) - 1)
    def _():
        for h in range(heads):
            o_ref[:, h * HEAD_DIM:(h + 1) * HEAD_DIM] = (acc_sc[h] / l_sc[h]).astype(o_ref.dtype)


def diagonal_attention(sq, queries, qpos, qstart, local_kv):
    rows, q_cols = queries.shape
    heads = q_cols // HEAD_DIM
    n_q = rows // SPAN
    kernel = functools.partial(diagonal_kernel, heads, 1.0 / math.sqrt(HEAD_DIM))
    state = lambda w: pl.BlockSpec((None, heads, SPAN, w), lambda i, s: (i, 0, 0, 0))
    cost = pl.CostEstimate(
        flops=4 * n_q * heads * SPAN * SPAN * HEAD_DIM,
        transcendentals=n_q * heads * SPAN * SPAN,
        bytes_accessed=2 * rows * q_cols + 4 * rows * HEAD_DIM + 4 * n_q * heads * SPAN * 130,
    )
    return pl.pallas_call(
        kernel,
        out_shape=(
            jax.ShapeDtypeStruct((n_q, heads, SPAN, 1), jnp.float32),
            jax.ShapeDtypeStruct((n_q, heads, SPAN, 1), jnp.float32),
            jax.ShapeDtypeStruct((n_q, heads, SPAN, HEAD_DIM), jnp.float32),
        ),
        grid_spec=pltpu.PrefetchScalarGridSpec(
            num_scalar_prefetch=1,
            grid=(n_q,),
            in_specs=[
                pl.BlockSpec((SPAN, q_cols), lambda i, s: (i, 0)),
                pl.BlockSpec((SPAN, 1), lambda i, s: (i, 0)),
                pl.BlockSpec((SPAN, 1), lambda i, s: (i, 0)),
                pl.BlockSpec((None, SPAN, HEAD_DIM), lambda i, s: (0, i, 0)),
                pl.BlockSpec((None, SPAN, HEAD_DIM), lambda i, s: (1, i, 0)),
            ],
            out_specs=[state(1), state(1), state(HEAD_DIM)],
        ),
        compiler_params=pltpu.CompilerParams(dimension_semantics=("arbitrary",)),
        cost_estimate=cost,
    )(sq, queries, qpos, qstart, local_kv, local_kv)


def span_attention(tbl, seq, cnt, full, queries, qpos, qstart, kv, m0, l0, acc0):
    rows, q_cols = queries.shape
    heads = q_cols // HEAD_DIM
    n_q = rows // SPAN
    slots = tbl.shape[1]
    kernel = functools.partial(attention_kernel, heads, 1.0 / math.sqrt(HEAD_DIM))
    steps = n_q * slots
    state = lambda w: pl.BlockSpec((None, heads, SPAN, w), lambda i, j, t, s, c, f: (i, 0, 0, 0))
    cost = pl.CostEstimate(
        flops=4 * steps * heads * SPAN * SPAN * HEAD_DIM,
        transcendentals=steps * heads * SPAN * SPAN,
        bytes_accessed=steps * 2 * SPAN * HEAD_DIM * 2 + 2 * rows * q_cols * 2,
    )
    return pl.pallas_call(
        kernel,
        out_shape=jax.ShapeDtypeStruct((rows, q_cols), jnp.bfloat16),
        grid_spec=pltpu.PrefetchScalarGridSpec(
            num_scalar_prefetch=4,
            grid=(n_q, slots),
            in_specs=[
                pl.BlockSpec((SPAN, q_cols), lambda i, j, t, s, c, f: (i, 0)),
                pl.BlockSpec((SPAN, 1), lambda i, j, t, s, c, f: (i, 0)),
                pl.BlockSpec((SPAN, 1), lambda i, j, t, s, c, f: (i, 0)),
                pl.BlockSpec((None, SPAN, HEAD_DIM), lambda i, j, t, s, c, f: (0, t[i, j], 0)),
                pl.BlockSpec((None, SPAN, HEAD_DIM), lambda i, j, t, s, c, f: (1, t[i, j], 0)),
                state(1), state(1), state(HEAD_DIM),
            ],
            out_specs=pl.BlockSpec((SPAN, q_cols), lambda i, j, t, s, c, f: (i, 0)),
            scratch_shapes=[
                pltpu.VMEM((heads, SPAN, 1), jnp.float32),
                pltpu.VMEM((heads, SPAN, 1), jnp.float32),
                pltpu.VMEM((heads, SPAN, HEAD_DIM), jnp.float32),
            ],
        ),
        compiler_params=pltpu.CompilerParams(dimension_semantics=("arbitrary", "arbitrary")),
        cost_estimate=cost,
    )(tbl, seq, cnt, full, queries, qpos, qstart, kv, kv, m0, l0, acc0)


def key_tables(span_order, doc_ends, query_spans):
    n_spans = span_order.shape[0]
    span_ids = jnp.arange(n_spans, dtype=jnp.int32)
    inverse = jnp.sum(
        jnp.where(span_order[None, :] == span_ids[:, None], span_ids[None, :], 0), axis=1)
    first_doc = jnp.sum((doc_ends[None, :] <= (span_ids * SPAN)[:, None]).astype(jnp.int32), axis=1)
    last_doc = jnp.sum(
        (doc_ends[None, :] <= (span_ids * SPAN + SPAN - 1)[:, None]).astype(jnp.int32), axis=1)
    sq = jnp.sum(jnp.where(query_spans[:, None] == span_ids[None, :], span_order[None, :], 0), axis=1)
    q_first = jnp.sum(jnp.where(sq[:, None] == span_ids[None, :], first_doc[None, :], 0), axis=1)
    back = jnp.arange(KEY_SLOTS, dtype=jnp.int32) - (KEY_SLOTS - 1)
    cand = sq[:, None] + back[None, :]
    cand_last = jnp.sum(
        jnp.where(cand[:, :, None] == span_ids[None, None, :], last_doc[None, None, :], 0), axis=2)
    valid = (cand >= 0) & (cand_last >= q_first[:, None])
    count = jnp.sum(valid.astype(jnp.int32), axis=1)
    before = count - 1
    slot = jnp.arange(KEY_SLOTS - 1, dtype=jnp.int32)
    last = jnp.maximum(sq - 1, 0)
    seq = jnp.clip(sq[:, None] - before[:, None] + slot[None, :], 0, last[:, None])
    tbl = jnp.sum(jnp.where(seq[:, :, None] == span_ids[None, None, :], inverse[None, None, :], 0),
                  axis=2)
    last_start = jnp.max(
        jnp.where(doc_ends[None, :] <= (sq * SPAN + SPAN - 1)[:, None], doc_ends[None, :], 0), axis=1)
    full = (seq < sq[:, None]) & (seq * SPAN >= last_start[:, None])
    return (tbl.astype(jnp.int32), seq.astype(jnp.int32), before.astype(jnp.int32),
            sq.astype(jnp.int32), full.astype(jnp.int32))


def shift_x(value, d, n):
    return lax.ppermute(value, "x", [(i, (i + d) % n) for i in range(n)])


def reduce_scatter_x(value):
    n = lax.axis_size("x")
    me = lax.axis_index("x")
    parts = value.reshape(n, value.shape[0] // n, *value.shape[1:])
    total = jnp.take(parts, me, axis=0).astype(jnp.float32)
    for d in range(1, n):
        total = total + shift_x(jnp.take(parts, (me + d) % n, axis=0), d, n).astype(jnp.float32)
    return total.astype(value.dtype)


def per_device(tokens, norm_gain, q_weight, k_weight, v_weight, o_weight, doc_lengths, span_order):
    local_rows = tokens.shape[1]
    tok_dev = local_rows * lax.axis_size(TENSOR)
    model_width = tokens.shape[2]
    head_dim = HEAD_DIM
    q_cols = q_weight.shape[1]
    kv_cols = k_weight.shape[1]
    q_heads = q_cols // head_dim
    kv_local = kv_cols // head_dim
    span_rows = tok_dev // 2
    base_row = lax.axis_index(CONTEXT) * tok_dev
    rows_float = tokens.astype(jnp.float32)
    normed = (
        rows_float
        * lax.rsqrt(jnp.mean(rows_float * rows_float, axis=-1, keepdims=True) + epsilon)
        * norm_gain
    ).astype(jnp.bfloat16)
    plane = lax.axis_index("yh")
    core = lax.axis_index("core")
    weights = jnp.concatenate([q_weight, k_weight, v_weight], axis=1)
    half_in = weights.shape[0] // 2
    sent_half = lax.dynamic_slice_in_dim(weights, core * half_in, half_in, 0)
    plane_rows = lax.all_gather(normed, "x", axis=1, tiled=True)
    partner_half = lax.ppermute(sent_half, ("yh", "ylo"), NEIGHBOUR)
    plane_rows, partner_half = lax.optimization_barrier((plane_rows, partner_half))
    other_half = lax.ppermute(partner_half, "core", [(0, 1), (1, 0)])
    half = plane_rows.shape[1]
    flat_rows = plane_rows.reshape(half, model_width)
    all_places = positions(base_row + jnp.arange(tok_dev, dtype=jnp.int32), span_order, span_rows)
    places = lax.dynamic_slice_in_dim(all_places, plane * half, half, 0)
    rows_mine = lax.dynamic_slice_in_dim(flat_rows, core * half_in, half_in, 1)
    rows_other = lax.dynamic_slice_in_dim(flat_rows, (1 - core) * half_in, half_in, 1)

    def finish(out):
        q = rotary(out[:, :q_cols].reshape(half, q_heads, head_dim), places)
        k = rotary(out[:, q_cols:q_cols + kv_cols].reshape(half, kv_local, head_dim), places)
        return jnp.concatenate(
            [q.reshape(half, q_cols), k.reshape(half, kv_cols), out[:, q_cols + kv_cols:]], axis=1
        ).astype(jnp.bfloat16)

    def project(w):
        return finish(jnp.dot(flat_rows, w, preferred_element_type=jnp.float32))

    for_partner = finish(
        jnp.dot(rows_mine, partner_half, preferred_element_type=jnp.float32)
        + jnp.dot(rows_other, other_half, preferred_element_type=jnp.float32))
    received = lax.ppermute(for_partner, "yh", [(0, 1), (1, 0)])
    flat_rows, for_partner = lax.optimization_barrier((flat_rows, for_partner))
    own = project(weights)
    first = jnp.where(plane == 0, own, received)
    second = jnp.where(plane == 0, received, own)
    projected = jnp.concatenate([first, second], axis=0)
    query_rows = projected[:, :q_cols]
    kv_pair = jnp.stack([projected[:, q_cols:q_cols + kv_cols], projected[:, q_cols + kv_cols:]])
    gathered = lax.all_gather(kv_pair, CONTEXT, axis=1, tiled=True)
    places = all_places
    row_count = tok_dev

    doc_ends = jnp.cumsum(doc_lengths)
    query_start = jnp.max(
        jnp.where(doc_ends[None, :] <= places[:, None], doc_ends[None, :], 0), axis=1)
    query_spans = lax.axis_index(CONTEXT) * 2 + jnp.arange(2, dtype=jnp.int32)
    tbl, seq, cnt, sq, full = key_tables(span_order, doc_ends, query_spans)
    qpos_col = places.astype(jnp.int32)[:, None]
    qstart_col = query_start.astype(jnp.int32)[:, None]
    m0, l0, acc0 = diagonal_attention(sq, query_rows, qpos_col, qstart_col, kv_pair)
    attended = span_attention(
        tbl, seq, cnt, full, query_rows, qpos_col, qstart_col, gathered, m0, l0, acc0)
    partner_o = lax.ppermute(o_weight, ("yh", "ylo"), NEIGHBOUR)
    half = row_count // 2
    own_rows = lax.dynamic_slice_in_dim(attended, plane * half, half, 0)
    other_rows = lax.dynamic_slice_in_dim(attended, (1 - plane) * half, half, 0)
    partner_rows = lax.ppermute(other_rows, "yh", [(0, 1), (1, 0)])
    mixed = jnp.dot(
        jnp.concatenate([own_rows, partner_rows], axis=1),
        jnp.concatenate([o_weight, partner_o], axis=0),
        preferred_element_type=jnp.float32,
    ).astype(jnp.bfloat16)
    mixed_rows = reduce_scatter_x(mixed)
    return mixed_rows.reshape(tokens.shape)


TENSOR = ("yh", "x")
NEIGHBOUR = [(0, 3), (3, 0), (1, 2), (2, 1)]
CONTEXT = ("z", "ylo", "core")


def solution(mesh):
    devices = mesh.devices.reshape(2, mesh.devices.shape[0] // 2, -1, 2, 2)
    split_mesh = jax.sharding.Mesh(devices, ("yh", "x", "z", "ylo", "core"))
    in_specs = (
        P(CONTEXT, TENSOR, None),
        P(),
        P(None, TENSOR),
        P(None, TENSOR),
        P(None, TENSOR),
        P(TENSOR, None),
        P(),
        P(),
    )
    out_specs = P(CONTEXT, TENSOR, None)
    return jax.shard_map(
        per_device, mesh=split_mesh, in_specs=in_specs, out_specs=out_specs, check_vma=False
    )
```

```python
import functools
import math

import jax
import jax.numpy as jnp
from jax import lax
from jax.experimental import pallas as pl
from jax.experimental.pallas import tpu as pltpu
from jax.sharding import PartitionSpec as P

HEAD_DIM = 128
SPAN = 512
KEY_SLOTS = 9

rope_theta = 500000.0
epsilon = 1e-05
masked_score = -1e30


def positions(rows, span_order, span_rows):
    slot_ids = jnp.arange(span_order.shape[0], dtype=jnp.int32)
    matches = (rows // span_rows)[:, None] == slot_ids[None, :]
    picked = jnp.sum(jnp.where(matches, span_order[None, :], 0), axis=1)
    return picked * span_rows + rows % span_rows


def rotary(values, places):
    head_dim = values.shape[-1]
    half_dim = head_dim // 2
    frequency = rope_theta ** (-(2.0 / head_dim) * jnp.arange(half_dim, dtype=jnp.float32))
    angles = places.astype(jnp.float32)[:, None] * frequency[None, :]
    cosine = jnp.cos(angles)[:, None, :]
    sine_part = jnp.sin(angles)[:, None, :]
    first_half = values[..., :half_dim]
    second = values[..., half_dim:]
    return jnp.concatenate(
        [first_half * cosine - second * sine_part, second * cosine + first_half * sine_part],
        axis=-1,
    )


def online_update(heads, scale, q_ref, k_ref, v_ref, visible, m_sc, l_sc, acc_sc):
    k = k_ref[...]
    v = v_ref[...]
    for h in range(heads):
        q = q_ref[:, h * HEAD_DIM:(h + 1) * HEAD_DIM]
        s = lax.dot_general(q, k, (((1,), (1,)), ((), ())),
                            preferred_element_type=jnp.float32) * scale
        m_old = m_sc[h]
        if visible is None:
            m_new = jnp.maximum(m_old, jnp.max(s, axis=-1, keepdims=True))
            p = jnp.exp(s - m_new)
        else:
            m_new = jnp.maximum(
                m_old, jnp.max(jnp.where(visible, s, masked_score), axis=-1, keepdims=True))
            p = jnp.where(visible, jnp.exp(s - m_new), 0.0)
        alpha = jnp.exp(m_old - m_new)
        l_sc[h] = alpha * l_sc[h] + jnp.sum(p, axis=-1, keepdims=True)
        acc_sc[h] = alpha * acc_sc[h] + jnp.dot(
            p.astype(jnp.bfloat16), v, preferred_element_type=jnp.float32)
        m_sc[h] = m_new


def diagonal_kernel(heads, scale, sq_ref, q_ref, qpos_ref, qstart_ref, k_ref, v_ref,
                    m_ref, l_ref, acc_ref):
    i = pl.program_id(0)
    m_ref[...] = jnp.full_like(m_ref, masked_score)
    l_ref[...] = jnp.zeros_like(l_ref)
    acc_ref[...] = jnp.zeros_like(acc_ref)
    span = k_ref.shape[0]
    kpos = sq_ref[i] * span + lax.broadcasted_iota(jnp.int32, (1, span), 1)
    visible = (kpos <= qpos_ref[...]) & (kpos >= qstart_ref[...])
    online_update(heads, scale, q_ref, k_ref, v_ref, visible, m_ref, l_ref, acc_ref)


def attention_kernel(heads, scale, tbl_ref, seq_ref, cnt_ref, full_ref, q_ref, qpos_ref, qstart_ref,
                     k_ref, v_ref, m_in, l_in, acc_in, o_ref, m_sc, l_sc, acc_sc):
    i = pl.program_id(0)
    j = pl.program_id(1)

    @pl.when(j == 0)
    def _():
        m_sc[...] = m_in[...]
        l_sc[...] = l_in[...]
        acc_sc[...] = acc_in[...]

    live = j < cnt_ref[i]
    full = full_ref[i, j] == 1

    @pl.when(live & full)
    def _():
        online_update(heads, scale, q_ref, k_ref, v_ref, None, m_sc, l_sc, acc_sc)

    @pl.when(live & jnp.logical_not(full))
    def _():
        span = k_ref.shape[0]
        kpos = seq_ref[i, j] * span + lax.broadcasted_iota(jnp.int32, (1, span), 1)
        visible = (kpos <= qpos_ref[...]) & (kpos >= qstart_ref[...])
        online_update(heads, scale, q_ref, k_ref, v_ref, visible, m_sc, l_sc, acc_sc)

    @pl.when(j == pl.num_programs(1) - 1)
    def _():
        for h in range(heads):
            o_ref[:, h * HEAD_DIM:(h + 1) * HEAD_DIM] = (acc_sc[h] / l_sc[h]).astype(o_ref.dtype)


def diagonal_attention(sq, queries, qpos, qstart, local_kv):
    rows, q_cols = queries.shape
    heads = q_cols // HEAD_DIM
    n_q = rows // SPAN
    kernel = functools.partial(diagonal_kernel, heads, 1.0 / math.sqrt(HEAD_DIM))
    state = lambda w: pl.BlockSpec((None, heads, SPAN, w), lambda i, s: (i, 0, 0, 0))
    cost = pl.CostEstimate(
        flops=4 * n_q * heads * SPAN * SPAN * HEAD_DIM,
        transcendentals=n_q * heads * SPAN * SPAN,
        bytes_accessed=2 * rows * q_cols + 4 * rows * HEAD_DIM + 4 * n_q * heads * SPAN * 130,
    )
    return pl.pallas_call(
        kernel,
        out_shape=(
            jax.ShapeDtypeStruct((n_q, heads, SPAN, 1), jnp.float32),
            jax.ShapeDtypeStruct((n_q, heads, SPAN, 1), jnp.float32),
            jax.ShapeDtypeStruct((n_q, heads, SPAN, HEAD_DIM), jnp.float32),
        ),
        grid_spec=pltpu.PrefetchScalarGridSpec(
            num_scalar_prefetch=1,
            grid=(n_q,),
            in_specs=[
                pl.BlockSpec((SPAN, q_cols), lambda i, s: (i, 0)),
                pl.BlockSpec((SPAN, 1), lambda i, s: (i, 0)),
                pl.BlockSpec((SPAN, 1), lambda i, s: (i, 0)),
                pl.BlockSpec((None, SPAN, HEAD_DIM), lambda i, s: (0, i, 0)),
                pl.BlockSpec((None, SPAN, HEAD_DIM), lambda i, s: (1, i, 0)),
            ],
            out_specs=[state(1), state(1), state(HEAD_DIM)],
        ),
        compiler_params=pltpu.CompilerParams(dimension_semantics=("arbitrary",)),
        cost_estimate=cost,
    )(sq, queries, qpos, qstart, local_kv, local_kv)


def span_attention(tbl, seq, cnt, full, queries, qpos, qstart, kv, m0, l0, acc0):
    rows, q_cols = queries.shape
    heads = q_cols // HEAD_DIM
    n_q = rows // SPAN
    slots = tbl.shape[1]
    kernel = functools.partial(attention_kernel, heads, 1.0 / math.sqrt(HEAD_DIM))
    steps = n_q * slots
    state = lambda w: pl.BlockSpec((None, heads, SPAN, w), lambda i, j, t, s, c, f: (i, 0, 0, 0))
    cost = pl.CostEstimate(
        flops=4 * steps * heads * SPAN * SPAN * HEAD_DIM,
        transcendentals=steps * heads * SPAN * SPAN,
        bytes_accessed=steps * 2 * SPAN * HEAD_DIM * 2 + 2 * rows * q_cols * 2,
    )
    return pl.pallas_call(
        kernel,
        out_shape=jax.ShapeDtypeStruct((rows, q_cols), jnp.bfloat16),
        grid_spec=pltpu.PrefetchScalarGridSpec(
            num_scalar_prefetch=4,
            grid=(n_q, slots),
            in_specs=[
                pl.BlockSpec((SPAN, q_cols), lambda i, j, t, s, c, f: (i, 0)),
                pl.BlockSpec((SPAN, 1), lambda i, j, t, s, c, f: (i, 0)),
                pl.BlockSpec((SPAN, 1), lambda i, j, t, s, c, f: (i, 0)),
                pl.BlockSpec((None, SPAN, HEAD_DIM), lambda i, j, t, s, c, f: (0, t[i, j], 0)),
                pl.BlockSpec((None, SPAN, HEAD_DIM), lambda i, j, t, s, c, f: (1, t[i, j], 0)),
                state(1), state(1), state(HEAD_DIM),
            ],
            out_specs=pl.BlockSpec((SPAN, q_cols), lambda i, j, t, s, c, f: (i, 0)),
            scratch_shapes=[
                pltpu.VMEM((heads, SPAN, 1), jnp.float32),
                pltpu.VMEM((heads, SPAN, 1), jnp.float32),
                pltpu.VMEM((heads, SPAN, HEAD_DIM), jnp.float32),
            ],
        ),
        compiler_params=pltpu.CompilerParams(dimension_semantics=("arbitrary", "arbitrary")),
        cost_estimate=cost,
    )(tbl, seq, cnt, full, queries, qpos, qstart, kv, kv, m0, l0, acc0)


def key_tables(span_order, doc_ends, query_spans):
    n_spans = span_order.shape[0]
    span_ids = jnp.arange(n_spans, dtype=jnp.int32)
    inverse = jnp.sum(
        jnp.where(span_order[None, :] == span_ids[:, None], span_ids[None, :], 0), axis=1)
    first_doc = jnp.sum((doc_ends[None, :] <= (span_ids * SPAN)[:, None]).astype(jnp.int32), axis=1)
    last_doc = jnp.sum(
        (doc_ends[None, :] <= (span_ids * SPAN + SPAN - 1)[:, None]).astype(jnp.int32), axis=1)
    sq = jnp.sum(jnp.where(query_spans[:, None] == span_ids[None, :], span_order[None, :], 0), axis=1)
    q_first = jnp.sum(jnp.where(sq[:, None] == span_ids[None, :], first_doc[None, :], 0), axis=1)
    back = jnp.arange(KEY_SLOTS, dtype=jnp.int32) - (KEY_SLOTS - 1)
    cand = sq[:, None] + back[None, :]
    cand_last = jnp.sum(
        jnp.where(cand[:, :, None] == span_ids[None, None, :], last_doc[None, None, :], 0), axis=2)
    valid = (cand >= 0) & (cand_last >= q_first[:, None])
    count = jnp.sum(valid.astype(jnp.int32), axis=1)
    before = count - 1
    slot = jnp.arange(KEY_SLOTS - 1, dtype=jnp.int32)
    last = jnp.maximum(sq - 1, 0)
    seq = jnp.clip(sq[:, None] - before[:, None] + slot[None, :], 0, last[:, None])
    tbl = jnp.sum(jnp.where(seq[:, :, None] == span_ids[None, None, :], inverse[None, None, :], 0),
                  axis=2)
    last_start = jnp.max(
        jnp.where(doc_ends[None, :] <= (sq * SPAN + SPAN - 1)[:, None], doc_ends[None, :], 0), axis=1)
    full = (seq < sq[:, None]) & (seq * SPAN >= last_start[:, None])
    return (tbl.astype(jnp.int32), seq.astype(jnp.int32), before.astype(jnp.int32),
            sq.astype(jnp.int32), full.astype(jnp.int32))


def shift_x(value, d, n):
    return lax.ppermute(value, "x", [(i, (i + d) % n) for i in range(n)])


def reduce_scatter_x(value):
    n = lax.axis_size("x")
    me = lax.axis_index("x")
    parts = value.reshape(n, value.shape[0] // n, *value.shape[1:])
    total = jnp.take(parts, me, axis=0).astype(jnp.float32)
    for d in range(1, n):
        total = total + shift_x(jnp.take(parts, (me + d) % n, axis=0), d, n).astype(jnp.float32)
    return total.astype(value.dtype)


def per_device(tokens, norm_gain, q_weight, k_weight, v_weight, o_weight, doc_lengths, span_order):
    local_rows = tokens.shape[1]
    tok_dev = local_rows * lax.axis_size(TENSOR)
    model_width = tokens.shape[2]
    head_dim = HEAD_DIM
    q_cols = q_weight.shape[1]
    kv_cols = k_weight.shape[1]
    q_heads = q_cols // head_dim
    kv_local = kv_cols // head_dim
    span_rows = tok_dev // 2
    base_row = lax.axis_index(CONTEXT) * tok_dev
    rows_float = tokens.astype(jnp.float32)
    normed = (
        rows_float
        * lax.rsqrt(jnp.mean(rows_float * rows_float, axis=-1, keepdims=True) + epsilon)
        * norm_gain
    ).astype(jnp.bfloat16)
    plane = lax.axis_index("yh")
    core = lax.axis_index("core")
    weights = jnp.concatenate([q_weight, k_weight, v_weight], axis=1)
    half_in = weights.shape[0] // 2
    sent_half = lax.dynamic_slice_in_dim(weights, core * half_in, half_in, 0)
    plane_rows = lax.all_gather(normed, "x", axis=1, tiled=True)
    partner_half = lax.ppermute(sent_half, ("yh", "ylo"), NEIGHBOUR)
    plane_rows, partner_half = lax.optimization_barrier((plane_rows, partner_half))
    other_half = lax.ppermute(partner_half, "core", [(0, 1), (1, 0)])
    half = plane_rows.shape[1]
    flat_rows = plane_rows.reshape(half, model_width)
    all_places = positions(base_row + jnp.arange(tok_dev, dtype=jnp.int32), span_order, span_rows)
    places = lax.dynamic_slice_in_dim(all_places, plane * half, half, 0)
    rows_mine = lax.dynamic_slice_in_dim(flat_rows, core * half_in, half_in, 1)
    rows_other = lax.dynamic_slice_in_dim(flat_rows, (1 - core) * half_in, half_in, 1)

    def finish(out):
        q = rotary(out[:, :q_cols].reshape(half, q_heads, head_dim), places)
        k = rotary(out[:, q_cols:q_cols + kv_cols].reshape(half, kv_local, head_dim), places)
        return jnp.concatenate(
            [q.reshape(half, q_cols), k.reshape(half, kv_cols), out[:, q_cols + kv_cols:]], axis=1
        ).astype(jnp.bfloat16)

    def project(w):
        return finish(jnp.dot(flat_rows, w, preferred_element_type=jnp.float32))

    for_partner = finish(
        jnp.dot(rows_mine, partner_half, preferred_element_type=jnp.float32)
        + jnp.dot(rows_other, other_half, preferred_element_type=jnp.float32))
    received = lax.ppermute(for_partner, "yh", [(0, 1), (1, 0)])
    flat_rows, for_partner = lax.optimization_barrier((flat_rows, for_partner))
    own = project(weights)
    first = jnp.where(plane == 0, own, received)
    second = jnp.where(plane == 0, received, own)
    projected = jnp.concatenate([first, second], axis=0)
    query_rows = projected[:, :q_cols]
    kv_pair = jnp.stack([projected[:, q_cols:q_cols + kv_cols], projected[:, q_cols + kv_cols:]])
    gathered = lax.all_gather(kv_pair, CONTEXT, axis=1, tiled=True)
    places = all_places
    row_count = tok_dev

    doc_ends = jnp.cumsum(doc_lengths)
    query_start = jnp.max(
        jnp.where(doc_ends[None, :] <= places[:, None], doc_ends[None, :], 0), axis=1)
    query_spans = lax.axis_index(CONTEXT) * 2 + jnp.arange(2, dtype=jnp.int32)
    tbl, seq, cnt, sq, full = key_tables(span_order, doc_ends, query_spans)
    qpos_col = places.astype(jnp.int32)[:, None]
    qstart_col = query_start.astype(jnp.int32)[:, None]
    m0, l0, acc0 = diagonal_attention(sq, query_rows, qpos_col, qstart_col, kv_pair)
    attended = span_attention(
        tbl, seq, cnt, full, query_rows, qpos_col, qstart_col, gathered, m0, l0, acc0)
    partner_o = lax.ppermute(o_weight, ("yh", "ylo"), NEIGHBOUR)
    half = row_count // 2
    own_rows = lax.dynamic_slice_in_dim(attended, plane * half, half, 0)
    other_rows = lax.dynamic_slice_in_dim(attended, (1 - plane) * half, half, 0)
    partner_rows = lax.ppermute(other_rows, "yh", [(0, 1), (1, 0)])
    mixed = (
        jnp.dot(own_rows, o_weight, preferred_element_type=jnp.float32)
        + jnp.dot(partner_rows, partner_o, preferred_element_type=jnp.float32)
    ).astype(jnp.bfloat16)
    mixed_rows = reduce_scatter_x(mixed)
    return mixed_rows.reshape(tokens.shape)


TENSOR = ("yh", "x")
NEIGHBOUR = [(0, 3), (3, 0), (1, 2), (2, 1)]
CONTEXT = ("z", "ylo", "core")


def solution(mesh):
    devices = mesh.devices.reshape(2, mesh.devices.shape[0] // 2, -1, 2, 2)
    split_mesh = jax.sharding.Mesh(devices, ("yh", "x", "z", "ylo", "core"))
    in_specs = (
        P(CONTEXT, TENSOR, None),
        P(),
        P(None, TENSOR),
        P(None, TENSOR),
        P(None, TENSOR),
        P(TENSOR, None),
        P(),
        P(),
    )
    out_specs = P(CONTEXT, TENSOR, None)
    return jax.shard_map(
        per_device, mesh=split_mesh, in_specs=in_specs, out_specs=out_specs, check_vma=False
    )
```

```python
import functools
import math

import jax
import jax.numpy as jnp
from jax import lax
from jax.experimental import pallas as pl
from jax.experimental.pallas import tpu as pltpu
from jax.sharding import PartitionSpec as P

HEAD_DIM = 128
SPAN = 512
KEY_SLOTS = 9

rope_theta = 500000.0
epsilon = 1e-05
masked_score = -1e30


def positions(rows, span_order, span_rows):
    slot_ids = jnp.arange(span_order.shape[0], dtype=jnp.int32)
    matches = (rows // span_rows)[:, None] == slot_ids[None, :]
    picked = jnp.sum(jnp.where(matches, span_order[None, :], 0), axis=1)
    return picked * span_rows + rows % span_rows


def rotary(values, places):
    head_dim = values.shape[-1]
    half_dim = head_dim // 2
    frequency = rope_theta ** (-(2.0 / head_dim) * jnp.arange(half_dim, dtype=jnp.float32))
    angles = places.astype(jnp.float32)[:, None] * frequency[None, :]
    cosine = jnp.cos(angles)[:, None, :]
    sine_part = jnp.sin(angles)[:, None, :]
    first_half = values[..., :half_dim]
    second = values[..., half_dim:]
    return jnp.concatenate(
        [first_half * cosine - second * sine_part, second * cosine + first_half * sine_part],
        axis=-1,
    )


def online_update(heads, scale, q_ref, k_ref, v_ref, visible, m_sc, l_sc, acc_sc):
    k = k_ref[...]
    v = v_ref[...]
    for h in range(heads):
        q = q_ref[:, h * HEAD_DIM:(h + 1) * HEAD_DIM]
        s = lax.dot_general(q, k, (((1,), (1,)), ((), ())),
                            preferred_element_type=jnp.float32) * scale
        m_old = m_sc[h]
        if visible is None:
            m_new = jnp.maximum(m_old, jnp.max(s, axis=-1, keepdims=True))
            p = jnp.exp(s - m_new)
        else:
            m_new = jnp.maximum(
                m_old, jnp.max(jnp.where(visible, s, masked_score), axis=-1, keepdims=True))
            p = jnp.where(visible, jnp.exp(s - m_new), 0.0)
        alpha = jnp.exp(m_old - m_new)
        l_sc[h] = alpha * l_sc[h] + jnp.sum(p, axis=-1, keepdims=True)
        acc_sc[h] = alpha * acc_sc[h] + jnp.dot(
            p.astype(jnp.bfloat16), v, preferred_element_type=jnp.float32)
        m_sc[h] = m_new


def diagonal_kernel(heads, scale, sq_ref, q_ref, qpos_ref, qstart_ref, k_ref, v_ref,
                    m_ref, l_ref, acc_ref):
    i = pl.program_id(0)
    m_ref[...] = jnp.full_like(m_ref, masked_score)
    l_ref[...] = jnp.zeros_like(l_ref)
    acc_ref[...] = jnp.zeros_like(acc_ref)
    span = k_ref.shape[0]
    kpos = sq_ref[i] * span + lax.broadcasted_iota(jnp.int32, (1, span), 1)
    visible = (kpos <= qpos_ref[...]) & (kpos >= qstart_ref[...])
    online_update(heads, scale, q_ref, k_ref, v_ref, visible, m_ref, l_ref, acc_ref)


def attention_kernel(heads, scale, tbl_ref, seq_ref, cnt_ref, full_ref, q_ref, qpos_ref, qstart_ref,
                     k_ref, v_ref, m_in, l_in, acc_in, o_ref, m_sc, l_sc, acc_sc):
    i = pl.program_id(0)
    j = pl.program_id(1)

    @pl.when(j == 0)
    def _():
        m_sc[...] = m_in[...]
        l_sc[...] = l_in[...]
        acc_sc[...] = acc_in[...]

    live = j < cnt_ref[i]
    full = full_ref[i, j] == 1

    @pl.when(live & full)
    def _():
        online_update(heads, scale, q_ref, k_ref, v_ref, None, m_sc, l_sc, acc_sc)

    @pl.when(live & jnp.logical_not(full))
    def _():
        span = k_ref.shape[0]
        kpos = seq_ref[i, j] * span + lax.broadcasted_iota(jnp.int32, (1, span), 1)
        visible = (kpos <= qpos_ref[...]) & (kpos >= qstart_ref[...])
        online_update(heads, scale, q_ref, k_ref, v_ref, visible, m_sc, l_sc, acc_sc)

    @pl.when(j == pl.num_programs(1) - 1)
    def _():
        for h in range(heads):
            o_ref[:, h * HEAD_DIM:(h + 1) * HEAD_DIM] = (acc_sc[h] / l_sc[h]).astype(o_ref.dtype)


def diagonal_attention(sq, queries, qpos, qstart, local_kv):
    rows, q_cols = queries.shape
    heads = q_cols // HEAD_DIM
    n_q = rows // SPAN
    kernel = functools.partial(diagonal_kernel, heads, 1.0 / math.sqrt(HEAD_DIM))
    state = lambda w: pl.BlockSpec((None, heads, SPAN, w), lambda i, s: (i, 0, 0, 0))
    cost = pl.CostEstimate(
        flops=4 * n_q * heads * SPAN * SPAN * HEAD_DIM,
        transcendentals=n_q * heads * SPAN * SPAN,
        bytes_accessed=2 * rows * q_cols + 4 * rows * HEAD_DIM + 4 * n_q * heads * SPAN * 130,
    )
    return pl.pallas_call(
        kernel,
        out_shape=(
            jax.ShapeDtypeStruct((n_q, heads, SPAN, 1), jnp.float32),
            jax.ShapeDtypeStruct((n_q, heads, SPAN, 1), jnp.float32),
            jax.ShapeDtypeStruct((n_q, heads, SPAN, HEAD_DIM), jnp.float32),
        ),
        grid_spec=pltpu.PrefetchScalarGridSpec(
            num_scalar_prefetch=1,
            grid=(n_q,),
            in_specs=[
                pl.BlockSpec((SPAN, q_cols), lambda i, s: (i, 0)),
                pl.BlockSpec((SPAN, 1), lambda i, s: (i, 0)),
                pl.BlockSpec((SPAN, 1), lambda i, s: (i, 0)),
                pl.BlockSpec((None, SPAN, HEAD_DIM), lambda i, s: (0, i, 0)),
                pl.BlockSpec((None, SPAN, HEAD_DIM), lambda i, s: (1, i, 0)),
            ],
            out_specs=[state(1), state(1), state(HEAD_DIM)],
        ),
        compiler_params=pltpu.CompilerParams(dimension_semantics=("arbitrary",)),
        cost_estimate=cost,
    )(sq, queries, qpos, qstart, local_kv, local_kv)


def span_attention(tbl, seq, cnt, full, queries, qpos, qstart, kv, m0, l0, acc0):
    rows, q_cols = queries.shape
    heads = q_cols // HEAD_DIM
    n_q = rows // SPAN
    slots = tbl.shape[1]
    kernel = functools.partial(attention_kernel, heads, 1.0 / math.sqrt(HEAD_DIM))
    steps = n_q * slots
    state = lambda w: pl.BlockSpec((None, heads, SPAN, w), lambda i, j, t, s, c, f: (i, 0, 0, 0))
    cost = pl.CostEstimate(
        flops=4 * steps * heads * SPAN * SPAN * HEAD_DIM,
        transcendentals=steps * heads * SPAN * SPAN,
        bytes_accessed=steps * 2 * SPAN * HEAD_DIM * 2 + 2 * rows * q_cols * 2,
    )
    return pl.pallas_call(
        kernel,
        out_shape=jax.ShapeDtypeStruct((rows, q_cols), jnp.bfloat16),
        grid_spec=pltpu.PrefetchScalarGridSpec(
            num_scalar_prefetch=4,
            grid=(n_q, slots),
            in_specs=[
                pl.BlockSpec((SPAN, q_cols), lambda i, j, t, s, c, f: (i, 0)),
                pl.BlockSpec((SPAN, 1), lambda i, j, t, s, c, f: (i, 0)),
                pl.BlockSpec((SPAN, 1), lambda i, j, t, s, c, f: (i, 0)),
                pl.BlockSpec((None, SPAN, HEAD_DIM), lambda i, j, t, s, c, f: (0, t[i, j], 0)),
                pl.BlockSpec((None, SPAN, HEAD_DIM), lambda i, j, t, s, c, f: (1, t[i, j], 0)),
                state(1), state(1), state(HEAD_DIM),
            ],
            out_specs=pl.BlockSpec((SPAN, q_cols), lambda i, j, t, s, c, f: (i, 0)),
            scratch_shapes=[
                pltpu.VMEM((heads, SPAN, 1), jnp.float32),
                pltpu.VMEM((heads, SPAN, 1), jnp.float32),
                pltpu.VMEM((heads, SPAN, HEAD_DIM), jnp.float32),
            ],
        ),
        compiler_params=pltpu.CompilerParams(dimension_semantics=("arbitrary", "arbitrary")),
        cost_estimate=cost,
    )(tbl, seq, cnt, full, queries, qpos, qstart, kv, kv, m0, l0, acc0)


def key_tables(span_order, doc_ends, query_spans):
    n_spans = span_order.shape[0]
    span_ids = jnp.arange(n_spans, dtype=jnp.int32)
    inverse = jnp.sum(
        jnp.where(span_order[None, :] == span_ids[:, None], span_ids[None, :], 0), axis=1)
    first_doc = jnp.sum((doc_ends[None, :] <= (span_ids * SPAN)[:, None]).astype(jnp.int32), axis=1)
    last_doc = jnp.sum(
        (doc_ends[None, :] <= (span_ids * SPAN + SPAN - 1)[:, None]).astype(jnp.int32), axis=1)
    sq = jnp.sum(jnp.where(query_spans[:, None] == span_ids[None, :], span_order[None, :], 0), axis=1)
    q_first = jnp.sum(jnp.where(sq[:, None] == span_ids[None, :], first_doc[None, :], 0), axis=1)
    back = jnp.arange(KEY_SLOTS, dtype=jnp.int32) - (KEY_SLOTS - 1)
    cand = sq[:, None] + back[None, :]
    cand_last = jnp.sum(
        jnp.where(cand[:, :, None] == span_ids[None, None, :], last_doc[None, None, :], 0), axis=2)
    valid = (cand >= 0) & (cand_last >= q_first[:, None])
    count = jnp.sum(valid.astype(jnp.int32), axis=1)
    before = count - 1
    slot = jnp.arange(KEY_SLOTS - 1, dtype=jnp.int32)
    last = jnp.maximum(sq - 1, 0)
    seq = jnp.clip(sq[:, None] - before[:, None] + slot[None, :], 0, last[:, None])
    tbl = jnp.sum(jnp.where(seq[:, :, None] == span_ids[None, None, :], inverse[None, None, :], 0),
                  axis=2)
    last_start = jnp.max(
        jnp.where(doc_ends[None, :] <= (sq * SPAN + SPAN - 1)[:, None], doc_ends[None, :], 0), axis=1)
    full = (seq < sq[:, None]) & (seq * SPAN >= last_start[:, None])
    return (tbl.astype(jnp.int32), seq.astype(jnp.int32), before.astype(jnp.int32),
            sq.astype(jnp.int32), full.astype(jnp.int32))


def shift_x(value, d, n):
    return lax.ppermute(value, "x", [(i, (i + d) % n) for i in range(n)])


def reduce_scatter_x(value):
    n = lax.axis_size("x")
    parts = value.reshape(n, value.shape[0] // n, *value.shape[1:])
    received = lax.all_to_all(parts, "x", 0, 0, tiled=True)
    return jnp.sum(received.astype(jnp.float32), axis=0).astype(value.dtype)


def per_device(tokens, norm_gain, q_weight, k_weight, v_weight, o_weight, doc_lengths, span_order):
    local_rows = tokens.shape[1]
    tok_dev = local_rows * lax.axis_size(TENSOR)
    model_width = tokens.shape[2]
    head_dim = HEAD_DIM
    q_cols = q_weight.shape[1]
    kv_cols = k_weight.shape[1]
    q_heads = q_cols // head_dim
    kv_local = kv_cols // head_dim
    span_rows = tok_dev // 2
    base_row = lax.axis_index(CONTEXT) * tok_dev
    rows_float = tokens.astype(jnp.float32)
    normed = (
        rows_float
        * lax.rsqrt(jnp.mean(rows_float * rows_float, axis=-1, keepdims=True) + epsilon)
        * norm_gain
    ).astype(jnp.bfloat16)
    plane = lax.axis_index("yh")
    core = lax.axis_index("core")
    weights = jnp.concatenate([q_weight, k_weight, v_weight], axis=1)
    half_in = weights.shape[0] // 2
    sent_half = lax.dynamic_slice_in_dim(weights, core * half_in, half_in, 0)
    plane_rows = lax.all_gather(normed, "x", axis=1, tiled=True)
    partner_half = lax.ppermute(sent_half, ("yh", "ylo"), NEIGHBOUR)
    plane_rows, partner_half = lax.optimization_barrier((plane_rows, partner_half))
    other_half = lax.ppermute(partner_half, "core", [(0, 1), (1, 0)])
    half = plane_rows.shape[1]
    flat_rows = plane_rows.reshape(half, model_width)
    all_places = positions(base_row + jnp.arange(tok_dev, dtype=jnp.int32), span_order, span_rows)
    places = lax.dynamic_slice_in_dim(all_places, plane * half, half, 0)
    rows_mine = lax.dynamic_slice_in_dim(flat_rows, core * half_in, half_in, 1)
    rows_other = lax.dynamic_slice_in_dim(flat_rows, (1 - core) * half_in, half_in, 1)

    def finish(out):
        q = rotary(out[:, :q_cols].reshape(half, q_heads, head_dim), places)
        k = rotary(out[:, q_cols:q_cols + kv_cols].reshape(half, kv_local, head_dim), places)
        return jnp.concatenate(
            [q.reshape(half, q_cols), k.reshape(half, kv_cols), out[:, q_cols + kv_cols:]], axis=1
        ).astype(jnp.bfloat16)

    def project(w):
        return finish(jnp.dot(flat_rows, w, preferred_element_type=jnp.float32))

    for_partner = finish(
        jnp.dot(rows_mine, partner_half, preferred_element_type=jnp.float32)
        + jnp.dot(rows_other, other_half, preferred_element_type=jnp.float32))
    received = lax.ppermute(for_partner, "yh", [(0, 1), (1, 0)])
    flat_rows, for_partner = lax.optimization_barrier((flat_rows, for_partner))
    own = project(weights)
    first = jnp.where(plane == 0, own, received)
    second = jnp.where(plane == 0, received, own)
    projected = jnp.concatenate([first, second], axis=0)
    query_rows = projected[:, :q_cols]
    kv_pair = jnp.stack([projected[:, q_cols:q_cols + kv_cols], projected[:, q_cols + kv_cols:]])
    gathered = lax.all_gather(kv_pair, CONTEXT, axis=1, tiled=True)
    places = all_places
    row_count = tok_dev

    doc_ends = jnp.cumsum(doc_lengths)
    query_start = jnp.max(
        jnp.where(doc_ends[None, :] <= places[:, None], doc_ends[None, :], 0), axis=1)
    query_spans = lax.axis_index(CONTEXT) * 2 + jnp.arange(2, dtype=jnp.int32)
    tbl, seq, cnt, sq, full = key_tables(span_order, doc_ends, query_spans)
    qpos_col = places.astype(jnp.int32)[:, None]
    qstart_col = query_start.astype(jnp.int32)[:, None]
    m0, l0, acc0 = diagonal_attention(sq, query_rows, qpos_col, qstart_col, kv_pair)
    attended = span_attention(
        tbl, seq, cnt, full, query_rows, qpos_col, qstart_col, gathered, m0, l0, acc0)
    partner_o = lax.ppermute(o_weight, ("yh", "ylo"), NEIGHBOUR)
    half = row_count // 2
    own_rows = lax.dynamic_slice_in_dim(attended, plane * half, half, 0)
    other_rows = lax.dynamic_slice_in_dim(attended, (1 - plane) * half, half, 0)
    partner_rows = lax.ppermute(other_rows, "yh", [(0, 1), (1, 0)])
    mixed = (
        jnp.dot(own_rows, o_weight, preferred_element_type=jnp.float32)
        + jnp.dot(partner_rows, partner_o, preferred_element_type=jnp.float32)
    ).astype(jnp.bfloat16)
    mixed_rows = reduce_scatter_x(mixed)
    return mixed_rows.reshape(tokens.shape)


TENSOR = ("yh", "x")
NEIGHBOUR = [(0, 3), (3, 0), (1, 2), (2, 1)]
CONTEXT = ("z", "ylo", "core")


def solution(mesh):
    devices = mesh.devices.reshape(2, mesh.devices.shape[0] // 2, -1, 2, 2)
    split_mesh = jax.sharding.Mesh(devices, ("yh", "x", "z", "ylo", "core"))
    in_specs = (
        P(CONTEXT, TENSOR, None),
        P(),
        P(None, TENSOR),
        P(None, TENSOR),
        P(None, TENSOR),
        P(TENSOR, None),
        P(),
        P(),
    )
    out_specs = P(CONTEXT, TENSOR, None)
    return jax.shard_map(
        per_device, mesh=split_mesh, in_specs=in_specs, out_specs=out_specs, check_vma=False
    )
```

```python
import functools
import math

import jax
import jax.numpy as jnp
from jax import lax
from jax.experimental import pallas as pl
from jax.experimental.pallas import tpu as pltpu
from jax.sharding import PartitionSpec as P

HEAD_DIM = 128
SPAN = 512
KEY_SLOTS = 9

rope_theta = 500000.0
epsilon = 1e-05
masked_score = -1e30


def positions(rows, span_order, span_rows):
    slot_ids = jnp.arange(span_order.shape[0], dtype=jnp.int32)
    matches = (rows // span_rows)[:, None] == slot_ids[None, :]
    picked = jnp.sum(jnp.where(matches, span_order[None, :], 0), axis=1)
    return picked * span_rows + rows % span_rows


def rotary(values, places):
    head_dim = values.shape[-1]
    half_dim = head_dim // 2
    frequency = rope_theta ** (-(2.0 / head_dim) * jnp.arange(half_dim, dtype=jnp.float32))
    angles = places.astype(jnp.float32)[:, None] * frequency[None, :]
    cosine = jnp.cos(angles)[:, None, :]
    sine_part = jnp.sin(angles)[:, None, :]
    first_half = values[..., :half_dim]
    second = values[..., half_dim:]
    return jnp.concatenate(
        [first_half * cosine - second * sine_part, second * cosine + first_half * sine_part],
        axis=-1,
    )


def online_update(heads, scale, q_ref, k_ref, v_ref, visible, m_sc, l_sc, acc_sc):
    k = k_ref[...]
    v = v_ref[...]
    for h in range(heads):
        q = q_ref[:, h * HEAD_DIM:(h + 1) * HEAD_DIM]
        s = lax.dot_general(q, k, (((1,), (1,)), ((), ())),
                            preferred_element_type=jnp.float32) * scale
        m_old = m_sc[h]
        if visible is None:
            m_new = jnp.maximum(m_old, jnp.max(s, axis=-1, keepdims=True))
            p = jnp.exp(s - m_new)
        else:
            m_new = jnp.maximum(
                m_old, jnp.max(jnp.where(visible, s, masked_score), axis=-1, keepdims=True))
            p = jnp.where(visible, jnp.exp(s - m_new), 0.0)
        alpha = jnp.exp(m_old - m_new)
        l_sc[h] = alpha * l_sc[h] + jnp.sum(p, axis=-1, keepdims=True)
        acc_sc[h] = alpha * acc_sc[h] + jnp.dot(
            p.astype(jnp.bfloat16), v, preferred_element_type=jnp.float32)
        m_sc[h] = m_new


def diagonal_kernel(heads, scale, sq_ref, q_ref, qpos_ref, qstart_ref, k_ref, v_ref, k2_ref, v2_ref,
                    m_ref, l_ref, acc_ref):
    i = pl.program_id(0)
    m_ref[...] = jnp.full_like(m_ref, masked_score)
    l_ref[...] = jnp.zeros_like(l_ref)
    acc_ref[...] = jnp.zeros_like(acc_ref)
    span = k_ref.shape[0]
    for which, kr, vr in ((i, k_ref, v_ref), (1 - i, k2_ref, v2_ref)):
        kpos = sq_ref[which] * span + lax.broadcasted_iota(jnp.int32, (1, span), 1)
        visible = (kpos <= qpos_ref[...]) & (kpos >= qstart_ref[...])
        online_update(heads, scale, q_ref, kr, vr, visible, m_ref, l_ref, acc_ref)


def attention_kernel(heads, scale, tbl_ref, seq_ref, cnt_ref, full_ref, q_ref, qpos_ref, qstart_ref,
                     k_ref, v_ref, m_in, l_in, acc_in, o_ref, m_sc, l_sc, acc_sc):
    i = pl.program_id(0)
    j = pl.program_id(1)

    @pl.when(j == 0)
    def _():
        m_sc[...] = m_in[...]
        l_sc[...] = l_in[...]
        acc_sc[...] = acc_in[...]

    live = (j < cnt_ref[i]) & (full_ref[i, j] != 2)
    full = full_ref[i, j] == 1

    @pl.when(live & full)
    def _():
        online_update(heads, scale, q_ref, k_ref, v_ref, None, m_sc, l_sc, acc_sc)

    @pl.when(live & jnp.logical_not(full))
    def _():
        span = k_ref.shape[0]
        kpos = seq_ref[i, j] * span + lax.broadcasted_iota(jnp.int32, (1, span), 1)
        visible = (kpos <= qpos_ref[...]) & (kpos >= qstart_ref[...])
        online_update(heads, scale, q_ref, k_ref, v_ref, visible, m_sc, l_sc, acc_sc)

    @pl.when(j == pl.num_programs(1) - 1)
    def _():
        for h in range(heads):
            o_ref[:, h * HEAD_DIM:(h + 1) * HEAD_DIM] = (acc_sc[h] / l_sc[h]).astype(o_ref.dtype)


def diagonal_attention(sq, queries, qpos, qstart, local_kv):
    rows, q_cols = queries.shape
    heads = q_cols // HEAD_DIM
    n_q = rows // SPAN
    kernel = functools.partial(diagonal_kernel, heads, 1.0 / math.sqrt(HEAD_DIM))
    state = lambda w: pl.BlockSpec((None, heads, SPAN, w), lambda i, s: (i, 0, 0, 0))
    cost = pl.CostEstimate(
        flops=8 * n_q * heads * SPAN * SPAN * HEAD_DIM,
        transcendentals=2 * n_q * heads * SPAN * SPAN,
        bytes_accessed=2 * rows * q_cols + 8 * rows * HEAD_DIM + 4 * n_q * heads * SPAN * 130,
    )
    return pl.pallas_call(
        kernel,
        out_shape=(
            jax.ShapeDtypeStruct((n_q, heads, SPAN, 1), jnp.float32),
            jax.ShapeDtypeStruct((n_q, heads, SPAN, 1), jnp.float32),
            jax.ShapeDtypeStruct((n_q, heads, SPAN, HEAD_DIM), jnp.float32),
        ),
        grid_spec=pltpu.PrefetchScalarGridSpec(
            num_scalar_prefetch=1,
            grid=(n_q,),
            in_specs=[
                pl.BlockSpec((SPAN, q_cols), lambda i, s: (i, 0)),
                pl.BlockSpec((SPAN, 1), lambda i, s: (i, 0)),
                pl.BlockSpec((SPAN, 1), lambda i, s: (i, 0)),
                pl.BlockSpec((None, SPAN, HEAD_DIM), lambda i, s: (0, i, 0)),
                pl.BlockSpec((None, SPAN, HEAD_DIM), lambda i, s: (1, i, 0)),
                pl.BlockSpec((None, SPAN, HEAD_DIM), lambda i, s: (0, 1 - i, 0)),
                pl.BlockSpec((None, SPAN, HEAD_DIM), lambda i, s: (1, 1 - i, 0)),
            ],
            out_specs=[state(1), state(1), state(HEAD_DIM)],
        ),
        compiler_params=pltpu.CompilerParams(dimension_semantics=("arbitrary",)),
        cost_estimate=cost,
    )(sq, queries, qpos, qstart, local_kv, local_kv, local_kv, local_kv)


def span_attention(tbl, seq, cnt, full, queries, qpos, qstart, kv, m0, l0, acc0):
    rows, q_cols = queries.shape
    heads = q_cols // HEAD_DIM
    n_q = rows // SPAN
    slots = tbl.shape[1]
    kernel = functools.partial(attention_kernel, heads, 1.0 / math.sqrt(HEAD_DIM))
    steps = n_q * slots
    state = lambda w: pl.BlockSpec((None, heads, SPAN, w), lambda i, j, t, s, c, f: (i, 0, 0, 0))
    cost = pl.CostEstimate(
        flops=4 * steps * heads * SPAN * SPAN * HEAD_DIM,
        transcendentals=steps * heads * SPAN * SPAN,
        bytes_accessed=steps * 2 * SPAN * HEAD_DIM * 2 + 2 * rows * q_cols * 2,
    )
    return pl.pallas_call(
        kernel,
        out_shape=jax.ShapeDtypeStruct((rows, q_cols), jnp.bfloat16),
        grid_spec=pltpu.PrefetchScalarGridSpec(
            num_scalar_prefetch=4,
            grid=(n_q, slots),
            in_specs=[
                pl.BlockSpec((SPAN, q_cols), lambda i, j, t, s, c, f: (i, 0)),
                pl.BlockSpec((SPAN, 1), lambda i, j, t, s, c, f: (i, 0)),
                pl.BlockSpec((SPAN, 1), lambda i, j, t, s, c, f: (i, 0)),
                pl.BlockSpec((None, SPAN, HEAD_DIM), lambda i, j, t, s, c, f: (0, t[i, j], 0)),
                pl.BlockSpec((None, SPAN, HEAD_DIM), lambda i, j, t, s, c, f: (1, t[i, j], 0)),
                state(1), state(1), state(HEAD_DIM),
            ],
            out_specs=pl.BlockSpec((SPAN, q_cols), lambda i, j, t, s, c, f: (i, 0)),
            scratch_shapes=[
                pltpu.VMEM((heads, SPAN, 1), jnp.float32),
                pltpu.VMEM((heads, SPAN, 1), jnp.float32),
                pltpu.VMEM((heads, SPAN, HEAD_DIM), jnp.float32),
            ],
        ),
        compiler_params=pltpu.CompilerParams(dimension_semantics=("arbitrary", "arbitrary")),
        cost_estimate=cost,
    )(tbl, seq, cnt, full, queries, qpos, qstart, kv, kv, m0, l0, acc0)


def key_tables(span_order, doc_ends, query_spans):
    n_spans = span_order.shape[0]
    span_ids = jnp.arange(n_spans, dtype=jnp.int32)
    inverse = jnp.sum(
        jnp.where(span_order[None, :] == span_ids[:, None], span_ids[None, :], 0), axis=1)
    first_doc = jnp.sum((doc_ends[None, :] <= (span_ids * SPAN)[:, None]).astype(jnp.int32), axis=1)
    last_doc = jnp.sum(
        (doc_ends[None, :] <= (span_ids * SPAN + SPAN - 1)[:, None]).astype(jnp.int32), axis=1)
    sq = jnp.sum(jnp.where(query_spans[:, None] == span_ids[None, :], span_order[None, :], 0), axis=1)
    q_first = jnp.sum(jnp.where(sq[:, None] == span_ids[None, :], first_doc[None, :], 0), axis=1)
    back = jnp.arange(KEY_SLOTS, dtype=jnp.int32) - (KEY_SLOTS - 1)
    cand = sq[:, None] + back[None, :]
    cand_last = jnp.sum(
        jnp.where(cand[:, :, None] == span_ids[None, None, :], last_doc[None, None, :], 0), axis=2)
    valid = (cand >= 0) & (cand_last >= q_first[:, None])
    count = jnp.sum(valid.astype(jnp.int32), axis=1)
    before = count - 1
    slot = jnp.arange(KEY_SLOTS - 1, dtype=jnp.int32)
    last = jnp.maximum(sq - 1, 0)
    seq = jnp.clip(sq[:, None] - before[:, None] + slot[None, :], 0, last[:, None])
    tbl = jnp.sum(jnp.where(seq[:, :, None] == span_ids[None, None, :], inverse[None, None, :], 0),
                  axis=2)
    last_start = jnp.max(
        jnp.where(doc_ends[None, :] <= (sq * SPAN + SPAN - 1)[:, None], doc_ends[None, :], 0), axis=1)
    full = (seq < sq[:, None]) & (seq * SPAN >= last_start[:, None])
    full = jnp.where(seq == sq[::-1][:, None], 2, full.astype(jnp.int32))
    return (tbl.astype(jnp.int32), seq.astype(jnp.int32), before.astype(jnp.int32),
            sq.astype(jnp.int32), full.astype(jnp.int32))


def shift_x(value, d, n):
    return lax.ppermute(value, "x", [(i, (i + d) % n) for i in range(n)])


def reduce_scatter_x(value):
    n = lax.axis_size("x")
    me = lax.axis_index("x")
    parts = value.reshape(n, value.shape[0] // n, *value.shape[1:])
    total = jnp.take(parts, me, axis=0).astype(jnp.float32)
    for d in range(1, n):
        total = total + shift_x(jnp.take(parts, (me + d) % n, axis=0), d, n).astype(jnp.float32)
    return total.astype(value.dtype)


def per_device(tokens, norm_gain, q_weight, k_weight, v_weight, o_weight, doc_lengths, span_order):
    local_rows = tokens.shape[1]
    tok_dev = local_rows * lax.axis_size(TENSOR)
    model_width = tokens.shape[2]
    head_dim = HEAD_DIM
    q_cols = q_weight.shape[1]
    kv_cols = k_weight.shape[1]
    q_heads = q_cols // head_dim
    kv_local = kv_cols // head_dim
    span_rows = tok_dev // 2
    base_row = lax.axis_index(CONTEXT) * tok_dev
    rows_float = tokens.astype(jnp.float32)
    normed = (
        rows_float
        * lax.rsqrt(jnp.mean(rows_float * rows_float, axis=-1, keepdims=True) + epsilon)
        * norm_gain
    ).astype(jnp.bfloat16)
    plane = lax.axis_index("yh")
    core = lax.axis_index("core")
    weights = jnp.concatenate([q_weight, k_weight, v_weight], axis=1)
    half_in = weights.shape[0] // 2
    sent_half = lax.dynamic_slice_in_dim(weights, core * half_in, half_in, 0)
    plane_rows = lax.all_gather(normed, "x", axis=1, tiled=True)
    partner_half = lax.ppermute(sent_half, ("yh", "ylo"), NEIGHBOUR)
    plane_rows, partner_half = lax.optimization_barrier((plane_rows, partner_half))
    other_half = lax.ppermute(partner_half, "core", [(0, 1), (1, 0)])
    half = plane_rows.shape[1]
    flat_rows = plane_rows.reshape(half, model_width)
    all_places = positions(base_row + jnp.arange(tok_dev, dtype=jnp.int32), span_order, span_rows)
    places = lax.dynamic_slice_in_dim(all_places, plane * half, half, 0)
    rows_mine = lax.dynamic_slice_in_dim(flat_rows, core * half_in, half_in, 1)
    rows_other = lax.dynamic_slice_in_dim(flat_rows, (1 - core) * half_in, half_in, 1)

    def finish(out):
        q = rotary(out[:, :q_cols].reshape(half, q_heads, head_dim), places)
        k = rotary(out[:, q_cols:q_cols + kv_cols].reshape(half, kv_local, head_dim), places)
        return jnp.concatenate(
            [q.reshape(half, q_cols), k.reshape(half, kv_cols), out[:, q_cols + kv_cols:]], axis=1
        ).astype(jnp.bfloat16)

    def project(w):
        return finish(jnp.dot(flat_rows, w, preferred_element_type=jnp.float32))

    for_partner = finish(
        jnp.dot(rows_mine, partner_half, preferred_element_type=jnp.float32)
        + jnp.dot(rows_other, other_half, preferred_element_type=jnp.float32))
    received = lax.ppermute(for_partner, "yh", [(0, 1), (1, 0)])
    flat_rows, for_partner = lax.optimization_barrier((flat_rows, for_partner))
    own = project(weights)
    first = jnp.where(plane == 0, own, received)
    second = jnp.where(plane == 0, received, own)
    projected = jnp.concatenate([first, second], axis=0)
    query_rows = projected[:, :q_cols]
    kv_pair = jnp.stack([projected[:, q_cols:q_cols + kv_cols], projected[:, q_cols + kv_cols:]])
    gathered = lax.all_gather(kv_pair, CONTEXT, axis=1, tiled=True)
    places = all_places
    row_count = tok_dev

    doc_ends = jnp.cumsum(doc_lengths)
    query_start = jnp.max(
        jnp.where(doc_ends[None, :] <= places[:, None], doc_ends[None, :], 0), axis=1)
    query_spans = lax.axis_index(CONTEXT) * 2 + jnp.arange(2, dtype=jnp.int32)
    tbl, seq, cnt, sq, full = key_tables(span_order, doc_ends, query_spans)
    qpos_col = places.astype(jnp.int32)[:, None]
    qstart_col = query_start.astype(jnp.int32)[:, None]
    m0, l0, acc0 = diagonal_attention(sq, query_rows, qpos_col, qstart_col, kv_pair)
    attended = span_attention(
        tbl, seq, cnt, full, query_rows, qpos_col, qstart_col, gathered, m0, l0, acc0)
    partner_o = lax.ppermute(o_weight, ("yh", "ylo"), NEIGHBOUR)
    half = row_count // 2
    own_rows = lax.dynamic_slice_in_dim(attended, plane * half, half, 0)
    other_rows = lax.dynamic_slice_in_dim(attended, (1 - plane) * half, half, 0)
    partner_rows = lax.ppermute(other_rows, "yh", [(0, 1), (1, 0)])
    mixed = (
        jnp.dot(own_rows, o_weight, preferred_element_type=jnp.float32)
        + jnp.dot(partner_rows, partner_o, preferred_element_type=jnp.float32)
    ).astype(jnp.bfloat16)
    mixed_rows = reduce_scatter_x(mixed)
    return mixed_rows.reshape(tokens.shape)


TENSOR = ("yh", "x")
NEIGHBOUR = [(0, 3), (3, 0), (1, 2), (2, 1)]
CONTEXT = ("z", "ylo", "core")


def solution(mesh):
    devices = mesh.devices.reshape(2, mesh.devices.shape[0] // 2, -1, 2, 2)
    split_mesh = jax.sharding.Mesh(devices, ("yh", "x", "z", "ylo", "core"))
    in_specs = (
        P(CONTEXT, TENSOR, None),
        P(),
        P(None, TENSOR),
        P(None, TENSOR),
        P(None, TENSOR),
        P(TENSOR, None),
        P(),
        P(),
    )
    out_specs = P(CONTEXT, TENSOR, None)
    return jax.shard_map(
        per_device, mesh=split_mesh, in_specs=in_specs, out_specs=out_specs, check_vma=False
    )
```

```python
import functools
import math

import jax
import jax.numpy as jnp
from jax import lax
from jax.experimental import pallas as pl
from jax.experimental.pallas import tpu as pltpu
from jax.sharding import PartitionSpec as P

HEAD_DIM = 128
SPAN = 512
KEY_SLOTS = 9

rope_theta = 500000.0
epsilon = 1e-05
masked_score = -1e30


def positions(rows, span_order, span_rows):
    slot_ids = jnp.arange(span_order.shape[0], dtype=jnp.int32)
    matches = (rows // span_rows)[:, None] == slot_ids[None, :]
    picked = jnp.sum(jnp.where(matches, span_order[None, :], 0), axis=1)
    return picked * span_rows + rows % span_rows


def rotary(values, places):
    head_dim = values.shape[-1]
    half_dim = head_dim // 2
    frequency = rope_theta ** (-(2.0 / head_dim) * jnp.arange(half_dim, dtype=jnp.float32))
    angles = places.astype(jnp.float32)[:, None] * frequency[None, :]
    cosine = jnp.cos(angles)[:, None, :]
    sine_part = jnp.sin(angles)[:, None, :]
    first_half = values[..., :half_dim]
    second = values[..., half_dim:]
    return jnp.concatenate(
        [first_half * cosine - second * sine_part, second * cosine + first_half * sine_part],
        axis=-1,
    )


def online_update(heads, scale, q_ref, k_ref, v_ref, visible, m_sc, l_sc, acc_sc):
    k = k_ref[...]
    v = v_ref[...]
    for h in range(heads):
        q = q_ref[:, h * HEAD_DIM:(h + 1) * HEAD_DIM]
        s = lax.dot_general(q, k, (((1,), (1,)), ((), ())),
                            preferred_element_type=jnp.float32) * scale
        m_old = m_sc[h]
        if visible is None:
            m_new = jnp.maximum(m_old, jnp.max(s, axis=-1, keepdims=True))
            p = jnp.exp(s - m_new)
        else:
            m_new = jnp.maximum(
                m_old, jnp.max(jnp.where(visible, s, masked_score), axis=-1, keepdims=True))
            p = jnp.where(visible, jnp.exp(s - m_new), 0.0)
        alpha = jnp.exp(m_old - m_new)
        l_sc[h] = alpha * l_sc[h] + jnp.sum(p, axis=-1, keepdims=True)
        acc_sc[h] = alpha * acc_sc[h] + jnp.dot(
            p.astype(jnp.bfloat16), v, preferred_element_type=jnp.float32)
        m_sc[h] = m_new


def diagonal_kernel(heads, scale, sq_ref, q_ref, qpos_ref, qstart_ref, k_ref, v_ref,
                    m_ref, l_ref, acc_ref):
    i = pl.program_id(0)
    m_ref[...] = jnp.full_like(m_ref, masked_score)
    l_ref[...] = jnp.zeros_like(l_ref)
    acc_ref[...] = jnp.zeros_like(acc_ref)
    span = k_ref.shape[0]
    kpos = sq_ref[i] * span + lax.broadcasted_iota(jnp.int32, (1, span), 1)
    visible = (kpos <= qpos_ref[...]) & (kpos >= qstart_ref[...])
    online_update(heads, scale, q_ref, k_ref, v_ref, visible, m_ref, l_ref, acc_ref)


def attention_kernel(heads, scale, tbl_ref, seq_ref, cnt_ref, full_ref, q_ref, qpos_ref, qstart_ref,
                     k_ref, v_ref, m_in, l_in, acc_in, o_ref, m_sc, l_sc, acc_sc):
    i = pl.program_id(0)
    j = pl.program_id(1)

    @pl.when(j == 0)
    def _():
        m_sc[...] = m_in[...]
        l_sc[...] = l_in[...]
        acc_sc[...] = acc_in[...]

    live = j < cnt_ref[i]
    full = full_ref[i, j] == 1

    @pl.when(live & full)
    def _():
        online_update(heads, scale, q_ref, k_ref, v_ref, None, m_sc, l_sc, acc_sc)

    @pl.when(live & jnp.logical_not(full))
    def _():
        span = k_ref.shape[0]
        kpos = seq_ref[i, j] * span + lax.broadcasted_iota(jnp.int32, (1, span), 1)
        visible = (kpos <= qpos_ref[...]) & (kpos >= qstart_ref[...])
        online_update(heads, scale, q_ref, k_ref, v_ref, visible, m_sc, l_sc, acc_sc)

    @pl.when(j == pl.num_programs(1) - 1)
    def _():
        for h in range(heads):
            o_ref[:, h * HEAD_DIM:(h + 1) * HEAD_DIM] = (acc_sc[h] / l_sc[h]).astype(o_ref.dtype)


def diagonal_attention(sq, queries, qpos, qstart, local_kv):
    rows, q_cols = queries.shape
    heads = q_cols // HEAD_DIM
    n_q = rows // SPAN
    kernel = functools.partial(diagonal_kernel, heads, 1.0 / math.sqrt(HEAD_DIM))
    state = lambda w: pl.BlockSpec((None, heads, SPAN, w), lambda i, s: (i, 0, 0, 0))
    cost = pl.CostEstimate(
        flops=4 * n_q * heads * SPAN * SPAN * HEAD_DIM,
        transcendentals=n_q * heads * SPAN * SPAN,
        bytes_accessed=2 * rows * q_cols + 4 * rows * HEAD_DIM + 4 * n_q * heads * SPAN * 130,
    )
    return pl.pallas_call(
        kernel,
        out_shape=(
            jax.ShapeDtypeStruct((n_q, heads, SPAN, 1), jnp.float32),
            jax.ShapeDtypeStruct((n_q, heads, SPAN, 1), jnp.float32),
            jax.ShapeDtypeStruct((n_q, heads, SPAN, HEAD_DIM), jnp.float32),
        ),
        grid_spec=pltpu.PrefetchScalarGridSpec(
            num_scalar_prefetch=1,
            grid=(n_q,),
            in_specs=[
                pl.BlockSpec((SPAN, q_cols), lambda i, s: (i, 0)),
                pl.BlockSpec((SPAN, 1), lambda i, s: (i, 0)),
                pl.BlockSpec((SPAN, 1), lambda i, s: (i, 0)),
                pl.BlockSpec((None, SPAN, HEAD_DIM), lambda i, s: (0, i, 0)),
                pl.BlockSpec((None, SPAN, HEAD_DIM), lambda i, s: (1, i, 0)),
            ],
            out_specs=[state(1), state(1), state(HEAD_DIM)],
        ),
        compiler_params=pltpu.CompilerParams(dimension_semantics=("arbitrary",)),
        cost_estimate=cost,
    )(sq, queries, qpos, qstart, local_kv, local_kv)


def span_attention(tbl, seq, cnt, full, queries, qpos, qstart, kv, m0, l0, acc0):
    rows, q_cols = queries.shape
    heads = q_cols // HEAD_DIM
    n_q = rows // SPAN
    slots = tbl.shape[1]
    kernel = functools.partial(attention_kernel, heads, 1.0 / math.sqrt(HEAD_DIM))
    steps = n_q * slots
    state = lambda w: pl.BlockSpec((None, heads, SPAN, w), lambda i, j, t, s, c, f: (i, 0, 0, 0))
    cost = pl.CostEstimate(
        flops=4 * steps * heads * SPAN * SPAN * HEAD_DIM,
        transcendentals=steps * heads * SPAN * SPAN,
        bytes_accessed=steps * 2 * SPAN * HEAD_DIM * 2 + 2 * rows * q_cols * 2,
    )
    return pl.pallas_call(
        kernel,
        out_shape=jax.ShapeDtypeStruct((rows, q_cols), jnp.bfloat16),
        grid_spec=pltpu.PrefetchScalarGridSpec(
            num_scalar_prefetch=4,
            grid=(n_q, slots),
            in_specs=[
                pl.BlockSpec((SPAN, q_cols), lambda i, j, t, s, c, f: (i, 0)),
                pl.BlockSpec((SPAN, 1), lambda i, j, t, s, c, f: (i, 0)),
                pl.BlockSpec((SPAN, 1), lambda i, j, t, s, c, f: (i, 0)),
                pl.BlockSpec((None, SPAN, HEAD_DIM), lambda i, j, t, s, c, f: (0, t[i, j], 0)),
                pl.BlockSpec((None, SPAN, HEAD_DIM), lambda i, j, t, s, c, f: (1, t[i, j], 0)),
                state(1), state(1), state(HEAD_DIM),
            ],
            out_specs=pl.BlockSpec((SPAN, q_cols), lambda i, j, t, s, c, f: (i, 0)),
            scratch_shapes=[
                pltpu.VMEM((heads, SPAN, 1), jnp.float32),
                pltpu.VMEM((heads, SPAN, 1), jnp.float32),
                pltpu.VMEM((heads, SPAN, HEAD_DIM), jnp.float32),
            ],
        ),
        compiler_params=pltpu.CompilerParams(dimension_semantics=("arbitrary", "arbitrary")),
        cost_estimate=cost,
    )(tbl, seq, cnt, full, queries, qpos, qstart, kv, kv, m0, l0, acc0)


def key_tables(span_order, doc_ends, query_spans):
    n_spans = span_order.shape[0]
    span_ids = jnp.arange(n_spans, dtype=jnp.int32)
    inverse = jnp.sum(
        jnp.where(span_order[None, :] == span_ids[:, None], span_ids[None, :], 0), axis=1)
    first_doc = jnp.sum((doc_ends[None, :] <= (span_ids * SPAN)[:, None]).astype(jnp.int32), axis=1)
    last_doc = jnp.sum(
        (doc_ends[None, :] <= (span_ids * SPAN + SPAN - 1)[:, None]).astype(jnp.int32), axis=1)
    sq = jnp.sum(jnp.where(query_spans[:, None] == span_ids[None, :], span_order[None, :], 0), axis=1)
    q_first = jnp.sum(jnp.where(sq[:, None] == span_ids[None, :], first_doc[None, :], 0), axis=1)
    back = jnp.arange(KEY_SLOTS, dtype=jnp.int32) - (KEY_SLOTS - 1)
    cand = sq[:, None] + back[None, :]
    cand_last = jnp.sum(
        jnp.where(cand[:, :, None] == span_ids[None, None, :], last_doc[None, None, :], 0), axis=2)
    valid = (cand >= 0) & (cand_last >= q_first[:, None])
    count = jnp.sum(valid.astype(jnp.int32), axis=1)
    before = count - 1
    slot = jnp.arange(KEY_SLOTS - 1, dtype=jnp.int32)
    last = jnp.maximum(sq - 1, 0)
    seq = jnp.clip(sq[:, None] - before[:, None] + slot[None, :], 0, last[:, None])
    tbl = jnp.sum(jnp.where(seq[:, :, None] == span_ids[None, None, :], inverse[None, None, :], 0),
                  axis=2)
    last_start = jnp.max(
        jnp.where(doc_ends[None, :] <= (sq * SPAN + SPAN - 1)[:, None], doc_ends[None, :], 0), axis=1)
    full = (seq < sq[:, None]) & (seq * SPAN >= last_start[:, None])
    return (tbl.astype(jnp.int32), seq.astype(jnp.int32), before.astype(jnp.int32),
            sq.astype(jnp.int32), full.astype(jnp.int32))


def shift_x(value, d, n):
    return lax.ppermute(value, "x", [(i, (i + d) % n) for i in range(n)])


def reduce_scatter_x(value):
    n = lax.axis_size("x")
    me = lax.axis_index("x")
    parts = value.reshape(n, value.shape[0] // n, *value.shape[1:])
    total = jnp.take(parts, me, axis=0).astype(jnp.float32)
    for d in range(1, n):
        total = total + shift_x(jnp.take(parts, (me + d) % n, axis=0), d, n).astype(jnp.float32)
    return total.astype(value.dtype)


def per_device(tokens, norm_gain, q_weight, k_weight, v_weight, o_weight, doc_lengths, span_order):
    local_rows = tokens.shape[1]
    tok_dev = local_rows * lax.axis_size(TENSOR)
    model_width = tokens.shape[2]
    head_dim = HEAD_DIM
    q_cols = q_weight.shape[1]
    kv_cols = k_weight.shape[1]
    q_heads = q_cols // head_dim
    kv_local = kv_cols // head_dim
    span_rows = tok_dev // 2
    base_row = lax.axis_index(CONTEXT) * tok_dev
    rows_float = tokens.astype(jnp.float32)
    normed = (
        rows_float
        * lax.rsqrt(jnp.mean(rows_float * rows_float, axis=-1, keepdims=True) + epsilon)
        * norm_gain
    ).astype(jnp.bfloat16)
    plane = lax.axis_index("yh")
    core = lax.axis_index("core")
    weights = jnp.concatenate([q_weight, k_weight, v_weight], axis=1)
    half_in = weights.shape[0] // 2
    sent_half = jnp.concatenate(
        [lax.dynamic_slice_in_dim(w, core * half_in, half_in, 0) for w in (q_weight, k_weight, v_weight)],
        axis=1)
    plane_rows = lax.all_gather(normed, "x", axis=1, tiled=True)
    partner_half = lax.ppermute(sent_half, ("yh", "ylo"), NEIGHBOUR)
    plane_rows, partner_half = lax.optimization_barrier((plane_rows, partner_half))
    other_half = lax.ppermute(partner_half, "core", [(0, 1), (1, 0)])
    half = plane_rows.shape[1]
    flat_rows = plane_rows.reshape(half, model_width)
    all_places = positions(base_row + jnp.arange(tok_dev, dtype=jnp.int32), span_order, span_rows)
    places = lax.dynamic_slice_in_dim(all_places, plane * half, half, 0)
    rows_mine = lax.dynamic_slice_in_dim(flat_rows, core * half_in, half_in, 1)
    rows_other = lax.dynamic_slice_in_dim(flat_rows, (1 - core) * half_in, half_in, 1)

    def finish(out):
        q = rotary(out[:, :q_cols].reshape(half, q_heads, head_dim), places)
        k = rotary(out[:, q_cols:q_cols + kv_cols].reshape(half, kv_local, head_dim), places)
        return jnp.concatenate(
            [q.reshape(half, q_cols), k.reshape(half, kv_cols), out[:, q_cols + kv_cols:]], axis=1
        ).astype(jnp.bfloat16)

    def project(w):
        return finish(jnp.dot(flat_rows, w, preferred_element_type=jnp.float32))

    for_partner = finish(
        jnp.dot(rows_mine, partner_half, preferred_element_type=jnp.float32)
        + jnp.dot(rows_other, other_half, preferred_element_type=jnp.float32))
    received = lax.ppermute(for_partner, "yh", [(0, 1), (1, 0)])
    flat_rows, for_partner = lax.optimization_barrier((flat_rows, for_partner))
    own = project(weights)
    first = jnp.where(plane == 0, own, received)
    second = jnp.where(plane == 0, received, own)
    projected = jnp.concatenate([first, second], axis=0)
    query_rows = projected[:, :q_cols]
    kv_pair = jnp.stack([projected[:, q_cols:q_cols + kv_cols], projected[:, q_cols + kv_cols:]])
    gathered = lax.all_gather(kv_pair, CONTEXT, axis=1, tiled=True)
    places = all_places
    row_count = tok_dev

    doc_ends = jnp.cumsum(doc_lengths)
    query_start = jnp.max(
        jnp.where(doc_ends[None, :] <= places[:, None], doc_ends[None, :], 0), axis=1)
    query_spans = lax.axis_index(CONTEXT) * 2 + jnp.arange(2, dtype=jnp.int32)
    tbl, seq, cnt, sq, full = key_tables(span_order, doc_ends, query_spans)
    qpos_col = places.astype(jnp.int32)[:, None]
    qstart_col = query_start.astype(jnp.int32)[:, None]
    m0, l0, acc0 = diagonal_attention(sq, query_rows, qpos_col, qstart_col, kv_pair)
    attended = span_attention(
        tbl, seq, cnt, full, query_rows, qpos_col, qstart_col, gathered, m0, l0, acc0)
    partner_o = lax.ppermute(o_weight, ("yh", "ylo"), NEIGHBOUR)
    half = row_count // 2
    own_rows = lax.dynamic_slice_in_dim(attended, plane * half, half, 0)
    other_rows = lax.dynamic_slice_in_dim(attended, (1 - plane) * half, half, 0)
    partner_rows = lax.ppermute(other_rows, "yh", [(0, 1), (1, 0)])
    mixed = (
        jnp.dot(own_rows, o_weight, preferred_element_type=jnp.float32)
        + jnp.dot(partner_rows, partner_o, preferred_element_type=jnp.float32)
    ).astype(jnp.bfloat16)
    mixed_rows = reduce_scatter_x(mixed)
    return mixed_rows.reshape(tokens.shape)


TENSOR = ("yh", "x")
NEIGHBOUR = [(0, 3), (3, 0), (1, 2), (2, 1)]
CONTEXT = ("z", "ylo", "core")


def solution(mesh):
    devices = mesh.devices.reshape(2, mesh.devices.shape[0] // 2, -1, 2, 2)
    split_mesh = jax.sharding.Mesh(devices, ("yh", "x", "z", "ylo", "core"))
    in_specs = (
        P(CONTEXT, TENSOR, None),
        P(),
        P(None, TENSOR),
        P(None, TENSOR),
        P(None, TENSOR),
        P(TENSOR, None),
        P(),
        P(),
    )
    out_specs = P(CONTEXT, TENSOR, None)
    return jax.shard_map(
        per_device, mesh=split_mesh, in_specs=in_specs, out_specs=out_specs, check_vma=False
    )
```

```python
import functools
import math

import jax
import jax.numpy as jnp
from jax import lax
from jax.experimental import pallas as pl
from jax.experimental.pallas import tpu as pltpu
from jax.sharding import PartitionSpec as P

HEAD_DIM = 128
SPAN = 512
KEY_SLOTS = 9

rope_theta = 500000.0
epsilon = 1e-05
masked_score = -1e30


def positions(rows, span_order, span_rows):
    slot_ids = jnp.arange(span_order.shape[0], dtype=jnp.int32)
    matches = (rows // span_rows)[:, None] == slot_ids[None, :]
    picked = jnp.sum(jnp.where(matches, span_order[None, :], 0), axis=1)
    return picked * span_rows + rows % span_rows


def rotary(values, places):
    head_dim = values.shape[-1]
    half_dim = head_dim // 2
    frequency = rope_theta ** (-(2.0 / head_dim) * jnp.arange(half_dim, dtype=jnp.float32))
    angles = places.astype(jnp.float32)[:, None] * frequency[None, :]
    cosine = jnp.cos(angles)[:, None, :]
    sine_part = jnp.sin(angles)[:, None, :]
    first_half = values[..., :half_dim]
    second = values[..., half_dim:]
    return jnp.concatenate(
        [first_half * cosine - second * sine_part, second * cosine + first_half * sine_part],
        axis=-1,
    )


def online_update(heads, scale, q_ref, k_ref, v_ref, visible, m_sc, l_sc, acc_sc):
    k = k_ref[...]
    v = v_ref[...]
    for h in range(heads):
        q = q_ref[:, h * HEAD_DIM:(h + 1) * HEAD_DIM]
        s = lax.dot_general(q, k, (((1,), (1,)), ((), ())),
                            preferred_element_type=jnp.float32) * scale
        m_old = m_sc[h]
        if visible is None:
            m_new = jnp.maximum(m_old, jnp.max(s, axis=-1, keepdims=True))
            p = jnp.exp(s - m_new)
        else:
            m_new = jnp.maximum(
                m_old, jnp.max(jnp.where(visible, s, masked_score), axis=-1, keepdims=True))
            p = jnp.where(visible, jnp.exp(s - m_new), 0.0)
        alpha = jnp.exp(m_old - m_new)
        l_sc[h] = alpha * l_sc[h] + jnp.sum(p, axis=-1, keepdims=True)
        acc_sc[h] = alpha * acc_sc[h] + jnp.dot(
            p.astype(jnp.bfloat16), v, preferred_element_type=jnp.float32)
        m_sc[h] = m_new


def diagonal_kernel(heads, scale, sq_ref, q_ref, qpos_ref, qstart_ref, k_ref, v_ref,
                    m_ref, l_ref, acc_ref):
    i = pl.program_id(0)
    m_ref[...] = jnp.full_like(m_ref, masked_score)
    l_ref[...] = jnp.zeros_like(l_ref)
    acc_ref[...] = jnp.zeros_like(acc_ref)
    span = k_ref.shape[0]
    kpos = sq_ref[i] * span + lax.broadcasted_iota(jnp.int32, (1, span), 1)
    visible = (kpos <= qpos_ref[...]) & (kpos >= qstart_ref[...])
    online_update(heads, scale, q_ref, k_ref, v_ref, visible, m_ref, l_ref, acc_ref)


def attention_kernel(heads, scale, tbl_ref, seq_ref, cnt_ref, full_ref, q_ref, qpos_ref, qstart_ref,
                     k_ref, v_ref, m_in, l_in, acc_in, o_ref, m_sc, l_sc, acc_sc):
    i = pl.program_id(0)
    j = pl.program_id(1)

    @pl.when(j == 0)
    def _():
        m_sc[...] = m_in[...]
        l_sc[...] = l_in[...]
        acc_sc[...] = acc_in[...]

    live = j < cnt_ref[i]
    full = full_ref[i, j] == 1

    @pl.when(live & full)
    def _():
        online_update(heads, scale, q_ref, k_ref, v_ref, None, m_sc, l_sc, acc_sc)

    @pl.when(live & jnp.logical_not(full))
    def _():
        span = k_ref.shape[0]
        kpos = seq_ref[i, j] * span + lax.broadcasted_iota(jnp.int32, (1, span), 1)
        visible = (kpos <= qpos_ref[...]) & (kpos >= qstart_ref[...])
        online_update(heads, scale, q_ref, k_ref, v_ref, visible, m_sc, l_sc, acc_sc)

    @pl.when(j == pl.num_programs(1) - 1)
    def _():
        for h in range(heads):
            o_ref[:, h * HEAD_DIM:(h + 1) * HEAD_DIM] = (acc_sc[h] / l_sc[h]).astype(o_ref.dtype)


def diagonal_attention(sq, queries, qpos, qstart, local_kv):
    rows, q_cols = queries.shape
    heads = q_cols // HEAD_DIM
    n_q = rows // SPAN
    kernel = functools.partial(diagonal_kernel, heads, 1.0 / math.sqrt(HEAD_DIM))
    state = lambda w: pl.BlockSpec((None, heads, SPAN, w), lambda i, s: (i, 0, 0, 0))
    cost = pl.CostEstimate(
        flops=4 * n_q * heads * SPAN * SPAN * HEAD_DIM,
        transcendentals=n_q * heads * SPAN * SPAN,
        bytes_accessed=2 * rows * q_cols + 4 * rows * HEAD_DIM + 4 * n_q * heads * SPAN * 130,
    )
    return pl.pallas_call(
        kernel,
        out_shape=(
            jax.ShapeDtypeStruct((n_q, heads, SPAN, 1), jnp.float32),
            jax.ShapeDtypeStruct((n_q, heads, SPAN, 1), jnp.float32),
            jax.ShapeDtypeStruct((n_q, heads, SPAN, HEAD_DIM), jnp.float32),
        ),
        grid_spec=pltpu.PrefetchScalarGridSpec(
            num_scalar_prefetch=1,
            grid=(n_q,),
            in_specs=[
                pl.BlockSpec((SPAN, q_cols), lambda i, s: (i, 0)),
                pl.BlockSpec((SPAN, 1), lambda i, s: (i, 0)),
                pl.BlockSpec((SPAN, 1), lambda i, s: (i, 0)),
                pl.BlockSpec((None, SPAN, HEAD_DIM), lambda i, s: (0, i, 0)),
                pl.BlockSpec((None, SPAN, HEAD_DIM), lambda i, s: (1, i, 0)),
            ],
            out_specs=[state(1), state(1), state(HEAD_DIM)],
        ),
        compiler_params=pltpu.CompilerParams(dimension_semantics=("arbitrary",)),
        cost_estimate=cost,
    )(sq, queries, qpos, qstart, local_kv, local_kv)


def span_attention(tbl, seq, cnt, full, queries, qpos, qstart, kv, m0, l0, acc0):
    rows, q_cols = queries.shape
    heads = q_cols // HEAD_DIM
    n_q = rows // SPAN
    slots = tbl.shape[1]
    kernel = functools.partial(attention_kernel, heads, 1.0 / math.sqrt(HEAD_DIM))
    steps = n_q * slots
    state = lambda w: pl.BlockSpec((None, heads, SPAN, w), lambda i, j, t, s, c, f: (i, 0, 0, 0))
    cost = pl.CostEstimate(
        flops=4 * steps * heads * SPAN * SPAN * HEAD_DIM,
        transcendentals=steps * heads * SPAN * SPAN,
        bytes_accessed=steps * 2 * SPAN * HEAD_DIM * 2 + 2 * rows * q_cols * 2,
    )
    return pl.pallas_call(
        kernel,
        out_shape=jax.ShapeDtypeStruct((rows, q_cols), jnp.bfloat16),
        grid_spec=pltpu.PrefetchScalarGridSpec(
            num_scalar_prefetch=4,
            grid=(n_q, slots),
            in_specs=[
                pl.BlockSpec((SPAN, q_cols), lambda i, j, t, s, c, f: (i, 0)),
                pl.BlockSpec((SPAN, 1), lambda i, j, t, s, c, f: (i, 0)),
                pl.BlockSpec((SPAN, 1), lambda i, j, t, s, c, f: (i, 0)),
                pl.BlockSpec((None, SPAN, HEAD_DIM), lambda i, j, t, s, c, f: (0, t[i, j], 0)),
                pl.BlockSpec((None, SPAN, HEAD_DIM), lambda i, j, t, s, c, f: (1, t[i, j], 0)),
                state(1), state(1), state(HEAD_DIM),
            ],
            out_specs=pl.BlockSpec((SPAN, q_cols), lambda i, j, t, s, c, f: (i, 0)),
            scratch_shapes=[
                pltpu.VMEM((heads, SPAN, 1), jnp.float32),
                pltpu.VMEM((heads, SPAN, 1), jnp.float32),
                pltpu.VMEM((heads, SPAN, HEAD_DIM), jnp.float32),
            ],
        ),
        compiler_params=pltpu.CompilerParams(dimension_semantics=("arbitrary", "arbitrary")),
        cost_estimate=cost,
    )(tbl, seq, cnt, full, queries, qpos, qstart, kv, kv, m0, l0, acc0)


def key_tables(span_order, doc_ends, query_spans):
    n_spans = span_order.shape[0]
    span_ids = jnp.arange(n_spans, dtype=jnp.int32)
    inverse = jnp.sum(
        jnp.where(span_order[None, :] == span_ids[:, None], span_ids[None, :], 0), axis=1)
    first_doc = jnp.sum((doc_ends[None, :] <= (span_ids * SPAN)[:, None]).astype(jnp.int32), axis=1)
    last_doc = jnp.sum(
        (doc_ends[None, :] <= (span_ids * SPAN + SPAN - 1)[:, None]).astype(jnp.int32), axis=1)
    sq = jnp.sum(jnp.where(query_spans[:, None] == span_ids[None, :], span_order[None, :], 0), axis=1)
    q_first = jnp.sum(jnp.where(sq[:, None] == span_ids[None, :], first_doc[None, :], 0), axis=1)
    back = jnp.arange(KEY_SLOTS, dtype=jnp.int32) - (KEY_SLOTS - 1)
    cand = sq[:, None] + back[None, :]
    cand_last = jnp.sum(
        jnp.where(cand[:, :, None] == span_ids[None, None, :], last_doc[None, None, :], 0), axis=2)
    valid = (cand >= 0) & (cand_last >= q_first[:, None])
    count = jnp.sum(valid.astype(jnp.int32), axis=1)
    before = count - 1
    slot = jnp.arange(KEY_SLOTS - 1, dtype=jnp.int32)
    last = jnp.maximum(sq - 1, 0)
    seq = jnp.clip(sq[:, None] - before[:, None] + slot[None, :], 0, last[:, None])
    tbl = jnp.sum(jnp.where(seq[:, :, None] == span_ids[None, None, :], inverse[None, None, :], 0),
                  axis=2)
    last_start = jnp.max(
        jnp.where(doc_ends[None, :] <= (sq * SPAN + SPAN - 1)[:, None], doc_ends[None, :], 0), axis=1)
    full = (seq < sq[:, None]) & (seq * SPAN >= last_start[:, None])
    return (tbl.astype(jnp.int32), seq.astype(jnp.int32), before.astype(jnp.int32),
            sq.astype(jnp.int32), full.astype(jnp.int32))


def shift_x(value, d, n):
    return lax.ppermute(value, "x", [(i, (i + d) % n) for i in range(n)])


def reduce_scatter_x(value):
    n = lax.axis_size("x")
    me = lax.axis_index("x")
    parts = value.reshape(n, value.shape[0] // n, *value.shape[1:])
    total = jnp.take(parts, me, axis=0).astype(jnp.float32)
    for d in range(1, n):
        total = total + shift_x(jnp.take(parts, (me + d) % n, axis=0), d, n).astype(jnp.float32)
        if d < n - 1:
            total = lax.optimization_barrier(total)
    return total.astype(value.dtype)


def per_device(tokens, norm_gain, q_weight, k_weight, v_weight, o_weight, doc_lengths, span_order):
    local_rows = tokens.shape[1]
    tok_dev = local_rows * lax.axis_size(TENSOR)
    model_width = tokens.shape[2]
    head_dim = HEAD_DIM
    q_cols = q_weight.shape[1]
    kv_cols = k_weight.shape[1]
    q_heads = q_cols // head_dim
    kv_local = kv_cols // head_dim
    span_rows = tok_dev // 2
    base_row = lax.axis_index(CONTEXT) * tok_dev
    rows_float = tokens.astype(jnp.float32)
    normed = (
        rows_float
        * lax.rsqrt(jnp.mean(rows_float * rows_float, axis=-1, keepdims=True) + epsilon)
        * norm_gain
    ).astype(jnp.bfloat16)
    plane = lax.axis_index("yh")
    core = lax.axis_index("core")
    weights = jnp.concatenate([q_weight, k_weight, v_weight], axis=1)
    half_in = weights.shape[0] // 2
    sent_half = lax.dynamic_slice_in_dim(weights, core * half_in, half_in, 0)
    plane_rows = lax.all_gather(normed, "x", axis=1, tiled=True)
    partner_half = lax.ppermute(sent_half, ("yh", "ylo"), NEIGHBOUR)
    plane_rows, partner_half = lax.optimization_barrier((plane_rows, partner_half))
    other_half = lax.ppermute(partner_half, "core", [(0, 1), (1, 0)])
    half = plane_rows.shape[1]
    flat_rows = plane_rows.reshape(half, model_width)
    all_places = positions(base_row + jnp.arange(tok_dev, dtype=jnp.int32), span_order, span_rows)
    places = lax.dynamic_slice_in_dim(all_places, plane * half, half, 0)
    rows_mine = lax.dynamic_slice_in_dim(flat_rows, core * half_in, half_in, 1)
    rows_other = lax.dynamic_slice_in_dim(flat_rows, (1 - core) * half_in, half_in, 1)

    def finish(out):
        q = rotary(out[:, :q_cols].reshape(half, q_heads, head_dim), places)
        k = rotary(out[:, q_cols:q_cols + kv_cols].reshape(half, kv_local, head_dim), places)
        return jnp.concatenate(
            [q.reshape(half, q_cols), k.reshape(half, kv_cols), out[:, q_cols + kv_cols:]], axis=1
        ).astype(jnp.bfloat16)

    def project(w):
        return finish(jnp.dot(flat_rows, w, preferred_element_type=jnp.float32))

    for_partner = finish(
        jnp.dot(rows_mine, partner_half, preferred_element_type=jnp.float32)
        + jnp.dot(rows_other, other_half, preferred_element_type=jnp.float32))
    received = lax.ppermute(for_partner, "yh", [(0, 1), (1, 0)])
    flat_rows, for_partner = lax.optimization_barrier((flat_rows, for_partner))
    own = project(weights)
    first = jnp.where(plane == 0, own, received)
    second = jnp.where(plane == 0, received, own)
    projected = jnp.concatenate([first, second], axis=0)
    query_rows = projected[:, :q_cols]
    kv_pair = jnp.stack([projected[:, q_cols:q_cols + kv_cols], projected[:, q_cols + kv_cols:]])
    gathered = lax.all_gather(kv_pair, CONTEXT, axis=1, tiled=True)
    places = all_places
    row_count = tok_dev

    doc_ends = jnp.cumsum(doc_lengths)
    query_start = jnp.max(
        jnp.where(doc_ends[None, :] <= places[:, None], doc_ends[None, :], 0), axis=1)
    query_spans = lax.axis_index(CONTEXT) * 2 + jnp.arange(2, dtype=jnp.int32)
    tbl, seq, cnt, sq, full = key_tables(span_order, doc_ends, query_spans)
    qpos_col = places.astype(jnp.int32)[:, None]
    qstart_col = query_start.astype(jnp.int32)[:, None]
    m0, l0, acc0 = diagonal_attention(sq, query_rows, qpos_col, qstart_col, kv_pair)
    attended = span_attention(
        tbl, seq, cnt, full, query_rows, qpos_col, qstart_col, gathered, m0, l0, acc0)
    partner_o = lax.ppermute(o_weight, ("yh", "ylo"), NEIGHBOUR)
    half = row_count // 2
    own_rows = lax.dynamic_slice_in_dim(attended, plane * half, half, 0)
    other_rows = lax.dynamic_slice_in_dim(attended, (1 - plane) * half, half, 0)
    partner_rows = lax.ppermute(other_rows, "yh", [(0, 1), (1, 0)])
    mixed = (
        jnp.dot(own_rows, o_weight, preferred_element_type=jnp.float32)
        + jnp.dot(partner_rows, partner_o, preferred_element_type=jnp.float32)
    ).astype(jnp.bfloat16)
    mixed_rows = reduce_scatter_x(mixed)
    return mixed_rows.reshape(tokens.shape)


TENSOR = ("yh", "x")
NEIGHBOUR = [(0, 3), (3, 0), (1, 2), (2, 1)]
CONTEXT = ("z", "ylo", "core")


def solution(mesh):
    devices = mesh.devices.reshape(2, mesh.devices.shape[0] // 2, -1, 2, 2)
    split_mesh = jax.sharding.Mesh(devices, ("yh", "x", "z", "ylo", "core"))
    in_specs = (
        P(CONTEXT, TENSOR, None),
        P(),
        P(None, TENSOR),
        P(None, TENSOR),
        P(None, TENSOR),
        P(TENSOR, None),
        P(),
        P(),
    )
    out_specs = P(CONTEXT, TENSOR, None)
    return jax.shard_map(
        per_device, mesh=split_mesh, in_specs=in_specs, out_specs=out_specs, check_vma=False
    )
```
